32 devices in a mesh: section: 2 (over y), expert: 4 (over z), hid: 4 (over x, core).
Axes of the slice: x: 2, y: 2, z: 4, core: 2. Of those that a mesh axis runs over, the one named last changes fastest.
Arguments:
- saved_input: bfloat16 [2, 512, 4096], P('section', 'expert', 'hid'), may hold values from -6 to 6
- cotangent: bfloat16 [2, 512, 4096], P('section', 'expert', 'hid'), may hold values from -6 to 6
- next_input: bfloat16 [2, 512, 4096], P('section', 'expert', 'hid'), may hold values from -6 to 6
- routes_saved: int32 [2, 512, 2], P('section', 'expert'), may hold values from 0 to 3, all different within a row; in each aligned block of 128 rows (0 to 127, 128 to 255, ..., all dimensions but the last counted through in order) at most 96 rows name the same one
- routes_next: int32 [2, 512, 2], P('section', 'expert'), may hold values from 0 to 3, all different within a row; in each aligned block of 128 rows (0 to 127, 128 to 255, ..., all dimensions but the last counted through in order) at most 96 rows name the same one
- norm_gain: float32 [2, 4096], P('section', 'hid'), may hold values from 0.1 to 1.9
- router: float32 [2, 4096, 4], P('section', 'hid'), may hold values from -0.18 to 0.18
- expert_gate: bfloat16 [2, 4, 4096, 7168], P('section', 'expert', None, 'hid'), may hold values from -0.09375 to 0.09375
- expert_up: bfloat16 [2, 4, 4096, 7168], P('section', 'expert', None, 'hid'), may hold values from -0.09375 to 0.09375
- expert_down: bfloat16 [2, 4, 7168, 4096], P('section', 'expert', 'hid'), may hold values from -0.0625 to 0.0625
Outputs:
- leaving: bfloat16 [2, 512, 4096], P('section', 'expert', 'hid')
- arriving: bfloat16 [2, 512, 4096], P('section', 'expert', 'hid')
The draws below stay inside these ranges and needn't reach their ends.
Inputs may be any that keep to these rules, and one draw needn't show every extreme that they name: `routes_saved`: A token's two ids differ. In each aligned block of 128 tokens of a section no expert is named by more than 96 tokens, and some block names some expert exactly 96 times. `routes_next`: A token's two ids differ. In each aligned block of 128 tokens of a section no expert is named by more than 96 tokens, and some block names some expert exactly 96 times.
All inputs are finite; a program needn't handle non-finite values.
Results may differ from the reference program's by a relative error of at most 0.0052.
Values may be sent and summed in bfloat16 or wider, within the bound.
A program may use at most 128 MiB of HBM per device.

```python
import math
import jax
import jax.numpy as jnp
import numpy as np
from jax import lax

D = 4096
FF = 7168
TOK_DEV = 128
EXPERTS = 4
CAP = 96
TOKENS = 512
N_SECTION = 2
N_EXPERT = 4


def block_levels(key, shape, split, low, top_value):
    factor_of, own = 1.0, jax.random.fold_in(key, 6)
    for position, blocks in split:
        heights = jnp.exp(jax.random.uniform(jax.random.fold_in(own, position), (blocks,), jnp.float32, low / len(split), top_value / len(split)))
        factor_of = factor_of * jnp.repeat(heights, shape[position] // blocks).reshape([-1 if axis == position else 1 for axis in range(len(shape))])
    return factor_of


def shared_out(rng, own, number, rows, count, top, reach, lean):
    ranking = jax.random.permutation(rng, count)
    crowded, ordinary = portions_of(count, rows * top, reach, lean, True), portions_of(count, rows * top, reach, lean, False)
    places = jnp.arange(count)

    def named(tallies, offset_by):
        used = int((tallies > 0).sum())
        fixed = max(1, used // 4)
        passed = fixed + (places - fixed + offset_by * (used - fixed)) % max(1, count - fixed)
        return jnp.zeros((count,), jnp.int32).at[ranking[jnp.where(places < fixed, places, passed)]].set(jnp.asarray(tallies, jnp.int32))

    tallies = jnp.where(number % 4 == 0, named(crowded, number // 4), named(ordinary, number - number // 4 - 1))
    mixed = jax.random.permutation(jax.random.fold_in(own, 3), count)
    source_of, taker = mixed[0:count // 2 * 2:2], mixed[1:count // 2 * 2:2]
    margin = jnp.minimum(tallies[source_of] - 1, reach - tallies[taker]) // 2
    margin = jnp.where((source_of == ranking[0]) | (taker == ranking[0]) | (tallies[taker] == 0), 0, jnp.maximum(margin, 0))
    passed = jax.random.randint(jax.random.fold_in(own, 4), (count // 2,), 0, 1 << 20) % (margin + 1)
    tallies = tallies.at[source_of].add(-passed).at[taker].add(passed)
    items = jnp.searchsorted(jnp.cumsum(tallies), jnp.arange(rows * top), side="right").astype(jnp.int32)
    table = items.reshape(top, rows).T
    table = table[jax.random.permutation(jax.random.fold_in(own, 1), rows)]
    offset_by = jax.random.randint(jax.random.fold_in(own, 2), (rows, 1), 0, top)
    return jnp.take_along_axis(table, (jnp.arange(top)[None, :] + offset_by) % top, axis=1)


def portions_of(amount, total, reach, slope, full):
    weights = [(1 << 20) // math.isqrt(grade ** slope) + 1 for grade in range(1, amount + 1)]
    largest = reach if full else min(reach, max(-(-total // amount), total * weights[0] // sum(weights)))
    least = 1 if total - largest >= amount - 1 else 0
    holding, spare = [largest] + [least] * (amount - 1), total - largest - least * (amount - 1)
    while spare > 0:
        candidates = [i for i in range(1, amount) if holding[i] < largest] or [i for i in range(1, amount) if holding[i] < reach]
        pool, left = sum([weights[i] for i in candidates]), spare
        for i in candidates:
            more = min(reach - holding[i], max(1, left * weights[i] // pool), spare)
            holding[i] = holding[i] + more
            spare = spare - more
    return np.array(holding)


def normal_values(stream_key, extent, spread, limit, pieces=(), kind=jnp.bfloat16):
    drawn = jax.random.normal(stream_key, extent, jnp.float32) * spread
    if len(pieces) > 0:
        drawn = block_levels(stream_key, extent, pieces, -0.22, 0.18) * drawn
    return jnp.clip(drawn, min=-limit, max=limit).astype(kind)


def setup_inputs(seed: int = 0) -> dict:
    key_of = jax.random.split(jax.random.key(seed), 11)
    saved_input = normal_values(key_of[0], (N_SECTION, TOKENS, D), 1.0, 6.0, ((0, 2), (1, 4), (2, 4)))
    cotangent = normal_values(key_of[1], (N_SECTION, TOKENS, D), 1.0, 6.0, ((0, 2), (1, 4), (2, 4)))
    next_input = normal_values(key_of[2], (N_SECTION, TOKENS, D), 1.0, 6.0, ((0, 2), (1, 4), (2, 4)))
    routes_saved_keys = jax.random.split(jax.random.fold_in(key_of[3], 1), N_SECTION * TOKENS // TOK_DEV)
    routes_saved_turns = jax.random.permutation(jax.random.fold_in(key_of[3], 3), N_SECTION * TOKENS // TOK_DEV)
    routes_saved = jax.vmap(lambda own, number: shared_out(jax.random.fold_in(key_of[3], 2), own, number, TOK_DEV, EXPERTS, 2, CAP, 1))(routes_saved_keys, routes_saved_turns).reshape((N_SECTION, TOKENS, 2))
    routes_next_keys = jax.random.split(jax.random.fold_in(key_of[4], 1), N_SECTION * TOKENS // TOK_DEV)
    routes_next_turns = jax.random.permutation(jax.random.fold_in(key_of[4], 3), N_SECTION * TOKENS // TOK_DEV)
    routes_next = jax.vmap(lambda own, number: shared_out(jax.random.fold_in(key_of[4], 2), own, number, TOK_DEV, EXPERTS, 2, CAP, 1))(routes_next_keys, routes_next_turns).reshape((N_SECTION, TOKENS, 2))
    norm_gain = jnp.clip(1.0 + 0.18 * jax.random.normal(key_of[5], (N_SECTION, D), jnp.float32), 0.1, 1.9)
    router = normal_values(key_of[6], (N_SECTION, D, EXPERTS), 0.03, 0.18, ((0, 2), (1, 4)), jnp.float32)
    expert_gate = normal_values(key_of[7], (N_SECTION, EXPERTS, D, FF), D ** -0.5, 0.09375, ((0, 2), (1, 4), (3, 4)))
    expert_up = normal_values(key_of[8], (N_SECTION, EXPERTS, D, FF), D ** -0.5, 0.09375, ((0, 2), (1, 4), (3, 4)))
    expert_down = normal_values(key_of[9], (N_SECTION, EXPERTS, FF, D), FF ** -0.5, 0.0625, ((0, 2), (1, 4), (2, 4)))
    return {"saved_input": saved_input, "cotangent": cotangent, "next_input": next_input, "routes_saved": routes_saved, "routes_next": routes_next, "norm_gain": norm_gain, "router": router, "expert_gate": expert_gate, "expert_up": expert_up, "expert_down": expert_down}


EPSILON = 1e-05
HIGHEST = lax.Precision.HIGHEST

def norm_stats(inputs, gain, table):
    values = inputs.astype(jnp.float32)
    scale = lax.rsqrt(lax.optimization_barrier(jnp.sum(values * values, axis=1)) / D + EPSILON)
    scaled = values * scale[:, None] * gain[None, :]
    logits = jnp.dot(scaled, table, precision=HIGHEST)
    return (values, scale, scaled.astype(jnp.bfloat16), logits)

def placing(routes, logits):
    labels = jnp.arange(EXPERTS, dtype=jnp.int32)
    blocks = routes.reshape(N_EXPERT, TOK_DEV * 2).astype(jnp.int32)
    onehot = (blocks[:, :, None] == labels[None, None, :]).astype(jnp.int32)
    ranked = (jnp.cumsum(onehot, axis=1) - onehot).astype(jnp.int32)
    places = lax.optimization_barrier(jnp.sum(ranked * onehot, axis=2)).astype(jnp.int32)
    anchor = jnp.arange(N_EXPERT, dtype=jnp.int32)[:, None]
    targets = (blocks * (N_EXPERT * CAP) + anchor * CAP + places).astype(jnp.int32).reshape(TOKENS, 2)
    first_hit = (routes[:, 0:1] == labels[None, :]).astype(jnp.float32)
    second_hit = (routes[:, 1:2] == labels[None, :]).astype(jnp.float32)
    first_logit = lax.optimization_barrier(jnp.sum(logits * first_hit, axis=1))
    second_logit = lax.optimization_barrier(jnp.sum(logits * second_hit, axis=1))
    first_prob = jax.nn.sigmoid(first_logit - second_logit)
    second_prob = jax.nn.sigmoid(second_logit - first_logit)
    return (targets, first_prob, second_prob, first_hit - second_hit)

def spread_rows(targets, rows):
    total = EXPERTS * N_EXPERT * CAP
    doubled = jnp.repeat(rows, 2, axis=0)
    filled = jnp.zeros((total, rows.shape[1]), rows.dtype).at[targets.reshape(-1)].set(doubled)
    return filled.reshape(EXPERTS, N_EXPERT * CAP, rows.shape[1])

def blend(rows, targets, first_prob, second_prob):
    return first_prob[:, None] * rows[targets[:, 0]] + second_prob[:, None] * rows[targets[:, 1]]

def expert_rows(packed):
    saved_rows, cot_rows, next_rows, gate_matrix, up_matrix, down_matrix = packed
    gate_saved = jnp.dot(saved_rows, gate_matrix, preferred_element_type=jnp.float32)
    up_saved = jnp.dot(saved_rows, up_matrix, preferred_element_type=jnp.float32)
    grad_hidden = jnp.dot(cot_rows, down_matrix.T, preferred_element_type=jnp.float32)
    sig_saved = jax.nn.sigmoid(gate_saved)
    silu_saved = gate_saved * sig_saved
    hidden_saved = (silu_saved * up_saved).astype(jnp.bfloat16)
    row_dots = lax.optimization_barrier(jnp.sum(grad_hidden * hidden_saved.astype(jnp.float32), axis=1))
    grad_gate = (grad_hidden * up_saved * (sig_saved * (1.0 + gate_saved * (1.0 - sig_saved)))).astype(jnp.bfloat16)
    grad_up = (grad_hidden * silu_saved).astype(jnp.bfloat16)
    back_rows = jnp.dot(grad_gate, gate_matrix.T, preferred_element_type=jnp.float32) + jnp.dot(grad_up, up_matrix.T, preferred_element_type=jnp.float32)
    gate_next = jnp.dot(next_rows, gate_matrix, preferred_element_type=jnp.float32)
    up_next = jnp.dot(next_rows, up_matrix, preferred_element_type=jnp.float32)
    silu_next = gate_next * jax.nn.sigmoid(gate_next)
    hidden_next = (silu_next * up_next).astype(jnp.bfloat16)
    out_rows = jnp.dot(hidden_next, down_matrix, preferred_element_type=jnp.float32)
    return (back_rows, row_dots, out_rows)

def section_pass(saved, cotangent, upcoming, routes_saved, routes_next, gain, table, gate_all, up_all, down_all):
    values_saved, scale_saved, normed_saved, logits_saved = norm_stats(saved, gain, table)
    values_next, scale_next, normed_next, logits_next = norm_stats(upcoming, gain, table)
    targets_saved, first_saved, second_saved, diff_saved = placing(routes_saved, logits_saved)
    targets_next, first_next, second_next, diff_next = placing(routes_next, logits_next)
    buffer_saved = spread_rows(targets_saved, normed_saved)
    buffer_cot = spread_rows(targets_saved, cotangent)
    buffer_next = spread_rows(targets_next, normed_next)
    back_rows, row_dots, out_rows = lax.map(expert_rows, (buffer_saved, buffer_cot, buffer_next, gate_all, up_all, down_all))
    total = EXPERTS * N_EXPERT * CAP
    back_rows = back_rows.reshape(total, D)
    row_dots = row_dots.reshape(total)
    out_rows = out_rows.reshape(total, D)
    branch_next = blend(out_rows, targets_next, first_next, second_next)
    forward_out = (values_next + branch_next).astype(jnp.bfloat16)
    mixed_saved = blend(back_rows, targets_saved, first_saved, second_saved)
    grad_logit = (row_dots[targets_saved[:, 0]] - row_dots[targets_saved[:, 1]]) * first_saved * second_saved
    grad_normed = mixed_saved + jnp.dot(grad_logit[:, None] * diff_saved, table.T, precision=HIGHEST)
    scaled_grad = grad_normed * gain[None, :]
    inner = lax.optimization_barrier(jnp.sum(scaled_grad * values_saved, axis=1))
    cube = scale_saved * scale_saved * scale_saved
    grad_input = cotangent.astype(jnp.float32) + scale_saved[:, None] * scaled_grad - values_saved * cube[:, None] * (inner / D)[:, None]
    return (forward_out, grad_input.astype(jnp.bfloat16))

def reference(saved_input, cotangent, next_input, routes_saved, routes_next, norm_gain, router, expert_gate, expert_up, expert_down):
    forward_outs = []
    grad_inputs = []
    for section_index in range(N_SECTION):
        forward_out, grad_input = section_pass(saved_input[section_index], cotangent[section_index], next_input[section_index], routes_saved[section_index], routes_next[section_index], norm_gain[section_index], router[section_index], expert_gate[section_index], expert_up[section_index], expert_down[section_index])
        forward_outs.append(forward_out)
        grad_inputs.append(grad_input)
    leaving = jnp.stack([grad_inputs[0], forward_outs[1]])
    arriving = jnp.stack([grad_inputs[1], forward_outs[0]])
    return (leaving, arriving)
```

```python
import functools

import jax
import jax.numpy as jnp
from jax import lax
from jax.experimental import pallas as pl
from jax.experimental.pallas import tpu as pltpu
from jax.sharding import PartitionSpec as P

EPSILON = 1e-05
F32 = jnp.float32
BF16 = jnp.bfloat16
I32 = jnp.int32
NN = (((1,), (0,)), ((), ()))
NT = (((1,), (1,)), ((), ()))
LANES = 128
A_SLOTS = 3
R_SLOTS = 4
COT, NXT, SAV = 0, 1, 2


def bits_of(count):
    return [1 << bit for bit in range(count.bit_length() - 1)]


def low_bit(number):
    return number & -number


def flip(value, mask, count):
    total = 0
    for bit in bits_of(count):
        own = lax.rem(lax.div(value, bit), 2)
        if isinstance(mask, int):
            got = 1 - own if mask & bit else own
        else:
            other = lax.rem(lax.div(mask, bit), 2)
            got = own + other - 2 * own * other
        total = total + bit * got
    return total


def dot(a, b, dims=NN):
    return lax.dot_general(a, b, dims, preferred_element_type=F32)


def kernel(
    sizes,
    saved_ref, cot_ref, next_ref, routes_ref, gain_ref, table_ref, wg_ref, wu_ref, wd_ref,
    leaving_ref, arriving_ref,
    rows, slots, wa, wr, gh, hid_n, grads, rs_send, rs_recv, own_part, home_send, home,
    stat_send, stat_recv, dots_acc, dots_send, dots_recv, tail_send, tail_recv,
    cols, mixed, there_send, there_recv,
    wa_sem, wr_sem,
    z_send, z_recv, g_send, g_recv, s_send, s_recv, r_send, r_recv,
    b_send, b_recv, d_send, d_recv, t_send, t_recv, y_send, y_recv,
):
    E, H, T, F, D, ffd, cap, tn, tw = sizes
    n_tiles, n_cols = ffd // tn, F // tw
    steps = H * n_cols
    all_rows = E * cap
    sec, me, hi = lax.axis_index("section"), lax.axis_index("expert"), lax.axis_index("hid")
    hid_peer = [flip(hi, m, H) for m in range(H)]
    exp_peer = [flip(me, k, E) for k in range(E)]
    to_send = []
    none = me * 0

    def remote(src, dst, send, recv, e=None, h=None, s=None):
        where = (sec if s is None else s, me if e is None else e, hi if h is None else h)
        return pltpu.make_async_remote_copy(
            src_ref=src, dst_ref=dst, send_sem=send, recv_sem=recv,
            device_id=where, device_id_type=pl.DeviceIdType.MESH,
        )

    def send(build):
        build().start()
        to_send.append(build)

    def a_copies(kind, j, slot):
        if kind == "out":
            m = H - 1 - lax.div(j, n_cols)
            col = pl.multiple_of(flip(hi, m, H) * F + lax.rem(j, n_cols) * tw, tw)
            return [pltpu.make_async_copy(
                wd_ref.at[:, pl.ds(col, tw)], wa.at[slot, 0, pl.ds(0, ffd), pl.ds(0, tw)], wa_sem.at[slot, 0])]
        col = pl.multiple_of(j * tn, tn)
        return [
            pltpu.make_async_copy(w.at[:, pl.ds(col, tn)], wa.at[slot, half, :, pl.ds(0, tn)], wa_sem.at[slot, half])
            for half, w in enumerate((wg_ref, wu_ref))
        ]

    def start_a(g):
        slot = lax.rem(g, A_SLOTS)

        @pl.when((g < n_tiles) | (g >= n_tiles + steps) & (g < 2 * n_tiles + steps))
        def _():
            for copy in a_copies("pair", lax.rem(jnp.where(g < n_tiles, g, g - steps - n_tiles), n_tiles), slot):
                copy.start()

        @pl.when((g >= n_tiles) & (g < n_tiles + steps))
        def _():
            for copy in a_copies("out", g - n_tiles, slot):
                copy.start()

    def gh_copy(j):
        slot = lax.rem(j, R_SLOTS)
        return pltpu.make_async_copy(
            wd_ref.at[pl.ds(pl.multiple_of(j * tn, tn), tn), :], wr.at[slot, pl.ds(0, tn), pl.ds(0, D)],
            wr_sem.at[slot, 0])

    def back_copies(i):
        slot = lax.rem(i, R_SLOTS)
        m = H - 1 - lax.div(i, n_cols)
        row = pl.multiple_of(flip(hi, m, H) * F + lax.rem(i, n_cols) * tw, tw)
        return [
            pltpu.make_async_copy(
                w.at[pl.ds(row, tw), :], wr.at[slot, pl.ds(0, tw), pl.ds(half * ffd, ffd)], wr_sem.at[slot, half])
            for half, w in enumerate((wg_ref, wu_ref))
        ]

    for j in range(min(R_SLOTS - 1, n_tiles)):
        gh_copy(none + j).start()
    for g in range(A_SLOTS - 1):
        for copy in a_copies("pair", none + g, none + g):
            copy.start()

    barrier = pltpu.get_barrier_semaphore()
    partners = [(sec, me, hid_peer[m]) for m in range(1, H)]
    partners += [(sec, exp_peer[k], hi) for k in range(1, E)]
    partners += [(1 - sec, me, hi)]
    for where in partners:
        pl.semaphore_signal(barrier, inc=1, device_id=where, device_id_type=pl.DeviceIdType.MESH)
    lane = lax.broadcasted_iota(I32, (T, LANES), 1)
    gain = gain_ref[...]
    routes = routes_ref[...]
    route_cols = [routes[:, n:n + 1].astype(F32) for n in range(4)]
    spread = jnp.zeros((T, LANES), F32)
    for n in range(4):
        spread = spread + jnp.where(lane == n, route_cols[n], 0.0)
    route_rows = spread.T
    first_i = lax.broadcasted_iota(I32, (T, T), 0)
    second_i = lax.broadcasted_iota(I32, (T, T), 1)
    upper = jnp.where(first_i < second_i, 1.0, 0.0).astype(BF16)
    lower = jnp.where(first_i > second_i, 1.0, 0.0).astype(BF16)
    slot_i = lax.broadcasted_iota(I32, (cap, T), 0).astype(F32)
    lane_f = lane.astype(F32)

    def chosen(base, expert):
        first, second = route_rows[base:base + 1], route_rows[base + 1:base + 2]
        wanted = expert.astype(F32)
        hit = jnp.where(first == wanted, 1.0, 0.0) + jnp.where(second == wanted, 1.0, 0.0)
        rank = dot(jnp.broadcast_to(hit, (16, T)).astype(BF16), upper)[0:1]
        rank = jnp.where(hit > 0.5, rank, -1.0)
        return jnp.where(slot_i == rank, 1.0, 0.0).astype(BF16)

    def put(n, value):
        cols[:, n:n + 1] = value

    for n, base in enumerate((0, 2)):
        hits = jnp.where(lane_f == route_cols[base], 1.0, 0.0) + jnp.where(lane_f == route_cols[base + 1], 1.0, 0.0)
        ranks = dot(lower, hits.astype(BF16))
        for c in range(2):
            route = route_cols[base + c]
            put(16 + 2 * n + c, jnp.sum(jnp.where(lane_f == route, ranks, 0.0), axis=1, keepdims=True))
            put(20 + 2 * n + c, route)

    pl.semaphore_wait(barrier, len(partners))

    def region(tau, expert, feature):
        return rows.at[tau, pl.ds(pl.multiple_of(expert * cap, 16), cap), pl.ds(pl.multiple_of(feature * F, LANES), F)]

    def forward_copy(tau, piece, bit, k):
        part = region(tau, exp_peer[k], hid_peer[piece])
        return remote(part, part, g_send.at[tau, piece + bit, k], g_recv.at[tau, piece + bit, k], h=hid_peer[bit])

    def forward(tau, piece, k):
        for bit in reversed(bits_of(H)):
            if piece == 0 or bit < low_bit(piece):
                send(functools.partial(forward_copy, tau, piece, bit, k))

    def got_piece(tau, piece, k):
        part = region(tau, exp_peer[k], hid_peer[piece])
        remote(part, part, g_send.at[tau, piece, k], g_recv.at[tau, piece, k], h=hid_peer[low_bit(piece)]).wait_recv()

    def dispatch_copy(tau, k):
        return remote(
            slots.at[tau, k - 1], region(tau, me, hi), z_send.at[tau, k], z_recv.at[tau, k], e=exp_peer[k])

    def dispatch(tau, base, tokens):
        for k in list(range(E - 1, 0, -1)) + [0]:
            picked = dot(chosen(base, exp_peer[k]), tokens).astype(BF16)
            if k == 0:
                rows[tau, pl.ds(pl.multiple_of(me * cap, 16), cap), pl.ds(pl.multiple_of(hi * F, LANES), F)] = picked
                forward(tau, 0, 0)
            else:
                slots[tau, k - 1] = picked
                send(functools.partial(dispatch_copy, tau, k))

    def z_event(tau, k):
        part = region(tau, exp_peer[k], hi)
        remote(part, part, z_send.at[tau, k], z_recv.at[tau, k], e=exp_peer[k]).wait_recv()
        forward(tau, 0, k)

    relays = [p for top in reversed(bits_of(H)) if top > 1 for p in range(top, H, 2 * top)]

    def x_event(tau, k):
        for piece in relays:
            got_piece(tau, piece, k)
            forward(tau, piece, k)

    order = list(range(E - 1, 0, -1))

    def gather_events(tau):
        events = [functools.partial(x_event, tau, 0)]
        for k in order:
            events.insert(-1, functools.partial(z_event, tau, k))
            events.append(functools.partial(x_event, tau, k))
        return events

    def complete(tau):
        for piece in range(1, H, 2):
            for k in range(E):
                got_piece(tau, piece, k)

    dispatch(COT, 0, cot_ref[...])

    stats = jnp.zeros((T, LANES), F32)
    for offset, ref in ((0, saved_ref), (16, next_ref)):
        values = ref[...].astype(F32)
        stats = stats + jnp.where(lane == offset, jnp.sum(values * values, axis=1, keepdims=True), 0.0)
        for e in range(E):
            weights = table_ref[e:e + 1, :] * gain
            stats = stats + jnp.where(lane == offset + 1 + e, jnp.sum(values * weights, axis=1, keepdims=True), 0.0)
    stat_send[...] = stats.T[0:32]

    def all_to_hid(src, dst, sent, recv):
        copies = [remote(src, dst.at[m - 1], sent.at[m], recv.at[m], h=hid_peer[m]) for m in range(1, H)]
        for copy in copies:
            send(lambda copy=copy: copy)
        return copies

    stat_copies = all_to_hid(stat_send, stat_recv, s_send, s_recv)
    total = stats.T[0:32]
    for m, copy in enumerate(stat_copies):
        copy.wait_recv()
        total = total + stat_recv[m]
    stats = jnp.concatenate([total, jnp.zeros((LANES - 32, T), F32)], axis=0).T

    def finish_norm(offset, base, ref, keep):
        scale = lax.rsqrt(stats[:, offset:offset + 1] / D + EPSILON)
        first_score = jnp.zeros((T, 1), F32)
        second_score = jnp.zeros((T, 1), F32)
        for e in range(E):
            score = stats[:, offset + 1 + e:offset + 2 + e]
            first_score = first_score + jnp.where(route_cols[base] == e, score, 0.0)
            second_score = second_score + jnp.where(route_cols[base + 1] == e, score, 0.0)
        first, second = first_score * scale, second_score * scale
        put(keep, jax.nn.sigmoid(first - second))
        put(keep + 1, jax.nn.sigmoid(second - first))
        put(keep + 2, scale)
        put(keep + 3, first_score - second_score)
        return (ref[...].astype(F32) * scale * gain).astype(BF16)

    dispatch(NXT, 2, finish_norm(16, 2, next_ref, 4))
    dispatch(SAV, 0, finish_norm(0, 0, saved_ref, 0))

    def reduce_step(which, acc, i):
        m_now, c = H - 1 - lax.div(i, n_cols), lax.rem(i, n_cols)

        @pl.when(m_now == 0)
        def _():
            own_part[which, c] = acc

        for m in range(1, H):
            @pl.when(m_now == m)
            def _():
                value = acc
                for bit in bits_of(low_bit(m) * 2)[:-1]:
                    received(which, m + bit, c)
                    value = value + rs_recv[which, m + bit - 1, c].astype(F32)
                rs_send[which, m - 1, c] = value.astype(BF16)
                reduce_copy(which, m, c).start()

    def reduce_copy(which, m, c):
        return remote(
            rs_send.at[which, m - 1, c], rs_recv.at[which, m - 1, c],
            r_send.at[which, m, c], r_recv.at[which, m, c], h=hid_peer[low_bit(m)])

    def received(which, m, c):
        reduce_copy(which, m, c).wait_recv()

    def home_region(which, expert, c):
        return home.at[which, pl.ds(pl.multiple_of(expert * cap, 16), cap), pl.ds(c * tw, tw)]

    def home_copy(which, k, c):
        return remote(
            home_send.at[which, c, pl.ds(pl.multiple_of(exp_peer[k] * cap, 16), cap)], home_region(which, me, c),
            b_send.at[which, k, c], b_recv.at[which, k, c], e=exp_peer[k])

    def home_event(which, c):
        value = own_part[which, c]
        for bit in bits_of(H):
            received(which, bit, c)
            value = value + rs_recv[which, bit - 1, c].astype(F32)
        home_send[which, c] = value.astype(BF16)
        for k in order:
            send(functools.partial(home_copy, which, k, c))
        mine = pl.ds(pl.multiple_of(me * cap, 16), cap)
        home[which, mine, c * tw:(c + 1) * tw] = home_send[which, c, mine, :]

    def home_wait(which, c):
        for k in order:
            part = home_region(which, exp_peer[k], c)
            remote(part, part, b_send.at[which, k, c], b_recv.at[which, k, c], e=exp_peer[k]).wait_recv()

    wide_i = lax.broadcasted_iota(I32, (T, all_rows), 1).astype(F32)

    def selectors(n):
        picks = []
        for c in range(2):
            rank, route = cols[:, 16 + 2 * n + c:17 + 2 * n + c], cols[:, 20 + 2 * n + c:21 + 2 * n + c]
            picks.append(jnp.where(wide_i == route * cap + rank, 1.0, 0.0).astype(BF16))
        return picks

    def blended(which, n, keep, c, picks):
        part = home[which, :, c * tw:(c + 1) * tw]
        return cols[:, keep:keep + 1] * dot(picks[0], part) + cols[:, keep + 1:keep + 2] * dot(picks[1], part)

    def there_copy(n, height):
        part = pl.ds(n * height, height)
        return remote(there_send.at[part], there_recv.at[part], y_send.at[n], y_recv.at[n], s=1 - sec)

    halves = 2
    half_rows = T // halves

    def forward_out():
        picks = selectors(1)
        for c in range(n_cols):
            home_wait(0, c)
            part = slice(c * tw, (c + 1) * tw)
            value = (next_ref[:, part].astype(F32) + blended(0, 1, 4, c, picks)).astype(BF16)

            @pl.when(sec == 0)
            def _():
                there_send[:, part] = value

            @pl.when(sec == 1)
            def _():
                leaving_ref[:, part] = value

        @pl.when(sec == 0)
        def _():
            for n in range(halves):
                there_copy(n, half_rows).start()

    def run(events, index):
        for at, event in events:
            pl.when(index == at)(event)

    def place(events, spots, limit):
        return [(min(spot, limit - 1), event) for event, spot in zip(events, spots)]

    for event in gather_events(COT):
        event()
    complete(COT)
    next_events = gather_events(NXT)
    early = 4 if E == 4 else len(next_events) // 2
    spots = [(1 + 5 * n // early) for n in range(early)]
    gh_events = place(next_events[:early], spots, n_tiles)

    @pl.loop(0, n_tiles)
    def _(j):
        @pl.when(j + R_SLOTS - 1 < n_tiles)
        def _():
            gh_copy(j + R_SLOTS - 1).start()

        gh_copy(j).wait()
        slot = lax.rem(j, R_SLOTS)
        gh[:, pl.ds(pl.multiple_of(j * tn, tn), tn)] = dot(rows[COT], wr[slot, 0:tn, 0:D], NT)
        run(gh_events, j)

    for i in range(R_SLOTS - 1):
        for copy in back_copies(none + i):
            copy.start()

    for event in next_events[early:]:
        event()
    complete(NXT)

    saved_events = gather_events(SAV)
    late = 1
    count = len(saved_events) - late
    spots = [(n_tiles - 1) * n // max(1, count - 1) for n in range(count)]
    up_events = place(saved_events[:count], spots, n_tiles)

    @pl.loop(0, n_tiles)
    def _(j):
        start_a(j + A_SLOTS - 1)
        slot = lax.rem(j, A_SLOTS)
        for copy in a_copies("pair", j, slot):
            copy.wait()
        gate = dot(rows[NXT], wa[slot, 0, :, 0:tn])
        up = dot(rows[NXT], wa[slot, 1, :, 0:tn])
        hid_n[:, pl.ds(pl.multiple_of(j * tn, tn), tn)] = (gate * jax.nn.sigmoid(gate) * up).astype(BF16)
        run(up_events, j)

    out_events = place(saved_events[count:], [(3 * steps) // 4] * late, steps)

    @pl.loop(0, steps)
    def _(i):
        g = n_tiles + i
        start_a(g + A_SLOTS - 1)
        slot = lax.rem(g, A_SLOTS)
        for copy in a_copies("out", i, slot):
            copy.wait()
        reduce_step(0, dot(hid_n[...], wa[slot, 0, 0:ffd, 0:tw]), i)
        run(out_events, i)

    complete(SAV)

    dots_acc[...] = jnp.zeros_like(dots_acc)
    down_spots = [1 + 2 * c for c in range(n_cols)]
    in_gate = [c for c in range(n_cols) if down_spots[c] < n_tiles - 1]
    gate_events = [(down_spots[c], functools.partial(home_event, 0, c)) for c in in_gate]

    @pl.loop(0, n_tiles)
    def _(j):
        g = n_tiles + steps + j
        start_a(g + A_SLOTS - 1)
        slot = lax.rem(g, A_SLOTS)
        for copy in a_copies("pair", j, slot):
            copy.wait()
        gate = dot(rows[SAV], wa[slot, 0, :, 0:tn])
        up = dot(rows[SAV], wa[slot, 1, :, 0:tn])
        part = pl.ds(pl.multiple_of(j * tn, tn), tn)
        grad = gh[:, part]
        sig = jax.nn.sigmoid(gate)
        silu = gate * sig
        hidden = (silu * up).astype(BF16).astype(F32)
        grads[0, :, part] = (grad * up * (sig * (1.0 + gate * (1.0 - sig)))).astype(BF16)
        grads[1, :, part] = (grad * silu).astype(BF16)
        product = grad * hidden
        partial = product[:, 0:LANES]
        for n in range(1, tn // LANES):
            partial = partial + product[:, n * LANES:(n + 1) * LANES]
        dots_acc[...] += partial
        run(gate_events, j)

    def dots_copy(k):
        return remote(dots_send, dots_recv.at[k - 1], d_send.at[k], d_recv.at[k], e=exp_peer[k])

    dots_send[...] = jnp.broadcast_to(jnp.sum(dots_acc[...].T, axis=0, keepdims=True), (8, all_rows))
    for k in order:
        send(functools.partial(dots_copy, k))

    def dots_event():
        for k in order:
            dots_copy(k).wait_recv()
        gap = jnp.zeros((T, 1), F32)
        for k in range(E):
            row = dots_send[0:1] if k == 0 else dots_recv[k - 1, 0:1]
            expert = exp_peer[k].astype(F32)
            for c, sign in ((0, 1.0), (1, -1.0)):
                rank, route = cols[:, 16 + c:17 + c], cols[:, 20 + c:21 + c]
                spot = jnp.where(route == expert, me.astype(F32) * cap + rank, -1.0)
                gap = gap + sign * jnp.sum(jnp.where(wide_i == spot, row, 0.0), axis=1, keepdims=True)
        put(8, gap)

    late_events = [(1 + 2 * n, functools.partial(home_event, 0, c)) for n, c in enumerate(c for c in range(n_cols) if c not in in_gate)]
    back_events = late_events + [((steps * 5) // 8, dots_event), ((steps * 3) // 4, forward_out)]

    @pl.loop(0, steps)
    def _(i):
        @pl.when(i + R_SLOTS - 1 < steps)
        def _():
            for copy in back_copies(i + R_SLOTS - 1):
                copy.start()

        for copy in back_copies(i):
            copy.wait()
        slot = lax.rem(i, R_SLOTS)
        acc = dot(grads[0], wr[slot, 0:tw, 0:ffd], NT) + dot(grads[1], wr[slot, 0:tw, ffd:2 * ffd], NT)
        reduce_step(1, acc, i)
        run(back_events, i)

    for c in range(n_cols):
        home_event(1, c)
    picks = selectors(0)
    inner = jnp.zeros((T, 1), F32)
    for c in range(n_cols):
        home_wait(1, c)
        part = slice(c * tw, (c + 1) * tw)
        value = blended(1, 0, 0, c, picks) * gain_ref[:, part]
        mixed[:, part] = value
        inner = inner + jnp.sum(value * saved_ref[:, part].astype(F32), axis=1, keepdims=True)
    message = jnp.where(lane == 0, inner, 0.0) + jnp.where(lane == 1, cols[:, 8:9], 0.0)
    message = message.T[0:8]
    tail_send[...] = message
    for m, copy in enumerate(all_to_hid(tail_send, tail_recv, t_send, t_recv)):
        copy.wait_recv()
        message = message + tail_recv[m]
    message = jnp.concatenate([message, jnp.zeros((LANES - 8, T), F32)], axis=0).T
    scale = cols[:, 2:3]
    slope = message[:, 1:2] * cols[:, 0:1] * cols[:, 1:2]
    inner = message[:, 0:1] + slope * cols[:, 3:4]
    pull = scale * scale * scale * (inner / D)
    for n in range(halves):
        part = slice(n * half_rows, (n + 1) * half_rows)
        lean = jnp.zeros((half_rows, F), F32)
        for e in range(E):
            sign = jnp.where(cols[part, 20:21] == e, 1.0, 0.0) - jnp.where(cols[part, 21:22] == e, 1.0, 0.0)
            lean = lean + sign * table_ref[e:e + 1, :]
        grad = mixed[part, :] + slope[part] * lean * gain
        value = (
            cot_ref[part, :].astype(F32) + scale[part] * grad - saved_ref[part, :].astype(F32) * pull[part]
        ).astype(BF16)

        @pl.when(sec == 0)
        def _():
            leaving_ref[part, :] = value

        @pl.when(sec == 1)
        def _():
            there_send[part, :] = value
            there_copy(n, half_rows).start()

    for n in range(halves):
        copy = there_copy(n, half_rows)
        copy.wait_recv()
        arriving_ref[n * half_rows:(n + 1) * half_rows, :] = there_recv[n * half_rows:(n + 1) * half_rows, :]

    for build in to_send:
        build().wait_send()
    for which in range(2):
        for m in range(1, H):
            for c in range(n_cols):
                reduce_copy(which, m, c).wait_send()
    for n in range(halves):
        there_copy(n, half_rows).wait_send()


def per_device(
    saved_input,
    cotangent,
    next_input,
    routes_saved,
    routes_next,
    norm_gain,
    router,
    expert_gate,
    expert_up,
    expert_down,
):
    E, H = lax.axis_size("expert"), lax.axis_size("hid")
    T, F = saved_input.shape[1:]
    D, ffd = expert_gate.shape[2:]
    cap = 3 * T // router.shape[2]
    tn = 2 * LANES if ffd % (2 * LANES) == 0 else LANES
    tw = 2 * LANES if F % (2 * LANES) == 0 else LANES
    n_cols, all_rows = F // tw, E * cap
    deep, wide = max(tn, tw), max(D, 2 * ffd)
    routes = jnp.concatenate([routes_saved[0], routes_next[0]], axis=1)
    vmem = pl.BlockSpec(memory_space=pltpu.VMEM)
    hbm = pl.BlockSpec(memory_space=pl.ANY)
    dma = pltpu.SemaphoreType.DMA
    block = jax.ShapeDtypeStruct((T, F), BF16)
    scratch = [
        pltpu.VMEM((3, all_rows, D), BF16),
        pltpu.VMEM((3, E - 1, cap, F), BF16),
        pltpu.VMEM((A_SLOTS, 2, D, deep), BF16),
        pltpu.VMEM((R_SLOTS, deep, wide), BF16),
        pltpu.VMEM((all_rows, ffd), F32),
        pltpu.VMEM((all_rows, ffd), BF16),
        pltpu.VMEM((2, all_rows, ffd), BF16),
        pltpu.VMEM((2, H - 1, n_cols, all_rows, tw), BF16),
        pltpu.VMEM((2, H - 1, n_cols, all_rows, tw), BF16),
        pltpu.VMEM((2, n_cols, all_rows, tw), F32),
        pltpu.VMEM((2, n_cols, all_rows, tw), BF16),
        pltpu.VMEM((2, all_rows, F), BF16),
        pltpu.VMEM((32, T), F32),
        pltpu.VMEM((H - 1, 32, T), F32),
        pltpu.VMEM((all_rows, LANES), F32),
        pltpu.VMEM((8, all_rows), F32),
        pltpu.VMEM((E - 1, 8, all_rows), F32),
        pltpu.VMEM((8, T), F32),
        pltpu.VMEM((H - 1, 8, T), F32),
        pltpu.VMEM((T, LANES), F32),
        pltpu.VMEM((T, F), F32),
        pltpu.VMEM((T, F), BF16),
        pltpu.VMEM((T, F), BF16),
        dma((A_SLOTS, 2)),
        dma((R_SLOTS, 2)),
        dma((3, E)),
        dma((3, E)),
        dma((3, H, E)),
        dma((3, H, E)),
        dma((H,)),
        dma((H,)),
        dma((2, H, n_cols)),
        dma((2, H, n_cols)),
        dma((2, E, n_cols)),
        dma((2, E, n_cols)),
        dma((E,)),
        dma((E,)),
        dma((H,)),
        dma((H,)),
        dma((2,)),
        dma((2,)),
    ]
    leaving, arriving = pl.pallas_call(
        functools.partial(kernel, (E, H, T, F, D, ffd, cap, tn, tw)),
        out_shape=(block, block),
        in_specs=[vmem] * 6 + [hbm] * 3,
        out_specs=(vmem, vmem),
        scratch_shapes=scratch,
        compiler_params=pltpu.CompilerParams(
            collective_id=0, has_side_effects=True, vmem_limit_bytes=67043328
        ),
        name="relay",
    )(
        saved_input[0], cotangent[0], next_input[0], routes, norm_gain, router[0].T,
        expert_gate[0, 0], expert_up[0, 0], expert_down[0, 0],
    )
    return (leaving[None], arriving[None])


def solution(mesh):
    placed = (
        P("section", "expert", "hid"),
        P("section", "expert", "hid"),
        P("section", "expert", "hid"),
        P("section", "expert", None),
        P("section", "expert", None),
        P("section", "hid"),
        P("section", "hid", None),
        P("section", "expert", None, "hid"),
        P("section", "expert", None, "hid"),
        P("section", "expert", "hid", None),
    )
    return jax.shard_map(
        per_device,
        mesh=mesh,
        in_specs=placed,
        out_specs=(P("section", "expert", "hid"), P("section", "expert", "hid")),
        check_vma=False,
    )
```

```python
import functools

import jax
import jax.numpy as jnp
from jax import lax
from jax.experimental import pallas as pl
from jax.experimental.pallas import tpu as pltpu
from jax.sharding import PartitionSpec as P

EPSILON = 1e-05
F32 = jnp.float32
BF16 = jnp.bfloat16
I32 = jnp.int32
NN = (((1,), (0,)), ((), ()))
NT = (((1,), (1,)), ((), ()))
LANES = 128
A_SLOTS = 3
R_SLOTS = 4
COT, NXT, SAV = 0, 1, 2


def bits_of(count):
    return [1 << bit for bit in range(count.bit_length() - 1)]


def low_bit(number):
    return number & -number


def flip(value, mask, count):
    total = 0
    for bit in bits_of(count):
        own = lax.rem(lax.div(value, bit), 2)
        if isinstance(mask, int):
            got = 1 - own if mask & bit else own
        else:
            other = lax.rem(lax.div(mask, bit), 2)
            got = own + other - 2 * own * other
        total = total + bit * got
    return total


def dot(a, b, dims=NN):
    return lax.dot_general(a, b, dims, preferred_element_type=F32)


def kernel(
    sizes,
    saved_ref, cot_ref, next_ref, pair_saved_ref, pair_next_ref, gain_ref, table_ref, wg_ref, wu_ref, wd_ref,
    out_ref,
    rows, slots, wa, wr, gh, hid_n, grads, rs_send, rs_recv, own_part, home_send, home,
    stat_send, stat_recv, dots_acc, dots_send, dots_recv, tail_send, tail_recv,
    cols, mixed, there_send, there_recv, far_cot, far_saved, far_value, far_gain, far_table, far_cols, far_tail,
    wa_sem, wr_sem,
    z_send, z_recv, g_send, g_recv, s_send, s_recv, r_send, r_recv,
    b_send, b_recv, d_send, d_recv, t_send, t_recv, y_send, y_recv, e_send, e_recv, f_send, f_recv,
):
    E, H, T, F, D, ffd, cap, tn, tw = sizes
    n_tiles, n_cols = ffd // tn, F // tw
    steps = H * n_cols
    all_rows = E * cap
    sec, me, hi = lax.axis_index("section"), lax.axis_index("expert"), lax.axis_index("hid")
    hid_peer = [flip(hi, m, H) for m in range(H)]
    exp_peer = [flip(me, k, E) for k in range(E)]
    to_send = []
    none = me * 0

    def remote(src, dst, send, recv, e=None, h=None, s=None):
        where = (sec if s is None else s, me if e is None else e, hi if h is None else h)
        return pltpu.make_async_remote_copy(
            src_ref=src, dst_ref=dst, send_sem=send, recv_sem=recv,
            device_id=where, device_id_type=pl.DeviceIdType.MESH,
        )

    def send(build):
        build().start()
        to_send.append(build)

    def place_of(i):
        at = lax.rem(i, H)
        return H - 1 - 2 * at + lax.div(at, H // 2) * (H - 1), lax.div(i, H)

    def a_copies(kind, j, slot):
        if kind == "out":
            copies = []
            for half in range(2):
                m, c = place_of(2 * j + half)
                col = pl.multiple_of(flip(hi, m, H) * F + c * tw, tw)
                copies.append(pltpu.make_async_copy(
                    wd_ref.at[:, pl.ds(col, tw)], wa.at[slot, half, pl.ds(0, ffd), pl.ds(0, tw)],
                    wa_sem.at[slot, half]))
            return copies
        col = pl.multiple_of(j * tn, tn)
        return [
            pltpu.make_async_copy(w.at[:, pl.ds(col, tn)], wa.at[slot, half, :, pl.ds(0, tn)], wa_sem.at[slot, half])
            for half, w in enumerate((wg_ref, wu_ref))
        ]

    out_items = steps // 2

    def start_a(g):
        slot = lax.rem(g, A_SLOTS)

        @pl.when((g < n_tiles) | (g >= n_tiles + out_items) & (g < 2 * n_tiles + out_items))
        def _():
            for copy in a_copies("pair", lax.rem(jnp.where(g < n_tiles, g, g - out_items - n_tiles), n_tiles), slot):
                copy.start()

        @pl.when((g >= n_tiles) & (g < n_tiles + out_items))
        def _():
            for copy in a_copies("out", g - n_tiles, slot):
                copy.start()

    def gh_copy(j):
        slot = lax.rem(j, R_SLOTS)
        return pltpu.make_async_copy(
            wd_ref.at[pl.ds(pl.multiple_of(j * tn, tn), tn), :], wr.at[slot, pl.ds(0, tn), pl.ds(0, D)],
            wr_sem.at[slot, 0])

    def back_copies(i):
        slot = lax.rem(i, R_SLOTS)
        m, c = place_of(i)
        row = pl.multiple_of(flip(hi, m, H) * F + c * tw, tw)
        return [
            pltpu.make_async_copy(
                w.at[pl.ds(row, tw), :], wr.at[slot, pl.ds(0, tw), pl.ds(half * ffd, ffd)], wr_sem.at[slot, half])
            for half, w in enumerate((wg_ref, wu_ref))
        ]

    for j in range(min(R_SLOTS - 1, n_tiles)):
        gh_copy(none + j).start()
    for g in range(A_SLOTS - 1):
        for copy in a_copies("pair", none + g, none + g):
            copy.start()

    barrier = pltpu.get_barrier_semaphore()
    partners = [(sec, me, hid_peer[m]) for m in range(1, H)]
    partners += [(sec, exp_peer[k], hi) for k in range(1, E)]
    partners += [(1 - sec, me, hid_peer[m]) for m in range(H)]
    for where in partners:
        pl.semaphore_signal(barrier, inc=1, device_id=where, device_id_type=pl.DeviceIdType.MESH)
    lane = lax.broadcasted_iota(I32, (T, LANES), 1)
    gain = gain_ref[...]
    route_rows = jnp.concatenate(
        [pair_saved_ref[...].astype(F32), pair_next_ref[...].astype(F32), jnp.zeros((LANES - 4, T), F32)], axis=0)
    spread = route_rows.T
    route_cols = [spread[:, n:n + 1] for n in range(4)]
    first_i = lax.broadcasted_iota(I32, (T, T), 0)
    second_i = lax.broadcasted_iota(I32, (T, T), 1)
    upper = jnp.where(first_i < second_i, 1.0, 0.0).astype(BF16)
    lower = jnp.where(first_i > second_i, 1.0, 0.0).astype(BF16)
    slot_i = lax.broadcasted_iota(I32, (cap, T), 0).astype(F32)
    lane_f = lane.astype(F32)

    def chosen(base, expert):
        first, second = route_rows[base:base + 1], route_rows[base + 1:base + 2]
        wanted = expert.astype(F32)
        hit = jnp.where(first == wanted, 1.0, 0.0) + jnp.where(second == wanted, 1.0, 0.0)
        rank = dot(jnp.broadcast_to(hit, (16, T)).astype(BF16), upper)[0:1]
        rank = jnp.where(hit > 0.5, rank, -1.0)
        return jnp.where(slot_i == rank, 1.0, 0.0).astype(BF16)

    def put(n, value):
        cols[:, n:n + 1] = value

    for n, base in enumerate((0, 2)):
        hits = jnp.where(lane_f == route_cols[base], 1.0, 0.0) + jnp.where(lane_f == route_cols[base + 1], 1.0, 0.0)
        ranks = dot(lower, hits.astype(BF16))
        for c in range(2):
            route = route_cols[base + c]
            put(16 + 2 * n + c, jnp.sum(jnp.where(lane_f == route, ranks, 0.0), axis=1, keepdims=True))
            put(20 + 2 * n + c, route)

    pl.semaphore_wait(barrier, len(partners))

    def region(tau, expert, feature):
        return rows.at[tau, pl.ds(pl.multiple_of(expert * cap, 16), cap), pl.ds(pl.multiple_of(feature * F, LANES), F)]

    def forward_copy(tau, piece, bit, k):
        part = region(tau, exp_peer[k], hid_peer[piece])
        return remote(part, part, g_send.at[tau, piece + bit, k], g_recv.at[tau, piece + bit, k], h=hid_peer[bit])

    def forward(tau, piece, k):
        for bit in reversed(bits_of(H)):
            if piece == 0 or bit < low_bit(piece):
                send(functools.partial(forward_copy, tau, piece, bit, k))

    def got_piece(tau, piece, k):
        part = region(tau, exp_peer[k], hid_peer[piece])
        remote(part, part, g_send.at[tau, piece, k], g_recv.at[tau, piece, k], h=hid_peer[low_bit(piece)]).wait_recv()

    def dispatch_copy(tau, k):
        return remote(
            slots.at[tau, k - 1], region(tau, me, hi), z_send.at[tau, k], z_recv.at[tau, k], e=exp_peer[k])

    def dispatch(tau, base, tokens, onward):
        for k in list(range(E - 1, 0, -1)) + [0]:
            picked = dot(chosen(base, exp_peer[k]), tokens).astype(BF16)
            if k == 0:
                rows[tau, pl.ds(pl.multiple_of(me * cap, 16), cap), pl.ds(pl.multiple_of(hi * F, LANES), F)] = picked
                if onward:
                    forward(tau, 0, 0)
            else:
                slots[tau, k - 1] = picked
                send(functools.partial(dispatch_copy, tau, k))

    def z_event(tau, k):
        part = region(tau, exp_peer[k], hi)
        remote(part, part, z_send.at[tau, k], z_recv.at[tau, k], e=exp_peer[k]).wait_recv()
        forward(tau, 0, k)

    relays = [p for top in reversed(bits_of(H)) if top > 1 for p in range(top, H, 2 * top)]

    def x_event(tau, k):
        for piece in relays:
            got_piece(tau, piece, k)
            forward(tau, piece, k)

    order = list(range(E - 1, 0, -1))

    def gather_events(tau):
        events = [functools.partial(x_event, tau, 0)]
        for k in order:
            events.insert(-1, functools.partial(z_event, tau, k))
            events.append(functools.partial(x_event, tau, k))
        return events

    def complete(tau):
        for piece in range(1, H, 2):
            for k in range(E):
                got_piece(tau, piece, k)

    stats = jnp.zeros((T, LANES), F32)
    for offset, ref in ((0, saved_ref), (16, next_ref)):
        values = ref[...].astype(F32)
        stats = stats + jnp.where(lane == offset, jnp.sum(values * values, axis=1, keepdims=True), 0.0)
        for e in range(E):
            weights = table_ref[e:e + 1, :] * gain
            stats = stats + jnp.where(lane == offset + 1 + e, jnp.sum(values * weights, axis=1, keepdims=True), 0.0)
    stat_send[...] = stats.T[0:32]

    def all_to_hid(src, dst, sent, recv):
        copies = [remote(src, dst.at[m - 1], sent.at[m], recv.at[m], h=hid_peer[m]) for m in range(1, H)]
        for copy in copies:
            send(lambda copy=copy: copy)
        return copies

    stat_copies = all_to_hid(stat_send, stat_recv, s_send, s_recv)

    dispatch(COT, 0, cot_ref[...], True)

    total = stats.T[0:32]
    for m, copy in enumerate(stat_copies):
        copy.wait_recv()
        total = total + stat_recv[m]
    stats = jnp.concatenate([total, jnp.zeros((LANES - 32, T), F32)], axis=0).T

    def finish_norm(offset, base, ref, keep):
        scale = lax.rsqrt(stats[:, offset:offset + 1] / D + EPSILON)
        first_score = jnp.zeros((T, 1), F32)
        second_score = jnp.zeros((T, 1), F32)
        for e in range(E):
            score = stats[:, offset + 1 + e:offset + 2 + e]
            first_score = first_score + jnp.where(route_cols[base] == e, score, 0.0)
            second_score = second_score + jnp.where(route_cols[base + 1] == e, score, 0.0)
        first, second = first_score * scale, second_score * scale
        put(keep, jax.nn.sigmoid(first - second))
        put(keep + 1, jax.nn.sigmoid(second - first))
        put(keep + 2, scale)
        put(keep + 3, first_score - second_score)
        return (ref[...].astype(F32) * scale * gain).astype(BF16)

    dispatch(NXT, 2, finish_norm(16, 2, next_ref, 4), False)
    dispatch(SAV, 0, finish_norm(0, 0, saved_ref, 0), False)

    far = [(cot_ref, far_cot), (saved_ref, far_saved), (gain_ref, far_gain), (table_ref, far_table), (cols, far_cols)]

    def far_copy(n):
        return remote(far[n][0], far[n][1], e_send.at[n], e_recv.at[n], s=1 - sec)

    def far_value_copy(c):
        part = pl.ds(c * tw, tw)
        n = len(far) + c
        return remote(there_send.at[:, part], far_value.at[:, part], e_send.at[n], e_recv.at[n], s=1 - sec)

    @pl.when(sec == 1)
    def _():
        for n in range(len(far)):
            far_copy(n).start()

    def reduce_step(which, acc, i):
        m_now, c = place_of(i)

        @pl.when(m_now == 0)
        def _():
            own_part[which, c] = acc

        for m in range(1, H):
            @pl.when(m_now == m)
            def _():
                value = acc
                for bit in bits_of(low_bit(m) * 2)[:-1]:
                    received(which, m + bit, c)
                    value = value + rs_recv[which, m + bit - 1, c].astype(F32)
                rs_send[which, m - 1, c] = value.astype(BF16)
                reduce_copy(which, m, c).start()

    def reduce_copy(which, m, c):
        return remote(
            rs_send.at[which, m - 1, c], rs_recv.at[which, m - 1, c],
            r_send.at[which, m, c], r_recv.at[which, m, c], h=hid_peer[low_bit(m)])

    def received(which, m, c):
        reduce_copy(which, m, c).wait_recv()

    def home_region(which, expert, c):
        return home.at[which, pl.ds(pl.multiple_of(expert * cap, 16), cap), pl.ds(c * tw, tw)]

    def home_copy(which, k, c):
        return remote(
            home_send.at[which, c, pl.ds(pl.multiple_of(exp_peer[k] * cap, 16), cap)], home_region(which, me, c),
            b_send.at[which, k, c], b_recv.at[which, k, c], e=exp_peer[k])

    def home_event(which, c):
        value = own_part[which, c]
        for bit in bits_of(H):
            received(which, bit, c)
            value = value + rs_recv[which, bit - 1, c].astype(F32)
        home_send[which, c] = value.astype(BF16)
        for k in order:
            send(functools.partial(home_copy, which, k, c))
        mine = pl.ds(pl.multiple_of(me * cap, 16), cap)
        home[which, mine, c * tw:(c + 1) * tw] = home_send[which, c, mine, :]

    def home_wait(which, c):
        for k in order:
            part = home_region(which, exp_peer[k], c)
            remote(part, part, b_send.at[which, k, c], b_recv.at[which, k, c], e=exp_peer[k]).wait_recv()

    wide_i = lax.broadcasted_iota(I32, (T, all_rows), 1).astype(F32)

    def selectors(n):
        picks = []
        for c in range(2):
            rank, route = cols[:, 16 + 2 * n + c:17 + 2 * n + c], cols[:, 20 + 2 * n + c:21 + 2 * n + c]
            picks.append(jnp.where(wide_i == route * cap + rank, 1.0, 0.0).astype(BF16))
        return picks

    def blended(which, n, keep, c, picks):
        part = home[which, :, c * tw:(c + 1) * tw]
        return cols[:, keep:keep + 1] * dot(picks[0], part) + cols[:, keep + 1:keep + 2] * dot(picks[1], part)

    def there_copy(n, height):
        part = pl.ds(n * height, height)
        return remote(there_send.at[part], there_recv.at[part], y_send.at[n], y_recv.at[n], s=1 - sec)

    halves = 2
    half_rows = T // halves

    def forward_out():
        picks = selectors(1)
        for c in range(n_cols):
            home_wait(0, c)
            part = slice(c * tw, (c + 1) * tw)
            value = (next_ref[:, part].astype(F32) + blended(0, 1, 4, c, picks)).astype(BF16)

            @pl.when(sec == 0)
            def _():
                there_send[:, part] = value

            @pl.when(sec == 1)
            def _():
                out_ref[0, :, part] = value

        @pl.when(sec == 0)
        def _():
            for n in range(halves):
                there_copy(n, half_rows).start()

    def run(events, index):
        for at, event in events:
            pl.when(index == at)(event)

    def place(events, spots, limit):
        return [(min(spot, limit - 1), event) for event, spot in zip(events, spots)]

    for event in gather_events(COT):
        event()
    forward(NXT, 0, 0)
    complete(COT)
    next_events = gather_events(NXT)
    early = 4 if E == 4 else len(next_events) // 2
    spots = [(1 + 5 * n // early) for n in range(early)]
    gh_events = place(next_events[:early], spots, n_tiles)

    @pl.loop(0, n_tiles)
    def _(j):
        @pl.when(j + R_SLOTS - 1 < n_tiles)
        def _():
            gh_copy(j + R_SLOTS - 1).start()

        gh_copy(j).wait()
        slot = lax.rem(j, R_SLOTS)
        gh[:, pl.ds(pl.multiple_of(j * tn, tn), tn)] = dot(rows[COT], wr[slot, 0:tn, 0:D], NT)
        run(gh_events, j)

    for i in range(R_SLOTS - 1):
        for copy in back_copies(none + i):
            copy.start()

    for event in next_events[early:]:
        event()
    forward(SAV, 0, 0)
    complete(NXT)

    saved_events = gather_events(SAV)
    late = 1
    count = len(saved_events) - late
    spots = [(n_tiles - 1) * n // max(1, count - 1) for n in range(count)]
    up_events = place(saved_events[:count], spots, n_tiles)

    @pl.loop(0, n_tiles)
    def _(j):
        start_a(j + A_SLOTS - 1)
        slot = lax.rem(j, A_SLOTS)
        for copy in a_copies("pair", j, slot):
            copy.wait()
        gate = dot(rows[NXT], wa[slot, 0, :, 0:tn])
        up = dot(rows[NXT], wa[slot, 1, :, 0:tn])
        hid_n[:, pl.ds(pl.multiple_of(j * tn, tn), tn)] = (gate * jax.nn.sigmoid(gate) * up).astype(BF16)
        run(up_events, j)

    out_events = place(saved_events[count:], [(3 * out_items) // 4] * late, out_items)

    @pl.loop(0, out_items)
    def _(i):
        g = n_tiles + i
        start_a(g + A_SLOTS - 1)
        slot = lax.rem(g, A_SLOTS)
        for half, copy in enumerate(a_copies("out", i, slot)):
            copy.wait()
            reduce_step(0, dot(hid_n[...], wa[slot, half, 0:ffd, 0:tw]), 2 * i + half)
        run(out_events, i)

    complete(SAV)

    dots_acc[...] = jnp.zeros_like(dots_acc)
    down_spots = [1 + 2 * c for c in range(n_cols)]
    in_gate = [c for c in range(n_cols) if down_spots[c] < n_tiles - 1]
    gate_events = [(down_spots[c], functools.partial(home_event, 0, c)) for c in in_gate]

    @pl.loop(0, n_tiles)
    def _(j):
        g = n_tiles + out_items + j
        start_a(g + A_SLOTS - 1)
        slot = lax.rem(g, A_SLOTS)
        for copy in a_copies("pair", j, slot):
            copy.wait()
        gate = dot(rows[SAV], wa[slot, 0, :, 0:tn])
        up = dot(rows[SAV], wa[slot, 1, :, 0:tn])
        part = pl.ds(pl.multiple_of(j * tn, tn), tn)
        grad = gh[:, part]
        sig = jax.nn.sigmoid(gate)
        silu = gate * sig
        hidden = (silu * up).astype(BF16).astype(F32)
        grads[0, :, part] = (grad * up * (sig * (1.0 + gate * (1.0 - sig)))).astype(BF16)
        grads[1, :, part] = (grad * silu).astype(BF16)
        product = grad * hidden
        partial = product[:, 0:LANES]
        for n in range(1, tn // LANES):
            partial = partial + product[:, n * LANES:(n + 1) * LANES]
        dots_acc[...] += partial
        run(gate_events, j)

    def dots_copy(k):
        return remote(dots_send, dots_recv.at[k - 1], d_send.at[k], d_recv.at[k], e=exp_peer[k])

    dots_send[...] = jnp.broadcast_to(jnp.sum(dots_acc[...].T, axis=0, keepdims=True), (8, all_rows))
    for k in order:
        send(functools.partial(dots_copy, k))

    def dots_event():
        for k in order:
            dots_copy(k).wait_recv()
        gap = jnp.zeros((T, 1), F32)
        for k in range(E):
            row = dots_send[0:1] if k == 0 else dots_recv[k - 1, 0:1]
            expert = exp_peer[k].astype(F32)
            for c, sign in ((0, 1.0), (1, -1.0)):
                rank, route = cols[:, 16 + c:17 + c], cols[:, 20 + c:21 + c]
                spot = jnp.where(route == expert, me.astype(F32) * cap + rank, -1.0)
                gap = gap + sign * jnp.sum(jnp.where(wide_i == spot, row, 0.0), axis=1, keepdims=True)
        dots_acc[0:T, 0:1] = gap

    late_events = [(1 + 2 * n, functools.partial(home_event, 0, c)) for n, c in enumerate(c for c in range(n_cols) if c not in in_gate)]
    soon = [c for c in range(n_cols) if H * (c + 2) - 1 < steps]
    back_events = late_events + [(H * (c + 2) - 1, functools.partial(home_event, 1, c)) for c in soon]
    back_events += [((steps * 5) // 8, dots_event), ((steps * 3) // 4, forward_out)]

    @pl.loop(0, steps)
    def _(i):
        @pl.when(i + R_SLOTS - 1 < steps)
        def _():
            for copy in back_copies(i + R_SLOTS - 1):
                copy.start()

        for copy in back_copies(i):
            copy.wait()
        slot = lax.rem(i, R_SLOTS)
        acc = dot(grads[0], wr[slot, 0:tw, 0:ffd], NT) + dot(grads[1], wr[slot, 0:tw, ffd:2 * ffd], NT)
        reduce_step(1, acc, i)
        run(back_events, i)

    for c in range(n_cols):
        if c not in soon:
            home_event(1, c)
    picks = selectors(0)
    inner = jnp.zeros((T, 1), F32)
    for c in range(n_cols):
        home_wait(1, c)
        part = slice(c * tw, (c + 1) * tw)
        value = blended(1, 0, 0, c, picks) * gain_ref[:, part]
        mixed[:, part] = value

        @pl.when(sec == 1)
        def _():
            there_send[:, part] = value.astype(BF16)
            far_value_copy(c).start()

        inner = inner + jnp.sum(value * saved_ref[:, part].astype(F32), axis=1, keepdims=True)
    message = jnp.where(lane == 0, inner, 0.0) + jnp.where(lane == 1, dots_acc[0:T, 0:1], 0.0)
    message = message.T[0:8]
    tail_send[...] = message

    def tail_copy(m):
        return remote(tail_send, tail_recv.at[m - 1], t_send.at[m], t_recv.at[m], h=hid_peer[m])

    def far_tail_copy(m):
        return remote(tail_send, far_tail.at[m], f_send.at[m], f_recv.at[m], h=hid_peer[m], s=1 - sec)

    def input_gradient(message, cot, saved, value_of, gains, table, kept, place_in):
        message = jnp.concatenate([message, jnp.zeros((LANES - 8, T), F32)], axis=0).T
        scale = kept[:, 2:3]
        slope = message[:, 1:2] * kept[:, 0:1] * kept[:, 1:2]
        inner = message[:, 0:1] + slope * kept[:, 3:4]
        pull = scale * scale * scale * (inner / D)
        for n in range(halves):
            part = slice(n * half_rows, (n + 1) * half_rows)
            lean = jnp.zeros((half_rows, F), F32)
            for e in range(E):
                sign = jnp.where(kept[part, 20:21] == e, 1.0, 0.0) - jnp.where(kept[part, 21:22] == e, 1.0, 0.0)
                lean = lean + sign * table[e:e + 1, :]
            grad = value_of[part, :].astype(F32) + slope[part] * lean * gains[...]
            out_ref[place_in, part, :] = (
                cot[part, :].astype(F32) + scale[part] * grad - saved[part, :].astype(F32) * pull[part]
            ).astype(BF16)

    @pl.when(sec == 1)
    def _():
        for m in range(H):
            far_tail_copy(m).start()
        for n in range(halves):
            there_copy(n, half_rows).wait_recv()
        out_ref[1] = there_recv[...]
        for n in range(len(far)):
            far_copy(n).wait_send()
        for c in range(n_cols):
            far_value_copy(c).wait_send()
        for m in range(H):
            far_tail_copy(m).wait_send()

    @pl.when(sec == 0)
    def _():
        for m in range(1, H):
            tail_copy(m).start()
        total = message
        for m in range(1, H):
            tail_copy(m).wait_recv()
            total = total + tail_recv[m - 1]
        input_gradient(total, cot_ref, saved_ref, mixed, gain_ref, table_ref, cols, 0)
        for n in range(len(far)):
            far_copy(n).wait_recv()
        for c in range(n_cols):
            far_value_copy(c).wait_recv()
        total = jnp.zeros((8, T), F32)
        for m in range(H):
            far_tail_copy(m).wait_recv()
            total = total + far_tail[m]
        input_gradient(total, far_cot, far_saved, far_value, far_gain, far_table, far_cols, 1)
        for m in range(1, H):
            tail_copy(m).wait_send()
        for n in range(halves):
            there_copy(n, half_rows).wait_send()

    for build in to_send:
        build().wait_send()
    for which in range(2):
        for m in range(1, H):
            for c in range(n_cols):
                reduce_copy(which, m, c).wait_send()


def per_device(
    saved_input,
    cotangent,
    next_input,
    routes_saved,
    routes_next,
    norm_gain,
    router,
    expert_gate,
    expert_up,
    expert_down,
):
    E, H = lax.axis_size("expert"), lax.axis_size("hid")
    T, F = saved_input.shape[1:]
    D, ffd = expert_gate.shape[2:]
    cap = 3 * T // router.shape[2]
    tn = 2 * LANES if ffd % (2 * LANES) == 0 else LANES
    tw = 2 * LANES if F % (2 * LANES) == 0 else LANES
    n_cols, all_rows = F // tw, E * cap
    deep, wide = max(tn, tw), max(D, 2 * ffd)
    vmem = pl.BlockSpec(memory_space=pltpu.VMEM)
    hbm = pl.BlockSpec(memory_space=pl.ANY)
    dma = pltpu.SemaphoreType.DMA
    scratch = [
        pltpu.VMEM((3, all_rows, D), BF16),
        pltpu.VMEM((3, E - 1, cap, F), BF16),
        pltpu.VMEM((A_SLOTS, 2, D, deep), BF16),
        pltpu.VMEM((R_SLOTS, deep, wide), BF16),
        pltpu.VMEM((all_rows, ffd), F32),
        pltpu.VMEM((all_rows, ffd), BF16),
        pltpu.VMEM((2, all_rows, ffd), BF16),
        pltpu.VMEM((2, H - 1, n_cols, all_rows, tw), BF16),
        pltpu.VMEM((2, H - 1, n_cols, all_rows, tw), BF16),
        pltpu.VMEM((2, n_cols, all_rows, tw), F32),
        pltpu.VMEM((2, n_cols, all_rows, tw), BF16),
        pltpu.VMEM((2, all_rows, F), BF16),
        pltpu.VMEM((32, T), F32),
        pltpu.VMEM((H - 1, 32, T), F32),
        pltpu.VMEM((all_rows, LANES), F32),
        pltpu.VMEM((8, all_rows), F32),
        pltpu.VMEM((E - 1, 8, all_rows), F32),
        pltpu.VMEM((8, T), F32),
        pltpu.VMEM((H - 1, 8, T), F32),
        pltpu.VMEM((T, LANES), F32),
        pltpu.VMEM((T, F), F32),
        pltpu.VMEM((T, F), BF16),
        pltpu.VMEM((T, F), BF16),
        pltpu.VMEM((T, F), BF16),
        pltpu.VMEM((T, F), BF16),
        pltpu.VMEM((T, F), BF16),
        pltpu.VMEM((1, F), F32),
        pltpu.VMEM((E, F), F32),
        pltpu.VMEM((T, LANES), F32),
        pltpu.VMEM((H, 8, T), F32),
        dma((A_SLOTS, 2)),
        dma((R_SLOTS, 2)),
        dma((3, E)),
        dma((3, E)),
        dma((3, H, E)),
        dma((3, H, E)),
        dma((H,)),
        dma((H,)),
        dma((2, H, n_cols)),
        dma((2, H, n_cols)),
        dma((2, E, n_cols)),
        dma((2, E, n_cols)),
        dma((E,)),
        dma((E,)),
        dma((H,)),
        dma((H,)),
        dma((2,)),
        dma((2,)),
        dma((5 + n_cols,)),
        dma((5 + n_cols,)),
        dma((H,)),
        dma((H,)),
    ]
    result = pl.pallas_call(
        functools.partial(kernel, (E, H, T, F, D, ffd, cap, tn, tw)),
        out_shape=jax.ShapeDtypeStruct((2, T, F), BF16),
        in_specs=[vmem] * 7 + [hbm] * 3,
        out_specs=vmem,
        scratch_shapes=scratch,
        compiler_params=pltpu.CompilerParams(
            collective_id=0, has_side_effects=True, vmem_limit_bytes=67043328
        ),
        name="relay",
    )(
        saved_input[0], cotangent[0], next_input[0], routes_saved[0].T, routes_next[0].T, norm_gain, router[0].T,
        expert_gate[0, 0], expert_up[0, 0], expert_down[0, 0],
    )
    return (result[0:1], result[1:2])


def solution(mesh):
    placed = (
        P("section", "expert", "hid"),
        P("section", "expert", "hid"),
        P("section", "expert", "hid"),
        P("section", "expert", None),
        P("section", "expert", None),
        P("section", "hid"),
        P("section", "hid", None),
        P("section", "expert", None, "hid"),
        P("section", "expert", None, "hid"),
        P("section", "expert", "hid", None),
    )
    return jax.shard_map(
        per_device,
        mesh=mesh,
        in_specs=placed,
        out_specs=(P("section", "expert", "hid"), P("section", "expert", "hid")),
        check_vma=False,
    )
```

```python
import functools

import jax
import jax.numpy as jnp
from jax import lax
from jax.experimental import pallas as pl
from jax.experimental.pallas import tpu as pltpu
from jax.sharding import PartitionSpec as P

EPSILON = 1e-05
F32 = jnp.float32
BF16 = jnp.bfloat16
I32 = jnp.int32
NN = (((1,), (0,)), ((), ()))
NT = (((1,), (1,)), ((), ()))
LANES = 128
A_SLOTS = 3
R_SLOTS = 4
COT, NXT, SAV = 0, 1, 2


def bits_of(count):
    return [1 << bit for bit in range(count.bit_length() - 1)]


def low_bit(number):
    return number & -number


def flip(value, mask, count):
    total = 0
    for bit in bits_of(count):
        own = lax.rem(lax.div(value, bit), 2)
        if isinstance(mask, int):
            got = 1 - own if mask & bit else own
        else:
            other = lax.rem(lax.div(mask, bit), 2)
            got = own + other - 2 * own * other
        total = total + bit * got
    return total


def dot(a, b, dims=NN):
    return lax.dot_general(a, b, dims, preferred_element_type=F32)


def kernel(
    sizes,
    saved_ref, cot_ref, next_ref, pair_saved_ref, pair_next_ref, gain_ref, table_ref, wg_ref, wu_ref, wd_ref,
    out_ref,
    rows, slots, wa, wr, gh, hid_n, grads, rs_send, rs_recv, own_part, home_send, home,
    stat_send, stat_recv, dots_acc, dots_send, dots_recv, tail_send, tail_recv,
    cols, mixed, there_send, there_recv, far_cot, far_saved, far_value, far_gain, far_table, far_cols, far_tail,
    wa_sem, wr_sem,
    z_send, z_recv, g_send, g_recv, s_send, s_recv, r_send, r_recv,
    b_send, b_recv, d_send, d_recv, t_send, t_recv, y_send, y_recv, e_send, e_recv, f_send, f_recv,
):
    E, H, T, F, D, ffd, cap, tn, tw = sizes
    n_tiles, n_cols = ffd // tn, F // tw
    steps = H * n_cols
    all_rows = E * cap
    sec, me, hi = lax.axis_index("section"), lax.axis_index("expert"), lax.axis_index("hid")
    hid_peer = [flip(hi, m, H) for m in range(H)]
    exp_peer = [flip(me, k, E) for k in range(E)]
    to_send = []
    none = me * 0

    def remote(src, dst, send, recv, e=None, h=None, s=None):
        where = (sec if s is None else s, me if e is None else e, hi if h is None else h)
        return pltpu.make_async_remote_copy(
            src_ref=src, dst_ref=dst, send_sem=send, recv_sem=recv,
            device_id=where, device_id_type=pl.DeviceIdType.MESH,
        )

    def send(build):
        build().start()
        to_send.append(build)

    def place_of(i, kind):
        if kind == "out":
            return H - 1 - lax.div(i, n_cols // 2), lax.rem(i, n_cols // 2)
        at = lax.rem(i, H)
        return H - 1 - 2 * at + lax.div(at, H // 2) * (H - 1), lax.div(i, H)

    def out_copy(i, slot):
        m, c = place_of(i, "out")
        col = pl.multiple_of(flip(hi, m, H) * F + c * 2 * tw, 2 * tw)
        return pltpu.make_async_copy(
            wd_ref.at[:, pl.ds(col, 2 * tw)], wa.at[slot, pl.ds(0, ffd), pl.ds(0, 2 * tw)], wa_sem.at[slot, 0])

    def a_copies(kind, j, slot):
        if kind == "out":
            return [out_copy(j, slot)]
        col = pl.multiple_of(j * tn, tn)
        return [
            pltpu.make_async_copy(w.at[:, pl.ds(col, tn)], wa.at[slot, :, pl.ds(half * tn, tn)], wa_sem.at[slot, half])
            for half, w in enumerate((wg_ref, wu_ref))
        ]

    out_items = steps // 2

    def start_a(g):
        slot = lax.rem(g, A_SLOTS)

        @pl.when((g < n_tiles) | (g >= n_tiles + out_items) & (g < 2 * n_tiles + out_items))
        def _():
            for copy in a_copies("pair", lax.rem(jnp.where(g < n_tiles, g, g - out_items - n_tiles), n_tiles), slot):
                copy.start()

        @pl.when((g >= n_tiles) & (g < n_tiles + out_items))
        def _():
            for copy in a_copies("out", g - n_tiles, slot):
                copy.start()

    def gh_copy(j):
        slot = lax.rem(j, R_SLOTS)
        return pltpu.make_async_copy(
            wd_ref.at[pl.ds(pl.multiple_of(j * tn, tn), tn), :], wr.at[slot, pl.ds(0, tn), pl.ds(0, D)],
            wr_sem.at[slot, 0])

    def back_copies(i):
        slot = lax.rem(i, R_SLOTS)
        m, c = place_of(i, "back")
        row = pl.multiple_of(flip(hi, m, H) * F + c * tw, tw)
        return [
            pltpu.make_async_copy(
                w.at[pl.ds(row, tw), :], wr.at[slot, pl.ds(0, tw), pl.ds(half * ffd, ffd)], wr_sem.at[slot, half])
            for half, w in enumerate((wg_ref, wu_ref))
        ]

    for j in range(min(R_SLOTS - 1, n_tiles)):
        gh_copy(none + j).start()
    for g in range(A_SLOTS - 1):
        for copy in a_copies("pair", none + g, none + g):
            copy.start()

    barrier = pltpu.get_barrier_semaphore()
    partners = [(sec, me, hid_peer[m]) for m in range(1, H)]
    partners += [(sec, exp_peer[k], hi) for k in range(1, E)]
    partners += [(1 - sec, me, hid_peer[m]) for m in range(H)]
    for where in partners:
        pl.semaphore_signal(barrier, inc=1, device_id=where, device_id_type=pl.DeviceIdType.MESH)
    lane = lax.broadcasted_iota(I32, (T, LANES), 1)
    gain = gain_ref[...]
    route_rows = jnp.concatenate(
        [pair_saved_ref[...].astype(F32), pair_next_ref[...].astype(F32), jnp.zeros((LANES - 4, T), F32)], axis=0)
    spread = route_rows.T
    route_cols = [spread[:, n:n + 1] for n in range(4)]
    first_i = lax.broadcasted_iota(I32, (T, T), 0)
    second_i = lax.broadcasted_iota(I32, (T, T), 1)
    upper = jnp.where(first_i < second_i, 1.0, 0.0).astype(BF16)
    lower = jnp.where(first_i > second_i, 1.0, 0.0).astype(BF16)
    slot_i = lax.broadcasted_iota(I32, (cap, T), 0).astype(F32)
    lane_f = lane.astype(F32)

    def chosen(base, expert):
        first, second = route_rows[base:base + 1], route_rows[base + 1:base + 2]
        wanted = expert.astype(F32)
        hit = jnp.where(first == wanted, 1.0, 0.0) + jnp.where(second == wanted, 1.0, 0.0)
        rank = dot(jnp.broadcast_to(hit, (16, T)).astype(BF16), upper)[0:1]
        rank = jnp.where(hit > 0.5, rank, -1.0)
        return jnp.where(slot_i == rank, 1.0, 0.0).astype(BF16)

    def put(n, value):
        cols[:, n:n + 1] = value

    for n, base in enumerate((0, 2)):
        hits = jnp.where(lane_f == route_cols[base], 1.0, 0.0) + jnp.where(lane_f == route_cols[base + 1], 1.0, 0.0)
        ranks = dot(lower, hits.astype(BF16))
        for c in range(2):
            route = route_cols[base + c]
            put(16 + 2 * n + c, jnp.sum(jnp.where(lane_f == route, ranks, 0.0), axis=1, keepdims=True))
            put(20 + 2 * n + c, route)

    pl.semaphore_wait(barrier, len(partners))

    order = list(range(E - 1, 0, -1))
    inner = flip(lax.rem(me, 2), lax.rem(lax.div(me, 2), 2), 2)
    first_sends = ([1, 3, 2], [1, 3, 2]) if E == 4 else (order, order)
    late_send = None
    arrivals = ([1, 3, 2], [1, 3, 2]) if E == 4 else (order, order)

    def by_class(build):
        if E != 4:
            build(0)
            return
        for kind in range(2):
            pl.when(inner == kind)(functools.partial(build, kind))

    def first_wave(tau):
        by_class(lambda kind: [dispatch_copy(tau, k).start() for k in first_sends[kind]] and None)


    def region(tau, expert, feature):
        return rows.at[tau, pl.ds(pl.multiple_of(expert * cap, 16), cap), pl.ds(pl.multiple_of(feature * F, LANES), F)]

    def forward_copy(tau, piece, bit, k):
        part = region(tau, exp_peer[k], hid_peer[piece])
        return remote(part, part, g_send.at[tau, piece + bit, k], g_recv.at[tau, piece + bit, k], h=hid_peer[bit])

    def forwards(tau, piece, k):
        return [
            functools.partial(forward_copy, tau, piece, bit, k)
            for bit in reversed(bits_of(H)) if piece == 0 or bit < low_bit(piece)
        ]

    def forward(tau, k):
        for build in forwards(tau, 0, k):
            build().start()

    def got_piece(tau, piece, k):
        part = region(tau, exp_peer[k], hid_peer[piece])
        remote(part, part, g_send.at[tau, piece, k], g_recv.at[tau, piece, k], h=hid_peer[low_bit(piece)]).wait_recv()

    def dispatch_copy(tau, k):
        return remote(
            slots.at[tau, k - 1], region(tau, me, hi), z_send.at[tau, k], z_recv.at[tau, k], e=exp_peer[k])

    def dispatch(tau, base, tokens):
        for k in order + [0]:
            picked = dot(chosen(base, exp_peer[k]), tokens).astype(BF16)
            if k == 0:
                rows[tau, pl.ds(pl.multiple_of(me * cap, 16), cap), pl.ds(pl.multiple_of(hi * F, LANES), F)] = picked
            else:
                slots[tau, k - 1] = picked

    def z_event(tau, n):
        def take(kind):
            k = arrivals[kind][n]
            part = region(tau, exp_peer[k], hi)
            remote(part, part, z_send.at[tau, k], z_recv.at[tau, k], e=exp_peer[k]).wait_recv()
            for build in forwards(tau, 0, k):
                build().start()
            if n == 0 and kind == 1 and late_send:
                dispatch_copy(tau, late_send).start()
            if tau < SAV and n == E - 2:
                for k in first_sends[kind]:
                    dispatch_copy(tau + 1, k).start()

        by_class(take)
        if tau < SAV and n == 0:
            forward(tau + 1, 0)

    relays = [p for top in reversed(bits_of(H)) if top > 1 for p in range(top, H, 2 * top)]

    def relay(tau, k):
        for piece in relays:
            got_piece(tau, piece, k)
            for build in forwards(tau, piece, k):
                build().start()

    def x_event(tau, n):
        if n == 0:
            relay(tau, 0)
        else:
            by_class(lambda kind: relay(tau, arrivals[kind][n - 1]))

    def gather_events(tau):
        events = [functools.partial(x_event, tau, 0)]
        for n in range(E - 1):
            events.insert(-1, functools.partial(z_event, tau, n))
            events.append(functools.partial(x_event, tau, n + 1))
        return events

    def complete(tau):
        for piece in range(1, H, 2):
            for k in range(E):
                got_piece(tau, piece, k)

    stats = jnp.zeros((T, LANES), F32)
    for offset, ref in ((0, saved_ref), (16, next_ref)):
        values = ref[...].astype(F32)
        stats = stats + jnp.where(lane == offset, jnp.sum(values * values, axis=1, keepdims=True), 0.0)
        for e in range(E):
            weights = table_ref[e:e + 1, :] * gain
            stats = stats + jnp.where(lane == offset + 1 + e, jnp.sum(values * weights, axis=1, keepdims=True), 0.0)
    stat_send[...] = stats.T[0:32]

    def all_to_hid(src, dst, sent, recv):
        copies = [remote(src, dst.at[m - 1], sent.at[m], recv.at[m], h=hid_peer[m]) for m in range(1, H)]
        for copy in copies:
            send(lambda copy=copy: copy)
        return copies

    stat_copies = all_to_hid(stat_send, stat_recv, s_send, s_recv)

    dispatch(COT, 0, cot_ref[...])
    first_wave(COT)
    forward(COT, 0)

    total = stats.T[0:32]
    for m, copy in enumerate(stat_copies):
        copy.wait_recv()
        total = total + stat_recv[m]
    stats = jnp.concatenate([total, jnp.zeros((LANES - 32, T), F32)], axis=0).T

    def finish_norm(offset, base, ref, keep):
        scale = lax.rsqrt(stats[:, offset:offset + 1] / D + EPSILON)
        first_score = jnp.zeros((T, 1), F32)
        second_score = jnp.zeros((T, 1), F32)
        for e in range(E):
            score = stats[:, offset + 1 + e:offset + 2 + e]
            first_score = first_score + jnp.where(route_cols[base] == e, score, 0.0)
            second_score = second_score + jnp.where(route_cols[base + 1] == e, score, 0.0)
        first, second = first_score * scale, second_score * scale
        put(keep, jax.nn.sigmoid(first - second))
        put(keep + 1, jax.nn.sigmoid(second - first))
        put(keep + 2, scale)
        put(keep + 3, first_score - second_score)
        return (ref[...].astype(F32) * scale * gain).astype(BF16)

    dispatch(NXT, 2, finish_norm(16, 2, next_ref, 4))
    dispatch(SAV, 0, finish_norm(0, 0, saved_ref, 0))

    far = [(cot_ref, far_cot), (saved_ref, far_saved), (gain_ref, far_gain), (table_ref, far_table), (cols, far_cols)]

    def far_copy(n):
        return remote(far[n][0], far[n][1], e_send.at[n], e_recv.at[n], s=1 - sec)

    def far_value_copy(c):
        part = pl.ds(c * tw, tw)
        n = len(far) + c
        return remote(there_send.at[:, part], far_value.at[:, part], e_send.at[n], e_recv.at[n], s=1 - sec)

    @pl.when(sec == 1)
    def _():
        for n in range(len(far)):
            far_copy(n).start()

    def reduce_step(which, acc, m_now, c):

        @pl.when(m_now == 0)
        def _():
            own_part[which, c] = acc

        for m in range(1, H):
            @pl.when(m_now == m)
            def _():
                value = acc
                for bit in bits_of(low_bit(m) * 2)[:-1]:
                    received(which, m + bit, c)
                    value = value + rs_recv[which, m + bit - 1, c].astype(F32)
                rs_send[which, m - 1, c] = value.astype(BF16)
                reduce_copy(which, m, c).start()

    def reduce_copy(which, m, c):
        return remote(
            rs_send.at[which, m - 1, c], rs_recv.at[which, m - 1, c],
            r_send.at[which, m, c], r_recv.at[which, m, c], h=hid_peer[low_bit(m)])

    def received(which, m, c):
        reduce_copy(which, m, c).wait_recv()

    def home_region(which, expert, c):
        return home.at[which, pl.ds(pl.multiple_of(expert * cap, 16), cap), pl.ds(c * tw, tw)]

    def home_copy(which, k, c):
        return remote(
            home_send.at[which, c, pl.ds(pl.multiple_of(exp_peer[k] * cap, 16), cap)], home_region(which, me, c),
            b_send.at[which, k, c], b_recv.at[which, k, c], e=exp_peer[k])

    def home_event(which, c):
        value = own_part[which, c]
        for bit in bits_of(H):
            received(which, bit, c)
            value = value + rs_recv[which, bit - 1, c].astype(F32)
        home_send[which, c] = value.astype(BF16)
        for k in order:
            send(functools.partial(home_copy, which, k, c))
        mine = pl.ds(pl.multiple_of(me * cap, 16), cap)
        home[which, mine, c * tw:(c + 1) * tw] = home_send[which, c, mine, :]

    def home_wait(which, c):
        for k in order:
            part = home_region(which, exp_peer[k], c)
            remote(part, part, b_send.at[which, k, c], b_recv.at[which, k, c], e=exp_peer[k]).wait_recv()

    wide_i = lax.broadcasted_iota(I32, (T, all_rows), 1).astype(F32)

    def selectors(n):
        picks = []
        for c in range(2):
            rank, route = cols[:, 16 + 2 * n + c:17 + 2 * n + c], cols[:, 20 + 2 * n + c:21 + 2 * n + c]
            picks.append(jnp.where(wide_i == route * cap + rank, 1.0, 0.0).astype(BF16))
        return picks

    def blended(which, n, keep, c, picks):
        part = home[which, :, c * tw:(c + 1) * tw]
        return cols[:, keep:keep + 1] * dot(picks[0], part) + cols[:, keep + 1:keep + 2] * dot(picks[1], part)

    def there_copy(n, height):
        part = pl.ds(n * height, height)
        return remote(there_send.at[part], there_recv.at[part], y_send.at[n], y_recv.at[n], s=1 - sec)

    halves = 2
    half_rows = T // halves

    def forward_out():
        picks = selectors(1)
        for c in range(n_cols):
            home_wait(0, c)
            part = slice(c * tw, (c + 1) * tw)
            value = (next_ref[:, part].astype(F32) + blended(0, 1, 4, c, picks)).astype(BF16)

            @pl.when(sec == 0)
            def _():
                there_send[:, part] = value

            @pl.when(sec == 1)
            def _():
                out_ref[0, :, part] = value

        @pl.when(sec == 0)
        def _():
            for n in range(halves):
                there_copy(n, half_rows).start()

    def run(events, index):
        for at, event in events:
            pl.when(index == at)(event)

    def place(events, spots, limit):
        return [(min(spot, limit - 1), event) for event, spot in zip(events, spots)]

    for event in gather_events(COT):
        event()
    complete(COT)
    next_events = gather_events(NXT)
    for event in next_events[:2]:
        event()
    early = len(next_events) // 2 + 1
    gh_events = place(next_events[2:early], [n_tiles // 2 + n for n in range(early - 2)], n_tiles)

    @pl.loop(0, n_tiles)
    def _(j):
        @pl.when(j + R_SLOTS - 1 < n_tiles)
        def _():
            gh_copy(j + R_SLOTS - 1).start()

        gh_copy(j).wait()
        slot = lax.rem(j, R_SLOTS)
        gh[:, pl.ds(pl.multiple_of(j * tn, tn), tn)] = dot(rows[COT], wr[slot, 0:tn, 0:D], NT)
        run(gh_events, j)

    for i in range(R_SLOTS - 1):
        for copy in back_copies(none + i):
            copy.start()

    for event in next_events[early:]:
        event()
    complete(NXT)

    saved_events = gather_events(SAV)
    saved_events[0]()
    late = 2
    count = len(saved_events) - late
    spots = [n_tiles - count + n for n in range(count)]
    up_events = place(saved_events[1:count], [max(0, spot) for spot in spots[1:]], n_tiles)

    @pl.loop(0, n_tiles)
    def _(j):
        start_a(j + A_SLOTS - 1)
        slot = lax.rem(j, A_SLOTS)
        for copy in a_copies("pair", j, slot):
            copy.wait()
        both = dot(rows[NXT], wa[slot, :, 0:2 * tn])
        gate, up = both[:, 0:tn], both[:, tn:2 * tn]
        hid_n[:, pl.ds(pl.multiple_of(j * tn, tn), tn)] = (gate * jax.nn.sigmoid(gate) * up).astype(BF16)
        run(up_events, j)

    out_events = place(saved_events[count:], [out_items // 4, out_items // 2], out_items)

    @pl.loop(0, out_items)
    def _(i):
        g = n_tiles + i
        start_a(g + A_SLOTS - 1)
        slot = lax.rem(g, A_SLOTS)
        out_copy(i, slot).wait()
        acc = dot(hid_n[...], wa[slot, 0:ffd, 0:2 * tw])
        m, c = place_of(i, "out")
        for half in range(2):
            reduce_step(0, acc[:, half * tw:(half + 1) * tw], m, 2 * c + half)
        run(out_events, i)

    complete(SAV)

    dots_acc[...] = jnp.zeros_like(dots_acc)
    down_spots = [1 + 2 * c for c in range(n_cols)]
    in_gate = [c for c in range(n_cols) if down_spots[c] < n_tiles - 1]
    gate_events = [(down_spots[c], functools.partial(home_event, 0, c)) for c in in_gate]

    @pl.loop(0, n_tiles)
    def _(j):
        g = n_tiles + out_items + j
        start_a(g + A_SLOTS - 1)
        slot = lax.rem(g, A_SLOTS)
        for copy in a_copies("pair", j, slot):
            copy.wait()
        both = dot(rows[SAV], wa[slot, :, 0:2 * tn])
        gate, up = both[:, 0:tn], both[:, tn:2 * tn]
        part = pl.ds(pl.multiple_of(j * tn, tn), tn)
        grad = gh[:, part]
        sig = jax.nn.sigmoid(gate)
        silu = gate * sig
        hidden = (silu * up).astype(BF16).astype(F32)
        grads[0, :, part] = (grad * up * (sig * (1.0 + gate * (1.0 - sig)))).astype(BF16)
        grads[1, :, part] = (grad * silu).astype(BF16)
        product = grad * hidden
        partial = product[:, 0:LANES]
        for n in range(1, tn // LANES):
            partial = partial + product[:, n * LANES:(n + 1) * LANES]
        dots_acc[...] += partial
        run(gate_events, j)

    def dots_copy(k):
        return remote(dots_send, dots_recv.at[k - 1], d_send.at[k], d_recv.at[k], e=exp_peer[k])

    dots_send[...] = jnp.broadcast_to(jnp.sum(dots_acc[...].T, axis=0, keepdims=True), (8, all_rows))
    for k in order:
        send(functools.partial(dots_copy, k))

    def dots_event():
        for k in order:
            dots_copy(k).wait_recv()
        gap = jnp.zeros((T, 1), F32)
        for k in range(E):
            row = dots_send[0:1] if k == 0 else dots_recv[k - 1, 0:1]
            expert = exp_peer[k].astype(F32)
            for c, sign in ((0, 1.0), (1, -1.0)):
                rank, route = cols[:, 16 + c:17 + c], cols[:, 20 + c:21 + c]
                spot = jnp.where(route == expert, me.astype(F32) * cap + rank, -1.0)
                gap = gap + sign * jnp.sum(jnp.where(wide_i == spot, row, 0.0), axis=1, keepdims=True)
        dots_acc[0:T, 0:1] = gap

    late_events = [(1 + 2 * n, functools.partial(home_event, 0, c)) for n, c in enumerate(c for c in range(n_cols) if c not in in_gate)]
    soon = [c for c in range(n_cols) if H * (c + 2) < steps]
    back_events = late_events + [(H * (c + 2), functools.partial(home_event, 1, c)) for c in soon]

    @pl.loop(0, steps)
    def _(i):
        @pl.when(i + R_SLOTS - 1 < steps)
        def _():
            for copy in back_copies(i + R_SLOTS - 1):
                copy.start()

        for copy in back_copies(i):
            copy.wait()
        slot = lax.rem(i, R_SLOTS)
        acc = dot(grads[0], wr[slot, 0:tw, 0:ffd], NT) + dot(grads[1], wr[slot, 0:tw, ffd:2 * ffd], NT)
        reduce_step(1, acc, *place_of(i, "back"))
        run(back_events, i)

    later = [c for c in range(n_cols) if c not in soon]
    for c in later[:-1]:
        home_event(1, c)
    forward_out()
    dots_event()
    home_event(1, later[-1])
    picks = selectors(0)
    inner = jnp.zeros((T, 1), F32)
    for c in range(n_cols):
        home_wait(1, c)
        part = slice(c * tw, (c + 1) * tw)
        value = blended(1, 0, 0, c, picks) * gain_ref[:, part]
        mixed[:, part] = value

        @pl.when(sec == 1)
        def _():
            there_send[:, part] = value.astype(BF16)
            far_value_copy(c).start()

        inner = inner + jnp.sum(value * saved_ref[:, part].astype(F32), axis=1, keepdims=True)
    message = jnp.where(lane == 0, inner, 0.0) + jnp.where(lane == 1, dots_acc[0:T, 0:1], 0.0)
    message = message.T[0:8]
    tail_send[...] = message

    def tail_copy(m):
        return remote(tail_send, tail_recv.at[m - 1], t_send.at[m], t_recv.at[m], h=hid_peer[m])

    def far_tail_copy(m):
        return remote(tail_send, far_tail.at[m], f_send.at[m], f_recv.at[m], h=hid_peer[m], s=1 - sec)

    def input_gradient(message, cot, saved, value_of, gains, table, kept, place_in):
        message = jnp.concatenate([message, jnp.zeros((LANES - 8, T), F32)], axis=0).T
        scale = kept[:, 2:3]
        slope = message[:, 1:2] * kept[:, 0:1] * kept[:, 1:2]
        inner = message[:, 0:1] + slope * kept[:, 3:4]
        pull = scale * scale * scale * (inner / D)
        for n in range(halves):
            part = slice(n * half_rows, (n + 1) * half_rows)
            lean = jnp.zeros((half_rows, F), F32)
            for e in range(E):
                sign = jnp.where(kept[part, 20:21] == e, 1.0, 0.0) - jnp.where(kept[part, 21:22] == e, 1.0, 0.0)
                lean = lean + sign * table[e:e + 1, :]
            grad = value_of[part, :].astype(F32) + slope[part] * lean * gains[...]
            out_ref[place_in, part, :] = (
                cot[part, :].astype(F32) + scale[part] * grad - saved[part, :].astype(F32) * pull[part]
            ).astype(BF16)

    @pl.when(sec == 1)
    def _():
        for m in range(H):
            far_tail_copy(m).start()
        for n in range(halves):
            there_copy(n, half_rows).wait_recv()
        out_ref[1] = there_recv[...]
        for n in range(len(far)):
            far_copy(n).wait_send()
        for c in range(n_cols):
            far_value_copy(c).wait_send()
        for m in range(H):
            far_tail_copy(m).wait_send()

    @pl.when(sec == 0)
    def _():
        for m in range(1, H):
            tail_copy(m).start()
        total = message
        for m in range(1, H):
            tail_copy(m).wait_recv()
            total = total + tail_recv[m - 1]
        input_gradient(total, cot_ref, saved_ref, mixed, gain_ref, table_ref, cols, 0)
        for n in range(len(far)):
            far_copy(n).wait_recv()
        for c in range(n_cols):
            far_value_copy(c).wait_recv()
        total = jnp.zeros((8, T), F32)
        for m in range(H):
            far_tail_copy(m).wait_recv()
            total = total + far_tail[m]
        input_gradient(total, far_cot, far_saved, far_value, far_gain, far_table, far_cols, 1)
        for m in range(1, H):
            tail_copy(m).wait_send()
        for n in range(halves):
            there_copy(n, half_rows).wait_send()

    for build in to_send:
        build().wait_send()
    for tau in range(3):
        for k in range(E):
            if k:
                dispatch_copy(tau, k).wait_send()
            for piece in [0] + relays:
                for build in forwards(tau, piece, k):
                    build().wait_send()
    for which in range(2):
        for m in range(1, H):
            for c in range(n_cols):
                reduce_copy(which, m, c).wait_send()


def per_device(
    saved_input,
    cotangent,
    next_input,
    routes_saved,
    routes_next,
    norm_gain,
    router,
    expert_gate,
    expert_up,
    expert_down,
):
    E, H = lax.axis_size("expert"), lax.axis_size("hid")
    T, F = saved_input.shape[1:]
    D, ffd = expert_gate.shape[2:]
    cap = 3 * T // router.shape[2]
    tn = 2 * LANES if ffd % (2 * LANES) == 0 else LANES
    tw = 2 * LANES if F % (2 * LANES) == 0 else LANES
    n_cols, all_rows = F // tw, E * cap
    deep, wide = max(tn, tw), max(D, 2 * ffd)
    vmem = pl.BlockSpec(memory_space=pltpu.VMEM)
    hbm = pl.BlockSpec(memory_space=pl.ANY)
    dma = pltpu.SemaphoreType.DMA
    scratch = [
        pltpu.VMEM((3, all_rows, D), BF16),
        pltpu.VMEM((3, E - 1, cap, F), BF16),
        pltpu.VMEM((A_SLOTS, D, 2 * deep), BF16),
        pltpu.VMEM((R_SLOTS, deep, wide), BF16),
        pltpu.VMEM((all_rows, ffd), F32),
        pltpu.VMEM((all_rows, ffd), BF16),
        pltpu.VMEM((2, all_rows, ffd), BF16),
        pltpu.VMEM((2, H - 1, n_cols, all_rows, tw), BF16),
        pltpu.VMEM((2, H - 1, n_cols, all_rows, tw), BF16),
        pltpu.VMEM((2, n_cols, all_rows, tw), F32),
        pltpu.VMEM((2, n_cols, all_rows, tw), BF16),
        pltpu.VMEM((2, all_rows, F), BF16),
        pltpu.VMEM((32, T), F32),
        pltpu.VMEM((H - 1, 32, T), F32),
        pltpu.VMEM((all_rows, LANES), F32),
        pltpu.VMEM((8, all_rows), F32),
        pltpu.VMEM((E - 1, 8, all_rows), F32),
        pltpu.VMEM((8, T), F32),
        pltpu.VMEM((H - 1, 8, T), F32),
        pltpu.VMEM((T, LANES), F32),
        pltpu.VMEM((T, F), F32),
        pltpu.VMEM((T, F), BF16),
        pltpu.VMEM((T, F), BF16),
        pltpu.VMEM((T, F), BF16),
        pltpu.VMEM((T, F), BF16),
        pltpu.VMEM((T, F), BF16),
        pltpu.VMEM((1, F), F32),
        pltpu.VMEM((E, F), F32),
        pltpu.VMEM((T, LANES), F32),
        pltpu.VMEM((H, 8, T), F32),
        dma((A_SLOTS, 2)),
        dma((R_SLOTS, 2)),
        dma((3, E)),
        dma((3, E)),
        dma((3, H, E)),
        dma((3, H, E)),
        dma((H,)),
        dma((H,)),
        dma((2, H, n_cols)),
        dma((2, H, n_cols)),
        dma((2, E, n_cols)),
        dma((2, E, n_cols)),
        dma((E,)),
        dma((E,)),
        dma((H,)),
        dma((H,)),
        dma((2,)),
        dma((2,)),
        dma((5 + n_cols,)),
        dma((5 + n_cols,)),
        dma((H,)),
        dma((H,)),
    ]
    result = pl.pallas_call(
        functools.partial(kernel, (E, H, T, F, D, ffd, cap, tn, tw)),
        out_shape=jax.ShapeDtypeStruct((2, T, F), BF16),
        in_specs=[vmem] * 7 + [hbm] * 3,
        out_specs=vmem,
        scratch_shapes=scratch,
        compiler_params=pltpu.CompilerParams(
            collective_id=0, has_side_effects=True, vmem_limit_bytes=67043328
        ),
        name="relay",
    )(
        saved_input[0], cotangent[0], next_input[0], routes_saved[0].T, routes_next[0].T, norm_gain, router[0].T,
        expert_gate[0, 0], expert_up[0, 0], expert_down[0, 0],
    )
    return (result[0:1], result[1:2])


def solution(mesh):
    placed = (
        P("section", "expert", "hid"),
        P("section", "expert", "hid"),
        P("section", "expert", "hid"),
        P("section", "expert", None),
        P("section", "expert", None),
        P("section", "hid"),
        P("section", "hid", None),
        P("section", "expert", None, "hid"),
        P("section", "expert", None, "hid"),
        P("section", "expert", "hid", None),
    )
    return jax.shard_map(
        per_device,
        mesh=mesh,
        in_specs=placed,
        out_specs=(P("section", "expert", "hid"), P("section", "expert", "hid")),
        check_vma=False,
    )
```

```python
import functools

import jax
import jax.numpy as jnp
from jax import lax
from jax.experimental import pallas as pl
from jax.experimental.pallas import tpu as pltpu
from jax.sharding import PartitionSpec as P

EPSILON = 1e-05
F32 = jnp.float32
BF16 = jnp.bfloat16
I32 = jnp.int32
NN = (((1,), (0,)), ((), ()))
NT = (((1,), (1,)), ((), ()))
LANES = 128
A_SLOTS = 3
R_SLOTS = 4
NXT, SAV, COT = 0, 1, 2


def bits_of(count):
    return [1 << bit for bit in range(count.bit_length() - 1)]


def low_bit(number):
    return number & -number


def flip(value, mask, count):
    total = 0
    for bit in bits_of(count):
        own = lax.rem(lax.div(value, bit), 2)
        if isinstance(mask, int):
            got = 1 - own if mask & bit else own
        else:
            other = lax.rem(lax.div(mask, bit), 2)
            got = own + other - 2 * own * other
        total = total + bit * got
    return total


def dot(a, b, dims=NN):
    return lax.dot_general(a, b, dims, preferred_element_type=F32)


def kernel(
    sizes,
    saved_ref, cot_ref, next_ref, pair_saved_ref, pair_next_ref, gain_ref, table_ref, wg_ref, wu_ref, wd_ref,
    out_ref,
    rows, slots, wa, wr, pair, hid_n, grads, rs_send, rs_recv, own_part, home_send, home,
    stat_send, stat_recv, dots_acc, dots_send, dots_recv, tail_send, tail_recv,
    cols, mixed, there_send, there_recv, far_cot, far_saved, far_value, far_gain, far_table, far_cols, far_tail,
    wa_sem, wr_sem,
    z_send, z_recv, g_send, g_recv, s_send, s_recv, r_send, r_recv,
    b_send, b_recv, d_send, d_recv, t_send, t_recv, y_send, y_recv, e_send, e_recv, f_send, f_recv,
):
    E, H, T, F, D, ffd, cap, tn, tw = sizes
    n_tiles, n_cols = ffd // tn, F // tw
    steps = H * n_cols
    all_rows = E * cap
    sec, me, hi = lax.axis_index("section"), lax.axis_index("expert"), lax.axis_index("hid")
    hid_peer = [flip(hi, m, H) for m in range(H)]
    exp_peer = [flip(me, k, E) for k in range(E)]
    to_send = []
    none = me * 0

    def remote(src, dst, send, recv, e=None, h=None, s=None):
        where = (sec if s is None else s, me if e is None else e, hi if h is None else h)
        return pltpu.make_async_remote_copy(
            src_ref=src, dst_ref=dst, send_sem=send, recv_sem=recv,
            device_id=where, device_id_type=pl.DeviceIdType.MESH,
        )

    def send(build):
        build().start()
        to_send.append(build)

    def place_of(i, kind):
        if kind == "out":
            return H - 1 - lax.div(i, n_cols // 2), lax.rem(i, n_cols // 2)
        at = lax.rem(i, H)
        return H - 1 - 2 * at + lax.div(at, H // 2) * (H - 1), lax.div(i, H)

    def out_copy(i, slot):
        m, c = place_of(i, "out")
        col = pl.multiple_of(flip(hi, m, H) * F + c * 2 * tw, 2 * tw)
        return pltpu.make_async_copy(
            wd_ref.at[:, pl.ds(col, 2 * tw)], wa.at[slot, pl.ds(0, ffd), pl.ds(0, 2 * tw)], wa_sem.at[slot, 0])

    def a_copies(kind, j, slot):
        if kind == "out":
            return [out_copy(j, slot)]
        col = pl.multiple_of(j * tn, tn)
        return [
            pltpu.make_async_copy(w.at[:, pl.ds(col, tn)], wa.at[slot, :, pl.ds(half * tn, tn)], wa_sem.at[slot, half])
            for half, w in enumerate((wg_ref, wu_ref))
        ]

    out_items = steps // 2

    def start_a(g):
        slot = lax.rem(g, A_SLOTS)

        @pl.when((g < n_tiles) | (g >= n_tiles + out_items) & (g < 2 * n_tiles + out_items))
        def _():
            for copy in a_copies("pair", lax.rem(jnp.where(g < n_tiles, g, g - out_items - n_tiles), n_tiles), slot):
                copy.start()

        @pl.when((g >= n_tiles) & (g < n_tiles + out_items))
        def _():
            for copy in a_copies("out", g - n_tiles, slot):
                copy.start()

    def gh_copy(j):
        slot = lax.rem(j, R_SLOTS)
        return pltpu.make_async_copy(
            wd_ref.at[pl.ds(pl.multiple_of(j * tn, tn), tn), :], wr.at[slot, pl.ds(0, tn), pl.ds(0, D)],
            wr_sem.at[slot, 0])

    def back_copies(i):
        slot = lax.rem(n_tiles + i, R_SLOTS)
        m, c = place_of(i, "back")
        row = pl.multiple_of(flip(hi, m, H) * F + c * tw, tw)
        return [
            pltpu.make_async_copy(
                w.at[pl.ds(row, tw), :], wr.at[slot, pl.ds(0, tw), pl.ds(half * ffd, ffd)], wr_sem.at[slot, half])
            for half, w in enumerate((wg_ref, wu_ref))
        ]

    def start_r(g):
        @pl.when(g < n_tiles)
        def _():
            gh_copy(g).start()

        @pl.when((g >= n_tiles) & (g < n_tiles + steps))
        def _():
            for copy in back_copies(g - n_tiles):
                copy.start()

    for j in range(min(R_SLOTS - 1, n_tiles)):
        gh_copy(none + j).start()
    for g in range(A_SLOTS - 1):
        for copy in a_copies("pair", none + g, none + g):
            copy.start()

    barrier = pltpu.get_barrier_semaphore()
    partners = [(sec, me, hid_peer[m]) for m in range(1, H)]
    partners += [(sec, exp_peer[k], hi) for k in range(1, E)]
    partners += [(1 - sec, me, hid_peer[m]) for m in range(H)]
    for where in partners:
        pl.semaphore_signal(barrier, inc=1, device_id=where, device_id_type=pl.DeviceIdType.MESH)
    lane = lax.broadcasted_iota(I32, (T, LANES), 1)
    gain = gain_ref[...]
    route_rows = jnp.concatenate(
        [pair_saved_ref[...].astype(F32), pair_next_ref[...].astype(F32), jnp.zeros((LANES - 4, T), F32)], axis=0)
    spread = route_rows.T
    route_cols = [spread[:, n:n + 1] for n in range(4)]
    first_i = lax.broadcasted_iota(I32, (T, T), 0)
    second_i = lax.broadcasted_iota(I32, (T, T), 1)
    upper = jnp.where(first_i < second_i, 1.0, 0.0).astype(BF16)
    lower = jnp.where(first_i > second_i, 1.0, 0.0).astype(BF16)
    slot_i = lax.broadcasted_iota(I32, (cap, T), 0).astype(F32)
    lane_f = lane.astype(F32)

    def chosen(base, expert):
        first, second = route_rows[base:base + 1], route_rows[base + 1:base + 2]
        wanted = expert.astype(F32)
        hit = jnp.where(first == wanted, 1.0, 0.0) + jnp.where(second == wanted, 1.0, 0.0)
        rank = dot(jnp.broadcast_to(hit, (16, T)).astype(BF16), upper)[0:1]
        rank = jnp.where(hit > 0.5, rank, -1.0)
        return jnp.where(slot_i == rank, 1.0, 0.0).astype(BF16)

    def put(n, value):
        cols[:, n:n + 1] = value

    for n, base in enumerate((0, 2)):
        hits = jnp.where(lane_f == route_cols[base], 1.0, 0.0) + jnp.where(lane_f == route_cols[base + 1], 1.0, 0.0)
        ranks = dot(lower, hits.astype(BF16))
        for c in range(2):
            route = route_cols[base + c]
            put(16 + 2 * n + c, jnp.sum(jnp.where(lane_f == route, ranks, 0.0), axis=1, keepdims=True))
            put(20 + 2 * n + c, route)

    pl.semaphore_wait(barrier, len(partners))

    order = list(range(E - 1, 0, -1))
    inner = flip(lax.rem(me, 2), lax.rem(lax.div(me, 2), 2), 2)
    arrivals = [1, 3, 2] if E == 4 else order
    early_sends = []

    def by_class(build):
        if E != 4:
            build(0)
            return
        for kind in range(2):
            pl.when(inner == kind)(functools.partial(build, kind))

    def first_wave(tau):
        for k in arrivals:
            if tau != COT or k not in early_sends:
                dispatch_copy(tau, k).start()

    def region(tau, expert, feature):
        return rows.at[tau, pl.ds(pl.multiple_of(expert * cap, 16), cap), pl.ds(pl.multiple_of(feature * F, LANES), F)]

    def forward_copy(tau, piece, bit, k):
        part = region(tau, exp_peer[k], hid_peer[piece])
        return remote(part, part, g_send.at[tau, piece + bit, k], g_recv.at[tau, piece + bit, k], h=hid_peer[bit])

    def forwards(tau, piece, k):
        return [
            functools.partial(forward_copy, tau, piece, bit, k)
            for bit in reversed(bits_of(H)) if piece == 0 or bit < low_bit(piece)
        ]

    def forward(tau, k):
        for build in forwards(tau, 0, k):
            build().start()

    def got_piece(tau, piece, k):
        part = region(tau, exp_peer[k], hid_peer[piece])
        remote(part, part, g_send.at[tau, piece, k], g_recv.at[tau, piece, k], h=hid_peer[low_bit(piece)]).wait_recv()

    def dispatch_copy(tau, k):
        return remote(
            slots.at[tau, k - 1], region(tau, me, hi), z_send.at[tau, k], z_recv.at[tau, k], e=exp_peer[k])

    def dispatch(tau, base, tokens):
        for k in order + [0]:
            picked = dot(chosen(base, exp_peer[k]), tokens).astype(BF16)
            if k == 0:
                rows[tau, pl.ds(pl.multiple_of(me * cap, 16), cap), pl.ds(pl.multiple_of(hi * F, LANES), F)] = picked
            else:
                slots[tau, k - 1] = picked

    def z_event(tau, n):
        k = arrivals[n]
        part = region(tau, exp_peer[k], hi)
        remote(part, part, z_send.at[tau, k], z_recv.at[tau, k], e=exp_peer[k]).wait_recv()
        forward(tau, k)
        if tau == NXT and n == E - 2:
            first_wave(SAV)
        if tau == SAV and n >= E - 3:
            by_class(lambda kind: first_wave(COT) if kind == E - 2 - n or E != 4 and n == E - 2 else None)
        if tau + 1 == SAV and n == 0:
            forward(SAV, 0)

    relays = [p for top in reversed(bits_of(H)) if top > 1 for p in range(top, H, 2 * top)]

    def relay(tau, k):
        for piece in relays:
            got_piece(tau, piece, k)
            for build in forwards(tau, piece, k):
                build().start()

    def x_event(tau, n):
        relay(tau, arrivals[n - 1] if n else 0)

    def gather_events(tau):
        events = [functools.partial(x_event, tau, 0)]
        for n in range(E - 1):
            events.insert(-1, functools.partial(z_event, tau, n))
            events.append(functools.partial(x_event, tau, n + 1))
        return events

    def complete(tau):
        for piece in range(1, H, 2):
            for k in range(E):
                got_piece(tau, piece, k)

    stats = jnp.zeros((T, LANES), F32)
    for offset, ref in ((0, saved_ref), (16, next_ref)):
        values = ref[...].astype(F32)
        stats = stats + jnp.where(lane == offset, jnp.sum(values * values, axis=1, keepdims=True), 0.0)
        for e in range(E):
            weights = table_ref[e:e + 1, :] * gain
            stats = stats + jnp.where(lane == offset + 1 + e, jnp.sum(values * weights, axis=1, keepdims=True), 0.0)
    stat_send[...] = stats.T[0:32]

    def all_to_hid(src, dst, sent, recv):
        copies = [remote(src, dst.at[m - 1], sent.at[m], recv.at[m], h=hid_peer[m]) for m in range(1, H)]
        for copy in copies:
            send(lambda copy=copy: copy)
        return copies

    stat_copies = all_to_hid(stat_send, stat_recv, s_send, s_recv)

    dispatch(COT, 0, cot_ref[...])
    forward(COT, 0)
    for k in early_sends:
        dispatch_copy(COT, k).start()

    total = stats.T[0:32]
    for m, copy in enumerate(stat_copies):
        copy.wait_recv()
        total = total + stat_recv[m]
    stats = jnp.concatenate([total, jnp.zeros((LANES - 32, T), F32)], axis=0).T

    def finish_norm(offset, base, ref, keep):
        scale = lax.rsqrt(stats[:, offset:offset + 1] / D + EPSILON)
        first_score = jnp.zeros((T, 1), F32)
        second_score = jnp.zeros((T, 1), F32)
        for e in range(E):
            score = stats[:, offset + 1 + e:offset + 2 + e]
            first_score = first_score + jnp.where(route_cols[base] == e, score, 0.0)
            second_score = second_score + jnp.where(route_cols[base + 1] == e, score, 0.0)
        first, second = first_score * scale, second_score * scale
        put(keep, jax.nn.sigmoid(first - second))
        put(keep + 1, jax.nn.sigmoid(second - first))
        put(keep + 2, scale)
        put(keep + 3, first_score - second_score)
        return (ref[...].astype(F32) * scale * gain).astype(BF16)

    dispatch(NXT, 2, finish_norm(16, 2, next_ref, 4))
    first_wave(NXT)
    forward(NXT, 0)
    dispatch(SAV, 0, finish_norm(0, 0, saved_ref, 0))

    far = [(cot_ref, far_cot), (saved_ref, far_saved), (gain_ref, far_gain), (table_ref, far_table), (cols, far_cols)]

    def far_copy(n):
        return remote(far[n][0], far[n][1], e_send.at[n], e_recv.at[n], s=1 - sec)

    def far_value_copy(c):
        part = pl.ds(c * tw, tw)
        n = len(far) + c
        return remote(there_send.at[:, part], far_value.at[:, part], e_send.at[n], e_recv.at[n], s=1 - sec)

    @pl.when(sec == 1)
    def _():
        for n in range(len(far)):
            far_copy(n).start()

    def reduce_step(which, acc, m_now, c):

        @pl.when(m_now == 0)
        def _():
            own_part[which, c] = acc

        for m in range(1, H):
            @pl.when(m_now == m)
            def _():
                value = acc
                for bit in bits_of(low_bit(m) * 2)[:-1]:
                    received(which, m + bit, c)
                    value = value + rs_recv[which, m + bit - 1, c].astype(F32)
                rs_send[which, m - 1, c] = value.astype(BF16)
                if which == 1 or m == 1 or m != low_bit(m):
                    reduce_copy(which, m, c).start()

    def reduce_copy(which, m, c):
        return remote(
            rs_send.at[which, m - 1, c], rs_recv.at[which, m - 1, c],
            r_send.at[which, m, c], r_recv.at[which, m, c], h=hid_peer[low_bit(m)])

    def received(which, m, c):
        reduce_copy(which, m, c).wait_recv()

    def home_region(which, expert, c):
        return home.at[which, pl.ds(pl.multiple_of(expert * cap, 16), cap), pl.ds(c * tw, tw)]

    def home_copy(which, k, c):
        return remote(
            home_send.at[which, c, pl.ds(pl.multiple_of(exp_peer[k] * cap, 16), cap)], home_region(which, me, c),
            b_send.at[which, k, c], b_recv.at[which, k, c], e=exp_peer[k])

    def home_event(which, c):
        value = own_part[which, c]
        for bit in bits_of(H):
            received(which, bit, c)
            value = value + rs_recv[which, bit - 1, c].astype(F32)
        home_send[which, c] = value.astype(BF16)
        for k in order:
            send(functools.partial(home_copy, which, k, c))
        mine = pl.ds(pl.multiple_of(me * cap, 16), cap)
        home[which, mine, c * tw:(c + 1) * tw] = home_send[which, c, mine, :]

    def home_wait(which, c):
        for k in order:
            part = home_region(which, exp_peer[k], c)
            remote(part, part, b_send.at[which, k, c], b_recv.at[which, k, c], e=exp_peer[k]).wait_recv()

    wide_i = lax.broadcasted_iota(I32, (T, all_rows), 1).astype(F32)

    def selectors(n):
        picks = []
        for c in range(2):
            rank, route = cols[:, 16 + 2 * n + c:17 + 2 * n + c], cols[:, 20 + 2 * n + c:21 + 2 * n + c]
            picks.append(jnp.where(wide_i == route * cap + rank, 1.0, 0.0).astype(BF16))
        return picks

    def blended(which, n, keep, c, picks):
        part = home[which, :, c * tw:(c + 1) * tw]
        return cols[:, keep:keep + 1] * dot(picks[0], part) + cols[:, keep + 1:keep + 2] * dot(picks[1], part)

    def there_copy(n, height):
        part = pl.ds(n * height, height)
        return remote(there_send.at[part], there_recv.at[part], y_send.at[n], y_recv.at[n], s=1 - sec)

    halves = 2
    half_rows = T // halves

    def forward_out():
        picks = selectors(1)
        for c in range(n_cols):
            home_wait(0, c)
            part = slice(c * tw, (c + 1) * tw)
            value = (next_ref[:, part].astype(F32) + blended(0, 1, 4, c, picks)).astype(BF16)

            @pl.when(sec == 0)
            def _():
                there_send[:, part] = value

            @pl.when(sec == 1)
            def _():
                out_ref[0, :, part] = value

        @pl.when(sec == 0)
        def _():
            for n in range(halves):
                there_copy(n, half_rows).start()

    def run(events, index):
        for at, event in events:
            pl.when(index == at)(event)

    next_events, cot_events = gather_events(NXT), gather_events(COT)
    for event in next_events[:-2]:
        event()
    if early_sends:
        cot_events[0]()
    for event in next_events[-2:]:
        event()
    complete(NXT)

    def at(events, spots):
        return list(zip(spots, events))

    def split(event, late, soon):
        return [(late + (soon - late) * (1 - inner), event)]

    wide_sends = [(m, c) for m in reversed(bits_of(H)) if m > 1 for c in range(n_cols)]

    def wave(start, stop):
        return [functools.partial(lambda m, c: reduce_copy(0, m, c).start(), m, c) for m, c in wide_sends[start:stop]]

    downs = [functools.partial(home_event, 0, c) for c in range(n_cols)]
    tuned = E == 4 and H == 4 and n_cols == 4 and n_tiles == 7
    saved_events = gather_events(SAV)
    if tuned:
        up_events = at(saved_events[:6], [0, 1, 3, 3, 5, 6])
        out_events = at(saved_events[6:], [2]) + at(cot_events[:1], [3]) + at(wave(0, 1), [4])
        gate_events = at(cot_events[2:3], [0]) + at(cot_events[4:5], [3]) + at(wave(1, 4), [3, 3, 3])
        gate_events += at(cot_events[3:4], [3]) + at(downs[:1], [4]) + at(cot_events[5:], [5, 6])
        gh_events = at(downs[1:2], [4])
        back_events = at(downs[2:], [1, 4])
    else:
        up_events = at(saved_events, [n_tiles * n // len(saved_events) for n in range(len(saved_events))])
        out_events = []
        late_events = cot_events[:1] + cot_events[2:]
        gate_events = at(late_events, [n_tiles * n // len(late_events) for n in range(len(late_events))])
        waves = wave(0, len(wide_sends))
        gate_events += at(waves, [n_tiles - 1] * len(waves))
        gh_events = []
        back_events = at(downs, [2 + c for c in range(n_cols)])
    cot_events[1]()

    @pl.loop(0, n_tiles)
    def _(j):
        start_a(j + A_SLOTS - 1)
        run(up_events, j)
        slot = lax.rem(j, A_SLOTS)
        for copy in a_copies("pair", j, slot):
            copy.wait()
        both = dot(rows[NXT], wa[slot, :, 0:2 * tn])
        gate, up = both[:, 0:tn], both[:, tn:2 * tn]
        hid_n[:, pl.ds(pl.multiple_of(j * tn, tn), tn)] = (gate * jax.nn.sigmoid(gate) * up).astype(BF16)

    @pl.loop(0, out_items)
    def _(i):
        g = n_tiles + i
        start_a(g + A_SLOTS - 1)
        run(out_events, i)
        slot = lax.rem(g, A_SLOTS)
        out_copy(i, slot).wait()
        acc = dot(hid_n[...], wa[slot, 0:ffd, 0:2 * tw])
        m, c = place_of(i, "out")
        for half in range(2):
            reduce_step(0, acc[:, half * tw:(half + 1) * tw], m, 2 * c + half)

    complete(SAV)

    dots_acc[...] = jnp.zeros_like(dots_acc)
    @pl.loop(0, n_tiles)
    def _(j):
        g = n_tiles + out_items + j
        start_a(g + A_SLOTS - 1)
        run(gate_events, j)
        slot = lax.rem(g, A_SLOTS)
        for copy in a_copies("pair", j, slot):
            copy.wait()
        part = pl.ds(pl.multiple_of(j * tn, tn), tn)
        both = dot(rows[SAV], wa[slot, :, 0:2 * tn])
        pair[0, :, part] = both[:, 0:tn]
        pair[1, :, part] = both[:, tn:2 * tn]

    complete(COT)

    @pl.loop(0, n_tiles)
    def _(j):
        start_r(j + R_SLOTS - 1)
        run(gh_events, j)
        gh_copy(j).wait()
        slot = lax.rem(j, R_SLOTS)
        grad = dot(rows[COT], wr[slot, 0:tn, 0:D], NT)
        part = pl.ds(pl.multiple_of(j * tn, tn), tn)
        gate, up = pair[0, :, part], pair[1, :, part]
        sig = jax.nn.sigmoid(gate)
        silu = gate * sig
        hidden = (silu * up).astype(BF16).astype(F32)
        grads[0, :, part] = (grad * up * (sig * (1.0 + gate * (1.0 - sig)))).astype(BF16)
        grads[1, :, part] = (grad * silu).astype(BF16)
        product = grad * hidden
        partial = product[:, 0:LANES]
        for n in range(1, tn // LANES):
            partial = partial + product[:, n * LANES:(n + 1) * LANES]
        dots_acc[...] += partial

    def dots_copy(k):
        return remote(dots_send, dots_recv.at[k - 1], d_send.at[k], d_recv.at[k], e=exp_peer[k])

    dots_send[...] = jnp.broadcast_to(jnp.sum(dots_acc[...].T, axis=0, keepdims=True), (8, all_rows))
    for k in order:
        send(functools.partial(dots_copy, k))

    def dots_event():
        for k in order:
            dots_copy(k).wait_recv()
        gap = jnp.zeros((T, 1), F32)
        for k in range(E):
            row = dots_send[0:1] if k == 0 else dots_recv[k - 1, 0:1]
            expert = exp_peer[k].astype(F32)
            for c, sign in ((0, 1.0), (1, -1.0)):
                rank, route = cols[:, 16 + c:17 + c], cols[:, 20 + c:21 + c]
                spot = jnp.where(route == expert, me.astype(F32) * cap + rank, -1.0)
                gap = gap + sign * jnp.sum(jnp.where(wide_i == spot, row, 0.0), axis=1, keepdims=True)
        dots_acc[0:T, 0:1] = gap

    soon = [c for c in range(n_cols) if H * (c + 2) + 1 < steps]
    back_events += [(H * (c + 2) + 1, functools.partial(home_event, 1, c)) for c in soon]

    @pl.loop(0, steps)
    def _(i):
        start_r(n_tiles + i + R_SLOTS - 1)
        run(back_events, i)
        for copy in back_copies(i):
            copy.wait()
        slot = lax.rem(n_tiles + i, R_SLOTS)
        acc = dot(grads[0], wr[slot, 0:tw, 0:ffd], NT) + dot(grads[1], wr[slot, 0:tw, ffd:2 * ffd], NT)
        reduce_step(1, acc, *place_of(i, "back"))

    later = [c for c in range(n_cols) if c not in soon]
    for c in later[:-1]:
        home_event(1, c)
    forward_out()
    dots_event()
    home_event(1, later[-1])
    picks = selectors(0)
    inner = jnp.zeros((T, 1), F32)
    for c in range(n_cols):
        home_wait(1, c)
        part = slice(c * tw, (c + 1) * tw)
        value = blended(1, 0, 0, c, picks) * gain_ref[:, part]
        mixed[:, part] = value

        @pl.when(sec == 1)
        def _():
            there_send[:, part] = value.astype(BF16)
            far_value_copy(c).start()

        inner = inner + jnp.sum(value * saved_ref[:, part].astype(F32), axis=1, keepdims=True)
    message = jnp.where(lane == 0, inner, 0.0) + jnp.where(lane == 1, dots_acc[0:T, 0:1], 0.0)
    message = message.T[0:8]
    tail_send[...] = message

    def tail_copy(m):
        return remote(tail_send, tail_recv.at[m - 1], t_send.at[m], t_recv.at[m], h=hid_peer[m])

    def far_tail_copy(m):
        return remote(tail_send, far_tail.at[m], f_send.at[m], f_recv.at[m], h=hid_peer[m], s=1 - sec)

    def input_gradient(message, cot, saved, value_of, gains, table, kept, place_in):
        message = jnp.concatenate([message, jnp.zeros((LANES - 8, T), F32)], axis=0).T
        scale = kept[:, 2:3]
        slope = message[:, 1:2] * kept[:, 0:1] * kept[:, 1:2]
        inner = message[:, 0:1] + slope * kept[:, 3:4]
        pull = scale * scale * scale * (inner / D)
        for n in range(halves):
            part = slice(n * half_rows, (n + 1) * half_rows)
            lean = jnp.zeros((half_rows, F), F32)
            for e in range(E):
                sign = jnp.where(kept[part, 20:21] == e, 1.0, 0.0) - jnp.where(kept[part, 21:22] == e, 1.0, 0.0)
                lean = lean + sign * table[e:e + 1, :]
            grad = value_of[part, :].astype(F32) + slope[part] * lean * gains[...]
            out_ref[place_in, part, :] = (
                cot[part, :].astype(F32) + scale[part] * grad - saved[part, :].astype(F32) * pull[part]
            ).astype(BF16)

    @pl.when(sec == 1)
    def _():
        for m in range(H):
            far_tail_copy(m).start()
        for n in range(halves):
            there_copy(n, half_rows).wait_recv()
        out_ref[1] = there_recv[...]
        for n in range(len(far)):
            far_copy(n).wait_send()
        for c in range(n_cols):
            far_value_copy(c).wait_send()
        for m in range(H):
            far_tail_copy(m).wait_send()

    @pl.when(sec == 0)
    def _():
        for m in range(1, H):
            tail_copy(m).start()
        total = message
        for m in range(1, H):
            tail_copy(m).wait_recv()
            total = total + tail_recv[m - 1]
        input_gradient(total, cot_ref, saved_ref, mixed, gain_ref, table_ref, cols, 0)
        for n in range(len(far)):
            far_copy(n).wait_recv()
        for c in range(n_cols):
            far_value_copy(c).wait_recv()
        total = jnp.zeros((8, T), F32)
        for m in range(H):
            far_tail_copy(m).wait_recv()
            total = total + far_tail[m]
        input_gradient(total, far_cot, far_saved, far_value, far_gain, far_table, far_cols, 1)
        for m in range(1, H):
            tail_copy(m).wait_send()
        for n in range(halves):
            there_copy(n, half_rows).wait_send()

    for build in to_send:
        build().wait_send()
    for tau in range(3):
        for k in range(E):
            if k:
                dispatch_copy(tau, k).wait_send()
            for piece in [0] + relays:
                for build in forwards(tau, piece, k):
                    build().wait_send()
    for which in range(2):
        for m in range(1, H):
            for c in range(n_cols):
                reduce_copy(which, m, c).wait_send()


def per_device(
    saved_input,
    cotangent,
    next_input,
    routes_saved,
    routes_next,
    norm_gain,
    router,
    expert_gate,
    expert_up,
    expert_down,
):
    E, H = lax.axis_size("expert"), lax.axis_size("hid")
    T, F = saved_input.shape[1:]
    D, ffd = expert_gate.shape[2:]
    cap = 3 * T // router.shape[2]
    tn = 2 * LANES if ffd % (2 * LANES) == 0 else LANES
    tw = 2 * LANES if F % (2 * LANES) == 0 else LANES
    n_cols, all_rows = F // tw, E * cap
    deep, wide = max(tn, tw), max(D, 2 * ffd)
    vmem = pl.BlockSpec(memory_space=pltpu.VMEM)
    hbm = pl.BlockSpec(memory_space=pl.ANY)
    dma = pltpu.SemaphoreType.DMA
    scratch = [
        pltpu.VMEM((3, all_rows, D), BF16),
        pltpu.VMEM((3, E - 1, cap, F), BF16),
        pltpu.VMEM((A_SLOTS, D, 2 * deep), BF16),
        pltpu.VMEM((R_SLOTS, deep, wide), BF16),
        pltpu.VMEM((2, all_rows, ffd), F32),
        pltpu.VMEM((all_rows, ffd), BF16),
        pltpu.VMEM((2, all_rows, ffd), BF16),
        pltpu.VMEM((2, H - 1, n_cols, all_rows, tw), BF16),
        pltpu.VMEM((2, H - 1, n_cols, all_rows, tw), BF16),
        pltpu.VMEM((2, n_cols, all_rows, tw), F32),
        pltpu.VMEM((2, n_cols, all_rows, tw), BF16),
        pltpu.VMEM((2, all_rows, F), BF16),
        pltpu.VMEM((32, T), F32),
        pltpu.VMEM((H - 1, 32, T), F32),
        pltpu.VMEM((all_rows, LANES), F32),
        pltpu.VMEM((8, all_rows), F32),
        pltpu.VMEM((E - 1, 8, all_rows), F32),
        pltpu.VMEM((8, T), F32),
        pltpu.VMEM((H - 1, 8, T), F32),
        pltpu.VMEM((T, LANES), F32),
        pltpu.VMEM((T, F), F32),
        pltpu.VMEM((T, F), BF16),
        pltpu.VMEM((T, F), BF16),
        pltpu.VMEM((T, F), BF16),
        pltpu.VMEM((T, F), BF16),
        pltpu.VMEM((T, F), BF16),
        pltpu.VMEM((1, F), F32),
        pltpu.VMEM((E, F), F32),
        pltpu.VMEM((T, LANES), F32),
        pltpu.VMEM((H, 8, T), F32),
        dma((A_SLOTS, 2)),
        dma((R_SLOTS, 2)),
        dma((3, E)),
        dma((3, E)),
        dma((3, H, E)),
        dma((3, H, E)),
        dma((H,)),
        dma((H,)),
        dma((2, H, n_cols)),
        dma((2, H, n_cols)),
        dma((2, E, n_cols)),
        dma((2, E, n_cols)),
        dma((E,)),
        dma((E,)),
        dma((H,)),
        dma((H,)),
        dma((2,)),
        dma((2,)),
        dma((5 + n_cols,)),
        dma((5 + n_cols,)),
        dma((H,)),
        dma((H,)),
    ]
    result = pl.pallas_call(
        functools.partial(kernel, (E, H, T, F, D, ffd, cap, tn, tw)),
        out_shape=jax.ShapeDtypeStruct((2, T, F), BF16),
        in_specs=[vmem] * 7 + [hbm] * 3,
        out_specs=vmem,
        scratch_shapes=scratch,
        compiler_params=pltpu.CompilerParams(
            collective_id=0, has_side_effects=True, vmem_limit_bytes=67043328
        ),
        name="relay",
    )(
        saved_input[0], cotangent[0], next_input[0], routes_saved[0].T, routes_next[0].T, norm_gain, router[0].T,
        expert_gate[0, 0], expert_up[0, 0], expert_down[0, 0],
    )
    return (result[0:1], result[1:2])


def solution(mesh):
    placed = (
        P("section", "expert", "hid"),
        P("section", "expert", "hid"),
        P("section", "expert", "hid"),
        P("section", "expert", None),
        P("section", "expert", None),
        P("section", "hid"),
        P("section", "hid", None),
        P("section", "expert", None, "hid"),
        P("section", "expert", None, "hid"),
        P("section", "expert", "hid", None),
    )
    return jax.shard_map(
        per_device,
        mesh=mesh,
        in_specs=placed,
        out_specs=(P("section", "expert", "hid"), P("section", "expert", "hid")),
        check_vma=False,
    )
```

```python
import functools

import jax
import jax.numpy as jnp
from jax import lax
from jax.experimental import pallas as pl
from jax.experimental.pallas import tpu as pltpu
from jax.sharding import PartitionSpec as P

EPSILON = 1e-05
F32 = jnp.float32
BF16 = jnp.bfloat16
I32 = jnp.int32
NN = (((1,), (0,)), ((), ()))
NT = (((1,), (1,)), ((), ()))
LANES = 128
A_SLOTS = 3
R_SLOTS = 4
NXT, SAV, COT = 0, 1, 2


def bits_of(count):
    return [1 << bit for bit in range(count.bit_length() - 1)]


def low_bit(number):
    return number & -number


def flip(value, mask, count):
    total = 0
    for bit in bits_of(count):
        own = lax.rem(lax.div(value, bit), 2)
        if isinstance(mask, int):
            got = 1 - own if mask & bit else own
        else:
            other = lax.rem(lax.div(mask, bit), 2)
            got = own + other - 2 * own * other
        total = total + bit * got
    return total


def dot(a, b, dims=NN):
    return lax.dot_general(a, b, dims, preferred_element_type=F32)


def kernel(
    sizes,
    saved_ref, cot_ref, next_ref, pair_saved_ref, pair_next_ref, gain_ref, table_ref, wg_ref, wu_ref, wd_ref,
    out_ref,
    rows, slots, wa, wr, pair, hid_n, grads, rs_send, rs_recv, own_part, home_send, home,
    stat_send, stat_recv, dots_acc, dots_send, dots_recv, tail_send, tail_recv,
    cols, mixed, there_send, there_recv, far_cot, far_saved, far_value, far_gain, far_table, far_cols, far_tail, scale_send, scale_recv, scales,
    wa_sem, wr_sem,
    z_send, z_recv, g_send, g_recv, s_send, s_recv, r_send, r_recv,
    b_send, b_recv, d_send, d_recv, t_send, t_recv, y_send, y_recv, e_send, e_recv, f_send, f_recv, c_send, c_recv,
):
    E, H, T, F, D, ffd, cap, tn, tw = sizes
    n_tiles, n_cols = ffd // tn, F // tw
    steps = H * n_cols
    all_rows = E * cap
    sec, me, hi = lax.axis_index("section"), lax.axis_index("expert"), lax.axis_index("hid")
    hid_peer = [flip(hi, m, H) for m in range(H)]
    exp_peer = [flip(me, k, E) for k in range(E)]
    to_send = []
    none = me * 0

    def remote(src, dst, send, recv, e=None, h=None, s=None):
        where = (sec if s is None else s, me if e is None else e, hi if h is None else h)
        return pltpu.make_async_remote_copy(
            src_ref=src, dst_ref=dst, send_sem=send, recv_sem=recv,
            device_id=where, device_id_type=pl.DeviceIdType.MESH,
        )

    def send(build):
        build().start()
        to_send.append(build)

    def place_of(i, kind):
        if kind == "out":
            return H - 1 - lax.div(i, n_cols // 2), lax.rem(i, n_cols // 2)
        at = lax.rem(i, H)
        return H - 1 - 2 * at + lax.div(at, H // 2) * (H - 1), lax.div(i, H)

    def out_copy(i, slot):
        m, c = place_of(i, "out")
        col = pl.multiple_of(flip(hi, m, H) * F + c * 2 * tw, 2 * tw)
        return pltpu.make_async_copy(
            wd_ref.at[:, pl.ds(col, 2 * tw)], wa.at[slot, pl.ds(0, ffd), pl.ds(0, 2 * tw)], wa_sem.at[slot, 0])

    def a_copies(kind, j, slot):
        if kind == "out":
            return [out_copy(j, slot)]
        col = pl.multiple_of(j * tn, tn)
        return [
            pltpu.make_async_copy(w.at[:, pl.ds(col, tn)], wa.at[slot, :, pl.ds(half * tn, tn)], wa_sem.at[slot, half])
            for half, w in enumerate((wg_ref, wu_ref))
        ]

    out_items = steps // 2

    def start_a(g):
        slot = lax.rem(g, A_SLOTS)

        @pl.when((g < n_tiles) | (g >= n_tiles + out_items) & (g < 2 * n_tiles + out_items))
        def _():
            for copy in a_copies("pair", lax.rem(jnp.where(g < n_tiles, g, g - out_items - n_tiles), n_tiles), slot):
                copy.start()

        @pl.when((g >= n_tiles) & (g < n_tiles + out_items))
        def _():
            for copy in a_copies("out", g - n_tiles, slot):
                copy.start()

    def gh_copy(j):
        slot = lax.rem(j, R_SLOTS)
        return pltpu.make_async_copy(
            wd_ref.at[pl.ds(pl.multiple_of(j * tn, tn), tn), :], wr.at[slot, pl.ds(0, tn), pl.ds(0, D)],
            wr_sem.at[slot, 0])

    def back_copies(i):
        slot = lax.rem(n_tiles + i, R_SLOTS)
        m, c = place_of(i, "back")
        row = pl.multiple_of(flip(hi, m, H) * F + c * tw, tw)
        return [
            pltpu.make_async_copy(
                w.at[pl.ds(row, tw), :], wr.at[slot, pl.ds(0, tw), pl.ds(half * ffd, ffd)], wr_sem.at[slot, half])
            for half, w in enumerate((wg_ref, wu_ref))
        ]

    def start_r(g):
        @pl.when(g < n_tiles)
        def _():
            gh_copy(g).start()

        @pl.when((g >= n_tiles) & (g < n_tiles + steps))
        def _():
            for copy in back_copies(g - n_tiles):
                copy.start()

    for j in range(min(R_SLOTS - 1, n_tiles)):
        gh_copy(none + j).start()
    for g in range(A_SLOTS - 1):
        for copy in a_copies("pair", none + g, none + g):
            copy.start()

    barrier = pltpu.get_barrier_semaphore()
    partners = [(sec, me, hid_peer[m]) for m in range(1, H)]
    partners += [(sec, exp_peer[k], hi) for k in range(1, E)]
    partners += [(1 - sec, me, hid_peer[m]) for m in range(H)]
    for where in partners:
        pl.semaphore_signal(barrier, inc=1, device_id=where, device_id_type=pl.DeviceIdType.MESH)
    lane = lax.broadcasted_iota(I32, (T, LANES), 1)
    gain = gain_ref[...]
    route_rows = jnp.concatenate(
        [pair_saved_ref[...].astype(F32), pair_next_ref[...].astype(F32), jnp.zeros((LANES - 4, T), F32)], axis=0)
    spread = route_rows.T
    route_cols = [spread[:, n:n + 1] for n in range(4)]
    first_i = lax.broadcasted_iota(I32, (T, T), 0)
    second_i = lax.broadcasted_iota(I32, (T, T), 1)
    upper = jnp.where(first_i < second_i, 1.0, 0.0).astype(BF16)
    lower = jnp.where(first_i > second_i, 1.0, 0.0).astype(BF16)
    slot_i = lax.broadcasted_iota(I32, (cap, T), 0).astype(F32)
    lane_f = lane.astype(F32)

    def chosen(base, expert):
        first, second = route_rows[base:base + 1], route_rows[base + 1:base + 2]
        wanted = expert.astype(F32)
        hit = jnp.where(first == wanted, 1.0, 0.0) + jnp.where(second == wanted, 1.0, 0.0)
        rank = dot(jnp.broadcast_to(hit, (16, T)).astype(BF16), upper)[0:1]
        rank = jnp.where(hit > 0.5, rank, -1.0)
        return jnp.where(slot_i == rank, 1.0, 0.0).astype(BF16)

    def put(n, value):
        cols[:, n:n + 1] = value

    kept_ranks = []
    for n, base in enumerate((0, 2)):
        hits = jnp.where(lane_f == route_cols[base], 1.0, 0.0) + jnp.where(lane_f == route_cols[base + 1], 1.0, 0.0)
        ranks = dot(lower, hits.astype(BF16))
        kept_ranks.append((hits, ranks))
        for c in range(2):
            route = route_cols[base + c]
            put(16 + 2 * n + c, jnp.sum(jnp.where(lane_f == route, ranks, 0.0), axis=1, keepdims=True))
            put(20 + 2 * n + c, route)

    order = list(range(E - 1, 0, -1))
    inner = flip(lax.rem(me, 2), lax.rem(lax.div(me, 2), 2), 2)
    arrivals = [1, 3, 2] if E == 4 else order
    early_sends = []

    def by_class(build):
        if E != 4:
            build(0)
            return
        for kind in range(2):
            pl.when(inner == kind)(functools.partial(build, kind))

    def first_wave(tau):
        for k in arrivals:
            if tau != COT or k not in early_sends:
                dispatch_copy(tau, k).start()

    def region(tau, expert, feature):
        return rows.at[tau, pl.ds(pl.multiple_of(expert * cap, 16), cap), pl.ds(pl.multiple_of(feature * F, LANES), F)]

    def forward_copy(tau, piece, bit, k):
        part = region(tau, exp_peer[k], hid_peer[piece])
        return remote(part, part, g_send.at[tau, piece + bit, k], g_recv.at[tau, piece + bit, k], h=hid_peer[bit])

    def forwards(tau, piece, k):
        return [
            functools.partial(forward_copy, tau, piece, bit, k)
            for bit in reversed(bits_of(H)) if piece == 0 or bit < low_bit(piece)
        ]

    def forward(tau, k):
        for build in forwards(tau, 0, k):
            build().start()

    def got_piece(tau, piece, k):
        part = region(tau, exp_peer[k], hid_peer[piece])
        remote(part, part, g_send.at[tau, piece, k], g_recv.at[tau, piece, k], h=hid_peer[low_bit(piece)]).wait_recv()

    def dispatch_copy(tau, k):
        return remote(
            slots.at[tau, k - 1], region(tau, me, hi), z_send.at[tau, k], z_recv.at[tau, k], e=exp_peer[k])

    def dispatch(tau, base, tokens):
        for k in order + [0]:
            picked = dot(chosen(base, exp_peer[k]), tokens).astype(BF16)
            if k == 0:
                rows[tau, pl.ds(pl.multiple_of(me * cap, 16), cap), pl.ds(pl.multiple_of(hi * F, LANES), F)] = picked
            else:
                slots[tau, k - 1] = picked

    def z_event(tau, n):
        k = arrivals[n]
        part = region(tau, exp_peer[k], hi)
        remote(part, part, z_send.at[tau, k], z_recv.at[tau, k], e=exp_peer[k]).wait_recv()
        forward(tau, k)
        if tau == NXT and n == E - 2:
            first_wave(SAV)
        if tau == SAV and n >= E - 3:
            by_class(lambda kind: first_wave(COT) if kind == E - 2 - n or E != 4 and n == E - 2 else None)
        if tau + 1 == SAV and n == E - 2:
            forward(SAV, 0)

    relays = [p for top in reversed(bits_of(H)) if top > 1 for p in range(top, H, 2 * top)]

    def relay(tau, k):
        for piece in relays:
            got_piece(tau, piece, k)
            for build in forwards(tau, piece, k):
                build().start()

    def x_event(tau, n):
        relay(tau, arrivals[n - 1] if n else 0)

    def gather_events(tau):
        events = [functools.partial(x_event, tau, 0)]
        for n in range(E - 1):
            events.insert(-1, functools.partial(z_event, tau, n))
            events.append(functools.partial(x_event, tau, n + 1))
        return events

    def complete(tau):
        for piece in range(1, H, 2):
            for k in range(E):
                got_piece(tau, piece, k)

    stats = jnp.zeros((T, LANES), F32)
    for offset, ref in ((0, saved_ref), (16, next_ref)):
        values = ref[...].astype(F32)
        stats = stats + jnp.where(lane == offset, jnp.sum(values * values, axis=1, keepdims=True), 0.0)
        for e in range(E):
            weights = table_ref[e:e + 1, :] * gain
            stats = stats + jnp.where(lane == offset + 1 + e, jnp.sum(values * weights, axis=1, keepdims=True), 0.0)
    stat_send[...] = stats.T[0:32]

    def all_to_hid(src, dst, sent, recv):
        copies = [remote(src, dst.at[m - 1], sent.at[m], recv.at[m], h=hid_peer[m]) for m in range(1, H)]
        for copy in copies:
            send(lambda copy=copy: copy)
        return copies

    dispatch(NXT, 2, (next_ref[...].astype(F32) * gain).astype(BF16))
    dispatch(COT, 0, cot_ref[...])

    pl.semaphore_wait(barrier, len(partners))
    stat_copies = all_to_hid(stat_send, stat_recv, s_send, s_recv)
    first_wave(NXT)
    forward(NXT, 0)
    forward(COT, 0)
    total = stats.T[0:32]
    for m, copy in enumerate(stat_copies):
        copy.wait_recv()
        total = total + stat_recv[m]
    stats = jnp.concatenate([total, jnp.zeros((LANES - 32, T), F32)], axis=0).T

    def finish_norm(offset, base, keep):
        scale = lax.rsqrt(stats[:, offset:offset + 1] / D + EPSILON)
        first_score = jnp.zeros((T, 1), F32)
        second_score = jnp.zeros((T, 1), F32)
        for e in range(E):
            score = stats[:, offset + 1 + e:offset + 2 + e]
            first_score = first_score + jnp.where(route_cols[base] == e, score, 0.0)
            second_score = second_score + jnp.where(route_cols[base + 1] == e, score, 0.0)
        first, second = first_score * scale, second_score * scale
        put(keep, jax.nn.sigmoid(first - second))
        put(keep + 1, jax.nn.sigmoid(second - first))
        put(keep + 2, scale)
        put(keep + 3, first_score - second_score)
        return scale

    scale = finish_norm(16, 2, 4)
    hits, ranks = kept_ranks[1]
    for k in range(E):
        named = lane == exp_peer[k]
        rank = jnp.sum(jnp.where(named, ranks, 0.0), axis=1, keepdims=True)
        hit = jnp.sum(jnp.where(named, hits, 0.0), axis=1, keepdims=True)
        rank = jnp.where(hit > 0.5, rank, -1.0)
        row = jnp.sum(jnp.where(lane_f == rank, scale, 0.0), axis=0, keepdims=True)
        scale_send[k] = jnp.broadcast_to(row, (8, LANES))

    def scale_copy(k):
        return remote(scale_send.at[k], scale_recv.at[k - 1], c_send.at[k], c_recv.at[k], e=exp_peer[k])

    for k in range(1, E):
        send(functools.partial(scale_copy, k))
    scale = finish_norm(0, 0, 0)
    dispatch(SAV, 0, (saved_ref[...].astype(F32) * scale * gain).astype(BF16))

    far = [(cot_ref, far_cot), (saved_ref, far_saved), (gain_ref, far_gain), (table_ref, far_table), (cols, far_cols)]

    def far_copy(n):
        return remote(far[n][0], far[n][1], e_send.at[n], e_recv.at[n], s=1 - sec)

    def far_value_copy(c):
        part = pl.ds(c * tw, tw)
        n = len(far) + c
        return remote(there_send.at[:, part], far_value.at[:, part], e_send.at[n], e_recv.at[n], s=1 - sec)

    @pl.when(sec == 1)
    def _():
        for n in range(len(far)):
            far_copy(n).start()

    def reduce_step(which, acc, m_now, c):

        @pl.when(m_now == 0)
        def _():
            own_part[which, c] = acc

        for m in range(1, H):
            @pl.when(m_now == m)
            def _():
                value = acc
                for bit in bits_of(low_bit(m) * 2)[:-1]:
                    received(which, m + bit, c)
                    value = value + rs_recv[which, m + bit - 1, c].astype(F32)
                rs_send[which, m - 1, c] = value.astype(BF16)
                if which == 1 or m == 1 or m != low_bit(m):
                    reduce_copy(which, m, c).start()

    def reduce_copy(which, m, c):
        return remote(
            rs_send.at[which, m - 1, c], rs_recv.at[which, m - 1, c],
            r_send.at[which, m, c], r_recv.at[which, m, c], h=hid_peer[low_bit(m)])

    def received(which, m, c):
        reduce_copy(which, m, c).wait_recv()

    def home_region(which, expert, c):
        return home.at[which, pl.ds(pl.multiple_of(expert * cap, 16), cap), pl.ds(c * tw, tw)]

    def home_copy(which, k, c):
        return remote(
            home_send.at[which, c, pl.ds(pl.multiple_of(exp_peer[k] * cap, 16), cap)], home_region(which, me, c),
            b_send.at[which, k, c], b_recv.at[which, k, c], e=exp_peer[k])

    def home_event(which, c):
        value = own_part[which, c]
        for bit in bits_of(H):
            received(which, bit, c)
            value = value + rs_recv[which, bit - 1, c].astype(F32)
        home_send[which, c] = value.astype(BF16)
        for k in arrivals:
            send(functools.partial(home_copy, which, k, c))
        mine = pl.ds(pl.multiple_of(me * cap, 16), cap)
        home[which, mine, c * tw:(c + 1) * tw] = home_send[which, c, mine, :]

    def home_wait(which, c):
        for k in order:
            part = home_region(which, exp_peer[k], c)
            remote(part, part, b_send.at[which, k, c], b_recv.at[which, k, c], e=exp_peer[k]).wait_recv()

    wide_i = lax.broadcasted_iota(I32, (T, all_rows), 1).astype(F32)

    def selectors(n):
        picks = []
        for c in range(2):
            rank, route = cols[:, 16 + 2 * n + c:17 + 2 * n + c], cols[:, 20 + 2 * n + c:21 + 2 * n + c]
            picks.append(jnp.where(wide_i == route * cap + rank, 1.0, 0.0).astype(BF16))
        return picks

    def blended(which, n, keep, c, picks):
        part = home[which, :, c * tw:(c + 1) * tw]
        return cols[:, keep:keep + 1] * dot(picks[0], part) + cols[:, keep + 1:keep + 2] * dot(picks[1], part)

    def there_copy(n, height):
        part = pl.ds(n * height, height)
        return remote(there_send.at[part], there_recv.at[part], y_send.at[n], y_recv.at[n], s=1 - sec)

    halves = 2
    half_rows = T // halves

    def forward_out():
        picks = selectors(1)
        for c in range(n_cols):
            home_wait(0, c)
            part = slice(c * tw, (c + 1) * tw)
            value = (next_ref[:, part].astype(F32) + blended(0, 1, 4, c, picks)).astype(BF16)

            @pl.when(sec == 0)
            def _():
                there_send[:, part] = value

            @pl.when(sec == 1)
            def _():
                out_ref[0, :, part] = value

        @pl.when(sec == 0)
        def _():
            for n in range(halves):
                there_copy(n, half_rows).start()

    def run(events, index):
        for at, event in events:
            pl.when(index == at)(event)

    next_events, cot_events = gather_events(NXT), gather_events(COT)
    for event in next_events[:-2]:
        event()
    if early_sends:
        cot_events[0]()
    for event in next_events[-2:]:
        event()
    complete(NXT)
    for k in range(E):
        if k:
            scale_copy(k).wait_recv()
        row = scale_recv[k - 1, 0:1] if k else scale_send[0, 0:1]
        scales[pl.ds(pl.multiple_of(exp_peer[k] * cap, 16), cap), :] = jnp.broadcast_to(row, (LANES, LANES)).T[0:cap]

    def at(events, spots):
        return list(zip(spots, events))

    def split(event, late, soon):
        return [(late + (soon - late) * (1 - inner), event)]

    wide_sends = [(m, c) for m in reversed(bits_of(H)) if m > 1 for c in range(n_cols)]

    def wave(start, stop):
        return [functools.partial(lambda m, c: reduce_copy(0, m, c).start(), m, c) for m, c in wide_sends[start:stop]]

    downs = [functools.partial(home_event, 0, c) for c in range(n_cols)]
    tuned = E == 4 and H == 4 and n_cols == 4 and n_tiles == 7
    saved_events = gather_events(SAV)
    if tuned:
        up_events = at(saved_events[:6], [0, 1, 2, 3, 4, 5])
        out_events = at(saved_events[6:], [1]) + at(cot_events[:1], [1]) + at(wave(0, 1), [3]) + at(cot_events[2:4], [5, 5])
        gate_events = at(cot_events[4:5], [1]) + at(wave(1, 4), [1, 1, 1]) + at(downs[:1], [2]) + at(cot_events[5:], [3, 5])
        gh_events = at(downs[1:3], [1, 4])
        back_events = at(downs[3:], [1])
    else:
        up_events = at(saved_events, [n_tiles * n // len(saved_events) for n in range(len(saved_events))])
        out_events = []
        late_events = cot_events[:1] + cot_events[2:]
        gate_events = at(late_events, [n_tiles * n // len(late_events) for n in range(len(late_events))])
        waves = wave(0, len(wide_sends))
        gate_events += at(waves, [n_tiles - 1] * len(waves))
        gh_events = []
        back_events = at(downs, [2 + c for c in range(n_cols)])
    cot_events[1]()

    @pl.loop(0, n_tiles)
    def _(j):
        start_a(j + A_SLOTS - 1)
        run(up_events, j)
        slot = lax.rem(j, A_SLOTS)
        for copy in a_copies("pair", j, slot):
            copy.wait()
        both = dot(rows[NXT], wa[slot, :, 0:2 * tn]) * scales[:, 0:1]
        gate, up = both[:, 0:tn], both[:, tn:2 * tn]
        hid_n[:, pl.ds(pl.multiple_of(j * tn, tn), tn)] = (gate * jax.nn.sigmoid(gate) * up).astype(BF16)

    @pl.loop(0, out_items)
    def _(i):
        g = n_tiles + i
        start_a(g + A_SLOTS - 1)
        run(out_events, i)
        slot = lax.rem(g, A_SLOTS)
        out_copy(i, slot).wait()
        acc = dot(hid_n[...], wa[slot, 0:ffd, 0:2 * tw])
        m, c = place_of(i, "out")
        for half in range(2):
            reduce_step(0, acc[:, half * tw:(half + 1) * tw], m, 2 * c + half)

    complete(SAV)

    dots_acc[...] = jnp.zeros_like(dots_acc)
    @pl.loop(0, n_tiles)
    def _(j):
        g = n_tiles + out_items + j
        start_a(g + A_SLOTS - 1)
        run(gate_events, j)
        slot = lax.rem(g, A_SLOTS)
        for copy in a_copies("pair", j, slot):
            copy.wait()
        part = pl.ds(pl.multiple_of(j * tn, tn), tn)
        both = dot(rows[SAV], wa[slot, :, 0:2 * tn])
        pair[0, :, part] = both[:, 0:tn]
        pair[1, :, part] = both[:, tn:2 * tn]

    complete(COT)

    @pl.loop(0, n_tiles)
    def _(j):
        start_r(j + R_SLOTS - 1)
        run(gh_events, j)
        gh_copy(j).wait()
        slot = lax.rem(j, R_SLOTS)
        grad = dot(rows[COT], wr[slot, 0:tn, 0:D], NT)
        part = pl.ds(pl.multiple_of(j * tn, tn), tn)
        gate, up = pair[0, :, part], pair[1, :, part]
        sig = jax.nn.sigmoid(gate)
        silu = gate * sig
        hidden = (silu * up).astype(BF16).astype(F32)
        grads[0, :, part] = (grad * up * (sig * (1.0 + gate * (1.0 - sig)))).astype(BF16)
        grads[1, :, part] = (grad * silu).astype(BF16)
        product = grad * hidden
        partial = product[:, 0:LANES]
        for n in range(1, tn // LANES):
            partial = partial + product[:, n * LANES:(n + 1) * LANES]
        dots_acc[...] += partial

    def dots_copy(k):
        return remote(dots_send, dots_recv.at[k - 1], d_send.at[k], d_recv.at[k], e=exp_peer[k])

    dots_send[...] = jnp.broadcast_to(jnp.sum(dots_acc[...].T, axis=0, keepdims=True), (8, all_rows))
    for k in order:
        send(functools.partial(dots_copy, k))

    def dots_event():
        for k in order:
            dots_copy(k).wait_recv()
        gap = jnp.zeros((T, 1), F32)
        for k in range(E):
            row = dots_send[0:1] if k == 0 else dots_recv[k - 1, 0:1]
            expert = exp_peer[k].astype(F32)
            for c, sign in ((0, 1.0), (1, -1.0)):
                rank, route = cols[:, 16 + c:17 + c], cols[:, 20 + c:21 + c]
                spot = jnp.where(route == expert, me.astype(F32) * cap + rank, -1.0)
                gap = gap + sign * jnp.sum(jnp.where(wide_i == spot, row, 0.0), axis=1, keepdims=True)
        dots_acc[0:T, 0:1] = gap

    soon = [c for c in range(n_cols) if H * (c + 2) + 1 < steps]
    back_events += [(H * (c + 2) + 1, functools.partial(home_event, 1, c)) for c in soon]

    @pl.loop(0, steps)
    def _(i):
        start_r(n_tiles + i + R_SLOTS - 1)
        run(back_events, i)
        for copy in back_copies(i):
            copy.wait()
        slot = lax.rem(n_tiles + i, R_SLOTS)
        acc = dot(grads[0], wr[slot, 0:tw, 0:ffd], NT) + dot(grads[1], wr[slot, 0:tw, ffd:2 * ffd], NT)
        reduce_step(1, acc, *place_of(i, "back"))

    later = [c for c in range(n_cols) if c not in soon]
    for c in later[:-1]:
        home_event(1, c)
    forward_out()
    dots_event()
    home_event(1, later[-1])
    picks = selectors(0)
    inner = jnp.zeros((T, 1), F32)
    for c in range(n_cols):
        home_wait(1, c)
        part = slice(c * tw, (c + 1) * tw)
        value = blended(1, 0, 0, c, picks) * gain_ref[:, part]
        mixed[:, part] = value

        @pl.when(sec == 1)
        def _():
            there_send[:, part] = value.astype(BF16)
            far_value_copy(c).start()

        inner = inner + jnp.sum(value * saved_ref[:, part].astype(F32), axis=1, keepdims=True)
    message = jnp.where(lane == 0, inner, 0.0) + jnp.where(lane == 1, dots_acc[0:T, 0:1], 0.0)
    message = message.T[0:8]
    tail_send[...] = message

    def tail_copy(m):
        return remote(tail_send, tail_recv.at[m - 1], t_send.at[m], t_recv.at[m], h=hid_peer[m])

    def far_tail_copy(m):
        return remote(tail_send, far_tail.at[m], f_send.at[m], f_recv.at[m], h=hid_peer[m], s=1 - sec)

    def input_gradient(message, cot, saved, value_of, gains, table, kept, place_in):
        message = jnp.concatenate([message, jnp.zeros((LANES - 8, T), F32)], axis=0).T
        scale = kept[:, 2:3]
        slope = message[:, 1:2] * kept[:, 0:1] * kept[:, 1:2]
        inner = message[:, 0:1] + slope * kept[:, 3:4]
        pull = scale * scale * scale * (inner / D)
        for n in range(halves):
            part = slice(n * half_rows, (n + 1) * half_rows)
            lean = jnp.zeros((half_rows, F), F32)
            for e in range(E):
                sign = jnp.where(kept[part, 20:21] == e, 1.0, 0.0) - jnp.where(kept[part, 21:22] == e, 1.0, 0.0)
                lean = lean + sign * table[e:e + 1, :]
            grad = value_of[part, :].astype(F32) + slope[part] * lean * gains[...]
            out_ref[place_in, part, :] = (
                cot[part, :].astype(F32) + scale[part] * grad - saved[part, :].astype(F32) * pull[part]
            ).astype(BF16)

    @pl.when(sec == 1)
    def _():
        for m in range(H):
            far_tail_copy(m).start()
        for n in range(halves):
            there_copy(n, half_rows).wait_recv()
        out_ref[1] = there_recv[...]
        for n in range(len(far)):
            far_copy(n).wait_send()
        for c in range(n_cols):
            far_value_copy(c).wait_send()
        for m in range(H):
            far_tail_copy(m).wait_send()

    @pl.when(sec == 0)
    def _():
        for m in range(1, H):
            tail_copy(m).start()
        total = message
        for m in range(1, H):
            tail_copy(m).wait_recv()
            total = total + tail_recv[m - 1]
        input_gradient(total, cot_ref, saved_ref, mixed, gain_ref, table_ref, cols, 0)
        for n in range(len(far)):
            far_copy(n).wait_recv()
        for c in range(n_cols):
            far_value_copy(c).wait_recv()
        total = jnp.zeros((8, T), F32)
        for m in range(H):
            far_tail_copy(m).wait_recv()
            total = total + far_tail[m]
        input_gradient(total, far_cot, far_saved, far_value, far_gain, far_table, far_cols, 1)
        for m in range(1, H):
            tail_copy(m).wait_send()
        for n in range(halves):
            there_copy(n, half_rows).wait_send()

    for build in to_send:
        build().wait_send()
    for tau in range(3):
        for k in range(E):
            if k:
                dispatch_copy(tau, k).wait_send()
            for piece in [0] + relays:
                for build in forwards(tau, piece, k):
                    build().wait_send()
    for which in range(2):
        for m in range(1, H):
            for c in range(n_cols):
                reduce_copy(which, m, c).wait_send()


def per_device(
    saved_input,
    cotangent,
    next_input,
    routes_saved,
    routes_next,
    norm_gain,
    router,
    expert_gate,
    expert_up,
    expert_down,
):
    E, H = lax.axis_size("expert"), lax.axis_size("hid")
    T, F = saved_input.shape[1:]
    D, ffd = expert_gate.shape[2:]
    cap = 3 * T // router.shape[2]
    tn = 2 * LANES if ffd % (2 * LANES) == 0 else LANES
    tw = 2 * LANES if F % (2 * LANES) == 0 else LANES
    n_cols, all_rows = F // tw, E * cap
    deep, wide = max(tn, tw), max(D, 2 * ffd)
    vmem = pl.BlockSpec(memory_space=pltpu.VMEM)
    hbm = pl.BlockSpec(memory_space=pl.ANY)
    dma = pltpu.SemaphoreType.DMA
    scratch = [
        pltpu.VMEM((3, all_rows, D), BF16),
        pltpu.VMEM((3, E - 1, cap, F), BF16),
        pltpu.VMEM((A_SLOTS, D, 2 * deep), BF16),
        pltpu.VMEM((R_SLOTS, deep, wide), BF16),
        pltpu.VMEM((2, all_rows, ffd), F32),
        pltpu.VMEM((all_rows, ffd), BF16),
        pltpu.VMEM((2, all_rows, ffd), BF16),
        pltpu.VMEM((2, H - 1, n_cols, all_rows, tw), BF16),
        pltpu.VMEM((2, H - 1, n_cols, all_rows, tw), BF16),
        pltpu.VMEM((2, n_cols, all_rows, tw), F32),
        pltpu.VMEM((2, n_cols, all_rows, tw), BF16),
        pltpu.VMEM((2, all_rows, F), BF16),
        pltpu.VMEM((32, T), F32),
        pltpu.VMEM((H - 1, 32, T), F32),
        pltpu.VMEM((all_rows, LANES), F32),
        pltpu.VMEM((8, all_rows), F32),
        pltpu.VMEM((E - 1, 8, all_rows), F32),
        pltpu.VMEM((8, T), F32),
        pltpu.VMEM((H - 1, 8, T), F32),
        pltpu.VMEM((T, LANES), F32),
        pltpu.VMEM((T, F), F32),
        pltpu.VMEM((T, F), BF16),
        pltpu.VMEM((T, F), BF16),
        pltpu.VMEM((T, F), BF16),
        pltpu.VMEM((T, F), BF16),
        pltpu.VMEM((T, F), BF16),
        pltpu.VMEM((1, F), F32),
        pltpu.VMEM((E, F), F32),
        pltpu.VMEM((T, LANES), F32),
        pltpu.VMEM((H, 8, T), F32),
        pltpu.VMEM((E, 8, LANES), F32),
        pltpu.VMEM((E - 1, 8, LANES), F32),
        pltpu.VMEM((all_rows, LANES), F32),
        dma((A_SLOTS, 2)),
        dma((R_SLOTS, 2)),
        dma((3, E)),
        dma((3, E)),
        dma((3, H, E)),
        dma((3, H, E)),
        dma((H,)),
        dma((H,)),
        dma((2, H, n_cols)),
        dma((2, H, n_cols)),
        dma((2, E, n_cols)),
        dma((2, E, n_cols)),
        dma((E,)),
        dma((E,)),
        dma((H,)),
        dma((H,)),
        dma((2,)),
        dma((2,)),
        dma((5 + n_cols,)),
        dma((5 + n_cols,)),
        dma((H,)),
        dma((H,)),
        dma((E,)),
        dma((E,)),
    ]
    result = pl.pallas_call(
        functools.partial(kernel, (E, H, T, F, D, ffd, cap, tn, tw)),
        out_shape=jax.ShapeDtypeStruct((2, T, F), BF16),
        in_specs=[vmem] * 7 + [hbm] * 3,
        out_specs=vmem,
        scratch_shapes=scratch,
        compiler_params=pltpu.CompilerParams(
            collective_id=0, has_side_effects=True, vmem_limit_bytes=67043328
        ),
        name="relay",
    )(
        saved_input[0], cotangent[0], next_input[0], routes_saved[0].T, routes_next[0].T, norm_gain, router[0].T,
        expert_gate[0, 0], expert_up[0, 0], expert_down[0, 0],
    )
    return (result[0:1], result[1:2])


def solution(mesh):
    placed = (
        P("section", "expert", "hid"),
        P("section", "expert", "hid"),
        P("section", "expert", "hid"),
        P("section", "expert", None),
        P("section", "expert", None),
        P("section", "hid"),
        P("section", "hid", None),
        P("section", "expert", None, "hid"),
        P("section", "expert", None, "hid"),
        P("section", "expert", "hid", None),
    )
    return jax.shard_map(
        per_device,
        mesh=mesh,
        in_specs=placed,
        out_specs=(P("section", "expert", "hid"), P("section", "expert", "hid")),
        check_vma=False,
    )
```

```python
import functools

import jax
import jax.numpy as jnp
from jax import lax
from jax.experimental import pallas as pl
from jax.experimental.pallas import tpu as pltpu
from jax.sharding import PartitionSpec as P

EPSILON = 1e-05
F32 = jnp.float32
BF16 = jnp.bfloat16
I32 = jnp.int32
NN = (((1,), (0,)), ((), ()))
NT = (((1,), (1,)), ((), ()))
LANES = 128
A_SLOTS = 3
R_SLOTS = 4
NXT, SAV, COT = 0, 1, 2


def bits_of(count):
    return [1 << bit for bit in range(count.bit_length() - 1)]


def low_bit(number):
    return number & -number


def flip(value, mask, count):
    total = 0
    for bit in bits_of(count):
        own = lax.rem(lax.div(value, bit), 2)
        if isinstance(mask, int):
            got = 1 - own if mask & bit else own
        else:
            other = lax.rem(lax.div(mask, bit), 2)
            got = own + other - 2 * own * other
        total = total + bit * got
    return total


def dot(a, b, dims=NN):
    return lax.dot_general(a, b, dims, preferred_element_type=F32)


def kernel(
    sizes,
    saved_ref, cot_ref, next_ref, pair_saved_ref, pair_next_ref, gain_ref, table_ref, wg_ref, wu_ref, wd_ref,
    out_ref,
    rows, slots, wa, wr, pair, hid_n, grads, rs_send, rs_recv, own_part, home_send, home,
    stat_send, stat_recv, dots_acc, dots_send, dots_recv, tail_send, tail_recv,
    cols, mixed, there_send, there_recv, far_cot, far_saved, far_value, far_gain, far_table, far_cols, far_tail, scale_send, scale_recv, scales, leans,
    wa_sem, wr_sem,
    z_send, z_recv, g_send, g_recv, s_send, s_recv, r_send, r_recv,
    b_send, b_recv, d_send, d_recv, t_send, t_recv, y_send, y_recv, e_send, e_recv, f_send, f_recv, c_send, c_recv,
):
    E, H, T, F, D, ffd, cap, tn, tw, tc = sizes
    n_tiles, n_wide, n_cols = ffd // tn, F // tw, F // tc
    steps = H * n_wide
    all_rows = E * cap
    sec, me, hi = lax.axis_index("section"), lax.axis_index("expert"), lax.axis_index("hid")
    hid_peer = [flip(hi, m, H) for m in range(H)]
    exp_peer = [flip(me, k, E) for k in range(E)]
    to_send = []
    none = me * 0

    def remote(src, dst, send, recv, e=None, h=None, s=None):
        where = (sec if s is None else s, me if e is None else e, hi if h is None else h)
        return pltpu.make_async_remote_copy(
            src_ref=src, dst_ref=dst, send_sem=send, recv_sem=recv,
            device_id=where, device_id_type=pl.DeviceIdType.MESH,
        )

    def send(build):
        build().start()
        to_send.append(build)

    back_order = [(m, c) for c in range(n_wide) for m in reversed(range(H))]
    if H == 4 and n_wide == 4:
        back_order = [(m, c) for c in (0, 1) for m in (3, 2)] + [(1, 0), (0, 0)]
        back_order += [(m, c) for c in (2, 3) for m in (3, 2)] + [(m, c) for c in (1, 2, 3) for m in (1, 0)]

    def place_of(i, kind):
        if kind == "out":
            return H - 1 - lax.div(i, n_wide // 2), lax.rem(i, n_wide // 2)
        code = sum(jnp.where(i == j, m * n_wide + c, 0) for j, (m, c) in enumerate(back_order))
        return lax.div(code, n_wide), lax.rem(code, n_wide)

    def out_copy(i, slot):
        m, c = place_of(i, "out")
        col = pl.multiple_of(flip(hi, m, H) * F + c * 2 * tw, 2 * tw)
        return pltpu.make_async_copy(
            wd_ref.at[:, pl.ds(col, 2 * tw)], wa.at[slot, pl.ds(0, ffd), pl.ds(0, 2 * tw)], wa_sem.at[slot, 0])

    def a_copies(kind, j, slot):
        if kind == "out":
            return [out_copy(j, slot)]
        col = pl.multiple_of(j * tn, tn)
        return [
            pltpu.make_async_copy(w.at[:, pl.ds(col, tn)], wa.at[slot, :, pl.ds(half * tn, tn)], wa_sem.at[slot, half])
            for half, w in enumerate((wg_ref, wu_ref))
        ]

    out_items = steps // 2

    def start_a(g):
        slot = lax.rem(g, A_SLOTS)

        @pl.when((g < n_tiles) | (g >= n_tiles + out_items) & (g < 2 * n_tiles + out_items))
        def _():
            for copy in a_copies("pair", lax.rem(jnp.where(g < n_tiles, g, g - out_items - n_tiles), n_tiles), slot):
                copy.start()

        @pl.when((g >= n_tiles) & (g < n_tiles + out_items))
        def _():
            for copy in a_copies("out", g - n_tiles, slot):
                copy.start()

    def gh_copy(j):
        slot = lax.rem(j, R_SLOTS)
        return pltpu.make_async_copy(
            wd_ref.at[pl.ds(pl.multiple_of(j * tn, tn), tn), :], wr.at[slot, pl.ds(0, tn), pl.ds(0, D)],
            wr_sem.at[slot, 0])

    def back_copies(i):
        slot = lax.rem(n_tiles + i, R_SLOTS)
        m, c = place_of(i, "back")
        row = pl.multiple_of(flip(hi, m, H) * F + c * tw, tw)
        return [
            pltpu.make_async_copy(
                w.at[pl.ds(row, tw), :], wr.at[slot, pl.ds(0, tw), pl.ds(half * ffd, ffd)], wr_sem.at[slot, half])
            for half, w in enumerate((wg_ref, wu_ref))
        ]

    def start_r(g):
        @pl.when(g < n_tiles)
        def _():
            gh_copy(g).start()

        @pl.when((g >= n_tiles) & (g < n_tiles + steps))
        def _():
            for copy in back_copies(g - n_tiles):
                copy.start()

    for j in range(min(R_SLOTS - 1, n_tiles)):
        gh_copy(none + j).start()
    for g in range(A_SLOTS - 1):
        for copy in a_copies("pair", none + g, none + g):
            copy.start()

    barrier = pltpu.get_barrier_semaphore()
    partners = [(sec, me, hid_peer[m]) for m in range(1, H)]
    partners += [(sec, exp_peer[k], hi) for k in range(1, E)]
    partners += [(1 - sec, me, hid_peer[m]) for m in range(H)]
    for where in partners:
        pl.semaphore_signal(barrier, inc=1, device_id=where, device_id_type=pl.DeviceIdType.MESH)
    lane = lax.broadcasted_iota(I32, (T, LANES), 1)
    gain = gain_ref[...]
    route_rows = jnp.concatenate(
        [pair_saved_ref[...].astype(F32), pair_next_ref[...].astype(F32), jnp.zeros((LANES - 4, T), F32)], axis=0)
    spread = route_rows.T
    route_cols = [spread[:, n:n + 1] for n in range(4)]
    first_i = lax.broadcasted_iota(I32, (T, T), 0)
    second_i = lax.broadcasted_iota(I32, (T, T), 1)
    upper = jnp.where(first_i < second_i, 1.0, 0.0).astype(BF16)
    lower = jnp.where(first_i > second_i, 1.0, 0.0).astype(BF16)
    slot_i = lax.broadcasted_iota(I32, (cap, T), 0).astype(F32)
    lane_f = lane.astype(F32)

    def chosen(base, expert):
        first, second = route_rows[base:base + 1], route_rows[base + 1:base + 2]
        wanted = expert.astype(F32)
        hit = jnp.where(first == wanted, 1.0, 0.0) + jnp.where(second == wanted, 1.0, 0.0)
        rank = dot(jnp.broadcast_to(hit, (16, T)).astype(BF16), upper)[0:1]
        rank = jnp.where(hit > 0.5, rank, -1.0)
        return jnp.where(slot_i == rank, 1.0, 0.0).astype(BF16)

    def put(n, value):
        cols[:, n:n + 1] = value

    kept_ranks = []
    for n, base in enumerate((0, 2)):
        hits = jnp.where(lane_f == route_cols[base], 1.0, 0.0) + jnp.where(lane_f == route_cols[base + 1], 1.0, 0.0)
        ranks = dot(lower, hits.astype(BF16))
        kept_ranks.append((hits, ranks))
        for c in range(2):
            route = route_cols[base + c]
            put(16 + 2 * n + c, jnp.sum(jnp.where(lane_f == route, ranks, 0.0), axis=1, keepdims=True))
            put(20 + 2 * n + c, route)

    order = list(range(E - 1, 0, -1))
    inner = flip(lax.rem(me, 2), lax.rem(lax.div(me, 2), 2), 2)
    arrivals = [1, 3, 2] if E == 4 else order

    def by_class(build):
        if E != 4:
            build(0)
            return
        for kind in range(2):
            pl.when(inner == kind)(functools.partial(build, kind))

    def first_wave(tau):
        for k in arrivals:
            dispatch_copy(tau, k).start()

    def region(tau, expert, feature):
        return rows.at[tau, pl.ds(pl.multiple_of(expert * cap, 16), cap), pl.ds(pl.multiple_of(feature * F, LANES), F)]

    def forward_copy(tau, piece, bit, k):
        part = region(tau, exp_peer[k], hid_peer[piece])
        return remote(part, part, g_send.at[tau, piece + bit, k], g_recv.at[tau, piece + bit, k], h=hid_peer[bit])

    def forwards(tau, piece, k):
        return [
            functools.partial(forward_copy, tau, piece, bit, k)
            for bit in reversed(bits_of(H)) if piece == 0 or bit < low_bit(piece)
        ]

    def forward(tau, k):
        for build in forwards(tau, 0, k):
            build().start()

    def got_piece(tau, piece, k):
        part = region(tau, exp_peer[k], hid_peer[piece])
        remote(part, part, g_send.at[tau, piece, k], g_recv.at[tau, piece, k], h=hid_peer[low_bit(piece)]).wait_recv()

    def dispatch_copy(tau, k):
        return remote(
            slots.at[tau, k - 1], region(tau, me, hi), z_send.at[tau, k], z_recv.at[tau, k], e=exp_peer[k])

    def dispatch(tau, base, tokens):
        for k in order + [0]:
            picked = dot(chosen(base, exp_peer[k]), tokens).astype(BF16)
            if k == 0:
                rows[tau, pl.ds(pl.multiple_of(me * cap, 16), cap), pl.ds(pl.multiple_of(hi * F, LANES), F)] = picked
            else:
                slots[tau, k - 1] = picked

    def z_event(tau, n):
        k = arrivals[n]
        part = region(tau, exp_peer[k], hi)
        remote(part, part, z_send.at[tau, k], z_recv.at[tau, k], e=exp_peer[k]).wait_recv()
        forward(tau, k)
        if tau == NXT and n == E - 2:
            first_wave(SAV)
        if tau == SAV and n >= E - 3:
            by_class(lambda kind: first_wave(COT) if kind == E - 2 - n or E != 4 and n == E - 2 else None)
        if tau + 1 == SAV and n == E - 2:
            forward(SAV, 0)

    relays = [p for top in reversed(bits_of(H)) if top > 1 for p in range(top, H, 2 * top)]

    def relay(tau, k):
        for piece in relays:
            got_piece(tau, piece, k)
            for build in forwards(tau, piece, k):
                build().start()

    def x_event(tau, n):
        relay(tau, arrivals[n - 1] if n else 0)

    def gather_events(tau):
        events = [functools.partial(x_event, tau, 0)]
        for n in range(E - 1):
            events.insert(-1, functools.partial(z_event, tau, n))
            events.append(functools.partial(x_event, tau, n + 1))
        return events

    def complete(tau):
        for piece in range(1, H, 2):
            for k in range(E):
                got_piece(tau, piece, k)

    stats = jnp.zeros((T, LANES), F32)
    for offset, ref in ((0, saved_ref), (16, next_ref)):
        values = ref[...].astype(F32)
        stats = stats + jnp.where(lane == offset, jnp.sum(values * values, axis=1, keepdims=True), 0.0)
        for e in range(E):
            weights = table_ref[e:e + 1, :] * gain
            stats = stats + jnp.where(lane == offset + 1 + e, jnp.sum(values * weights, axis=1, keepdims=True), 0.0)
    stat_send[...] = stats.T[0:32]

    def all_to_hid(src, dst, sent, recv):
        copies = [remote(src, dst.at[m - 1], sent.at[m], recv.at[m], h=hid_peer[m]) for m in range(1, H)]
        for copy in copies:
            send(lambda copy=copy: copy)
        return copies

    dispatch(NXT, 2, (next_ref[...].astype(F32) * gain).astype(BF16))
    dispatch(COT, 0, cot_ref[...])

    pl.semaphore_wait(barrier, len(partners))
    stat_copies = all_to_hid(stat_send, stat_recv, s_send, s_recv)
    first_wave(NXT)
    forward(NXT, 0)
    forward(COT, 0)
    total = stats.T[0:32]
    for m, copy in enumerate(stat_copies):
        copy.wait_recv()
        total = total + stat_recv[m]
    stats = jnp.concatenate([total, jnp.zeros((LANES - 32, T), F32)], axis=0).T

    def finish_norm(offset, base, keep):
        scale = lax.rsqrt(stats[:, offset:offset + 1] / D + EPSILON)
        first_score = jnp.zeros((T, 1), F32)
        second_score = jnp.zeros((T, 1), F32)
        for e in range(E):
            score = stats[:, offset + 1 + e:offset + 2 + e]
            first_score = first_score + jnp.where(route_cols[base] == e, score, 0.0)
            second_score = second_score + jnp.where(route_cols[base + 1] == e, score, 0.0)
        first, second = first_score * scale, second_score * scale
        put(keep, jax.nn.sigmoid(first - second))
        put(keep + 1, jax.nn.sigmoid(second - first))
        put(keep + 2, scale)
        put(keep + 3, first_score - second_score)
        return scale

    scale = finish_norm(16, 2, 4)
    hits, ranks = kept_ranks[1]
    for k in range(E):
        named = lane == exp_peer[k]
        rank = jnp.sum(jnp.where(named, ranks, 0.0), axis=1, keepdims=True)
        hit = jnp.sum(jnp.where(named, hits, 0.0), axis=1, keepdims=True)
        rank = jnp.where(hit > 0.5, rank, -1.0)
        row = jnp.sum(jnp.where(lane_f == rank, scale, 0.0), axis=0, keepdims=True)
        scale_send[k] = jnp.broadcast_to(row, (8, LANES))

    def scale_copy(k):
        return remote(scale_send.at[k], scale_recv.at[k - 1], c_send.at[k], c_recv.at[k], e=exp_peer[k])

    for k in range(1, E):
        send(functools.partial(scale_copy, k))
    scale = finish_norm(0, 0, 0)
    dispatch(SAV, 0, (saved_ref[...].astype(F32) * scale * gain).astype(BF16))

    far = [(cols, far_cols), (gain_ref, far_gain), (table_ref, far_table), (cot_ref, far_cot), (saved_ref, far_saved)]

    def far_copy(n):
        return remote(far[n][0], far[n][1], e_send.at[n], e_recv.at[n], s=1 - sec)

    def far_value_copy(c):
        part = pl.ds(c * tc, tc)
        n = len(far) + c
        return remote(there_send.at[:, part], far_value.at[:, part], e_send.at[n], e_recv.at[n], s=1 - sec)

    @pl.when(sec == 1)
    def _():
        for n in range(len(far)):
            far_copy(n).start()

    def lean_of(place_in, kept, table, gains):
        total = jnp.zeros((T, F), F32)
        for e in range(E):
            sign = jnp.where(kept[:, 20:21] == e, 1.0, 0.0) - jnp.where(kept[:, 21:22] == e, 1.0, 0.0)
            total = total + sign * table[e:e + 1, :]
        leans[place_in] = kept[:, 2:3] * total * gains[...]

    def reduce_step(which, acc, m_now, first, count):
        @pl.when(m_now == 0)
        def _():
            for n in range(count):
                own_part[which, first + n] = acc[:, n * tc:(n + 1) * tc]

        for m in range(1, H):
            @pl.when(m_now == m)
            def _():
                for n in range(count):
                    c = first + n
                    value = acc[:, n * tc:(n + 1) * tc]
                    for bit in bits_of(low_bit(m) * 2)[:-1]:
                        received(which, m + bit, c)
                        value = value + rs_recv[which, m + bit - 1, c].astype(F32)
                    rs_send[which, m - 1, c] = value.astype(BF16)
                    if which == 1 or m == 1 or m != low_bit(m):
                        reduce_copy(which, m, c).start()

    def reduce_copy(which, m, c):
        return remote(
            rs_send.at[which, m - 1, c], rs_recv.at[which, m - 1, c],
            r_send.at[which, m, c], r_recv.at[which, m, c], h=hid_peer[low_bit(m)])

    def received(which, m, c):
        reduce_copy(which, m, c).wait_recv()

    def home_region(which, expert, c):
        return home.at[which, pl.ds(pl.multiple_of(expert * cap, 16), cap), pl.ds(c * tc, tc)]

    def home_copy(which, k, c):
        return remote(
            home_send.at[which, c, pl.ds(pl.multiple_of(exp_peer[k] * cap, 16), cap)], home_region(which, me, c),
            b_send.at[which, k, c], b_recv.at[which, k, c], e=exp_peer[k])

    def home_event(which, c):
        value = own_part[which, c]
        for bit in bits_of(H):
            received(which, bit, c)
            value = value + rs_recv[which, bit - 1, c].astype(F32)
        home_send[which, c] = value.astype(BF16)
        for k in arrivals:
            send(functools.partial(home_copy, which, k, c))
        mine = pl.ds(pl.multiple_of(me * cap, 16), cap)
        home[which, mine, c * tc:(c + 1) * tc] = home_send[which, c, mine, :]

    def home_wait(which, c):
        for k in order:
            part = home_region(which, exp_peer[k], c)
            remote(part, part, b_send.at[which, k, c], b_recv.at[which, k, c], e=exp_peer[k]).wait_recv()

    wide_i = lax.broadcasted_iota(I32, (T, all_rows), 1).astype(F32)

    def selectors(n):
        picks = []
        for c in range(2):
            rank, route = cols[:, 16 + 2 * n + c:17 + 2 * n + c], cols[:, 20 + 2 * n + c:21 + 2 * n + c]
            picks.append(jnp.where(wide_i == route * cap + rank, 1.0, 0.0).astype(BF16))
        return picks

    def blended(which, keep, part, picks):
        part = home[which, :, part]
        return cols[:, keep:keep + 1] * dot(picks[0], part) + cols[:, keep + 1:keep + 2] * dot(picks[1], part)

    def there_copy(n, height):
        part = pl.ds(n * height, height)
        return remote(there_send.at[part], there_recv.at[part], y_send.at[n], y_recv.at[n], s=1 - sec)

    halves = 2
    half_rows = T // halves

    def forward_out():
        picks = selectors(1)
        for c in range(n_wide):
            for n in range(c * tw // tc, (c + 1) * tw // tc):
                home_wait(0, n)
            part = slice(c * tw, (c + 1) * tw)
            value = (next_ref[:, part].astype(F32) + blended(0, 4, part, picks)).astype(BF16)

            @pl.when(sec == 0)
            def _():
                there_send[:, part] = value

            @pl.when(sec == 1)
            def _():
                out_ref[0, :, part] = value

        @pl.when(sec == 0)
        def _():
            for n in range(halves):
                there_copy(n, half_rows).start()

    def run(events, index):
        for at, event in events:
            pl.when(index == at)(event)

    next_events, cot_events = gather_events(NXT), gather_events(COT)
    for event in next_events[:-2]:
        event()
    lean_of(0, cols, table_ref, gain_ref)

    @pl.when(sec == 0)
    def _():
        for n in range(len(far)):
            far_copy(n).wait_recv()
        lean_of(1, far_cols, far_table, far_gain)

    for event in next_events[-2:]:
        event()
    complete(NXT)
    for k in range(E):
        if k:
            scale_copy(k).wait_recv()
        row = scale_recv[k - 1, 0:1] if k else scale_send[0, 0:1]
        scales[pl.ds(pl.multiple_of(exp_peer[k] * cap, 16), cap), :] = jnp.broadcast_to(row, (LANES, LANES)).T[0:cap]

    def at(events, spots):
        return list(zip(spots, events))

    def split(event, late, soon):
        return [(late + (soon - late) * (1 - inner), event)]

    wide_sends = [(m, c) for m in reversed(bits_of(H)) if m > 1 for c in range(n_cols)]

    def wave(start, stop):
        return [functools.partial(lambda m, c: reduce_copy(0, m, c).start(), m, c) for m, c in wide_sends[start:stop]]

    downs = [functools.partial(home_event, 0, c) for c in range(n_cols)]
    tuned = E == 4 and H == 4 and n_cols == 8 and n_wide == 4 and n_tiles == 7
    saved_events = gather_events(SAV)
    if tuned:
        up_events = at(saved_events[:6], [0, 1, 2, 3, 4, 5])
        out_events = at(saved_events[6:], [1]) + at(cot_events[:1], [2]) + at(cot_events[2:3], [6])
        gate_events = at(cot_events[3:5], [1, 1]) + at(wave(0, 8), [1] * 8) + at(cot_events[5:], [4, 6])
        gh_events = at(downs[:4], [1, 1, 4, 5])
        back_events = at(downs[4:], [1, 1, 4, 5])
        back_spots = [6, 8, 12, 12, 14]
    else:
        up_events = at(saved_events, [n_tiles * n // len(saved_events) for n in range(len(saved_events))])
        out_events = []
        late_events = cot_events[:1] + cot_events[2:]
        gate_events = at(late_events, [n_tiles * n // len(late_events) for n in range(len(late_events))])
        waves = wave(0, len(wide_sends))
        gate_events += at(waves, [n_tiles - 1] * len(waves))
        gh_events = []
        back_events = at(downs, [2 + c for c in range(n_cols)])
        back_spots = []
    cot_events[1]()

    @pl.loop(0, n_tiles)
    def _(j):
        start_a(j + A_SLOTS - 1)
        run(up_events, j)
        slot = lax.rem(j, A_SLOTS)
        for copy in a_copies("pair", j, slot):
            copy.wait()
        both = dot(rows[NXT], wa[slot, :, 0:2 * tn]) * scales[:, 0:1]
        gate, up = both[:, 0:tn], both[:, tn:2 * tn]
        hid_n[:, pl.ds(pl.multiple_of(j * tn, tn), tn)] = (gate * jax.nn.sigmoid(gate) * up).astype(BF16)

    @pl.loop(0, out_items)
    def _(i):
        g = n_tiles + i
        start_a(g + A_SLOTS - 1)
        run(out_events, i)
        slot = lax.rem(g, A_SLOTS)
        out_copy(i, slot).wait()
        acc = dot(hid_n[...], wa[slot, 0:ffd, 0:2 * tw])
        m, c = place_of(i, "out")
        reduce_step(0, acc, m, c * (2 * tw // tc), 2 * tw // tc)

    complete(SAV)

    dots_acc[...] = jnp.zeros_like(dots_acc)
    @pl.loop(0, n_tiles)
    def _(j):
        g = n_tiles + out_items + j
        start_a(g + A_SLOTS - 1)
        run(gate_events, j)
        slot = lax.rem(g, A_SLOTS)
        for copy in a_copies("pair", j, slot):
            copy.wait()
        part = pl.ds(pl.multiple_of(j * tn, tn), tn)
        both = dot(rows[SAV], wa[slot, :, 0:2 * tn])
        pair[0, :, part] = both[:, 0:tn]
        pair[1, :, part] = both[:, tn:2 * tn]

    complete(COT)

    @pl.loop(0, n_tiles)
    def _(j):
        start_r(j + R_SLOTS - 1)
        run(gh_events, j)
        gh_copy(j).wait()
        slot = lax.rem(j, R_SLOTS)
        grad = dot(rows[COT], wr[slot, 0:tn, 0:D], NT)
        part = pl.ds(pl.multiple_of(j * tn, tn), tn)
        gate, up = pair[0, :, part], pair[1, :, part]
        sig = jax.nn.sigmoid(gate)
        silu = gate * sig
        hidden = (silu * up).astype(BF16).astype(F32)
        grads[0, :, part] = (grad * up * (sig * (1.0 + gate * (1.0 - sig)))).astype(BF16)
        grads[1, :, part] = (grad * silu).astype(BF16)
        product = grad * hidden
        partial = product[:, 0:LANES]
        for n in range(1, tn // LANES):
            partial = partial + product[:, n * LANES:(n + 1) * LANES]
        dots_acc[...] += partial

    def dots_copy(k):
        return remote(dots_send, dots_recv.at[k - 1], d_send.at[k], d_recv.at[k], e=exp_peer[k])

    dots_send[...] = jnp.broadcast_to(jnp.sum(dots_acc[...].T, axis=0, keepdims=True), (8, all_rows))
    for k in order:
        send(functools.partial(dots_copy, k))

    def dots_event():
        for k in order:
            dots_copy(k).wait_recv()
        gap = jnp.zeros((T, 1), F32)
        for k in range(E):
            row = dots_send[0:1] if k == 0 else dots_recv[k - 1, 0:1]
            expert = exp_peer[k].astype(F32)
            for c, sign in ((0, 1.0), (1, -1.0)):
                rank, route = cols[:, 16 + c:17 + c], cols[:, 20 + c:21 + c]
                spot = jnp.where(route == expert, me.astype(F32) * cap + rank, -1.0)
                gap = gap + sign * jnp.sum(jnp.where(wide_i == spot, row, 0.0), axis=1, keepdims=True)
        dots_acc[0:T, 0:1] = gap

    back_events += at([functools.partial(home_event, 1, c) for c in range(n_cols)], back_spots)

    @pl.loop(0, steps)
    def _(i):
        start_r(n_tiles + i + R_SLOTS - 1)
        run(back_events, i)
        for copy in back_copies(i):
            copy.wait()
        slot = lax.rem(n_tiles + i, R_SLOTS)
        acc = dot(grads[0], wr[slot, 0:tw, 0:ffd], NT) + dot(grads[1], wr[slot, 0:tw, ffd:2 * ffd], NT)
        m, c = place_of(i, "back")
        reduce_step(1, acc, m, c * (tw // tc), tw // tc)

    later = list(range(len(back_spots), n_cols))
    for c in later[:1]:
        home_event(1, c)
    forward_out()
    dots_event()
    for c in later[1:]:
        home_event(1, c)
    picks = selectors(0)
    inner = jnp.zeros((T, 1), F32)
    for c in range(n_cols):
        home_wait(1, c)
        part = slice(c * tc, (c + 1) * tc)
        value = blended(1, 0, part, picks) * gain_ref[:, part]
        mixed[:, part] = cot_ref[:, part].astype(F32) + cols[:, 2:3] * value

        @pl.when(sec == 1)
        def _():
            there_send[:, part] = value.astype(BF16)
            far_value_copy(c).start()

        inner = inner + jnp.sum(value * saved_ref[:, part].astype(F32), axis=1, keepdims=True)
    message = jnp.where(lane == 0, inner, 0.0) + jnp.where(lane == 1, dots_acc[0:T, 0:1], 0.0)
    message = message.T[0:8]
    tail_send[...] = message

    def tail_copy(m):
        return remote(tail_send, tail_recv.at[m - 1], t_send.at[m], t_recv.at[m], h=hid_peer[m])

    def far_tail_copy(m):
        return remote(tail_send, far_tail.at[m], f_send.at[m], f_recv.at[m], h=hid_peer[m], s=1 - sec)

    def input_gradient(message, base, saved, kept, place_in):
        message = jnp.concatenate([message, jnp.zeros((LANES - 8, T), F32)], axis=0).T
        scale = kept[:, 2:3]
        slope = message[:, 1:2] * kept[:, 0:1] * kept[:, 1:2]
        inner = message[:, 0:1] + slope * kept[:, 3:4]
        pull = scale * scale * scale * (inner / D)
        out_ref[place_in] = (base() + slope * leans[place_in] - saved[...].astype(F32) * pull).astype(BF16)

    @pl.when(sec == 1)
    def _():
        for m in range(H):
            far_tail_copy(m).start()
        for n in range(halves):
            there_copy(n, half_rows).wait_recv()
        out_ref[1] = there_recv[...]
        for n in range(len(far)):
            far_copy(n).wait_send()
        for c in range(n_cols):
            far_value_copy(c).wait_send()
        for m in range(H):
            far_tail_copy(m).wait_send()

    @pl.when(sec == 0)
    def _():
        for m in range(1, H):
            tail_copy(m).start()
        total = message
        for m in range(1, H):
            tail_copy(m).wait_recv()
            total = total + tail_recv[m - 1]
        input_gradient(total, lambda: mixed[...], saved_ref, cols, 0)
        for c in range(n_cols):
            far_value_copy(c).wait_recv()
        total = jnp.zeros((8, T), F32)
        for m in range(H):
            far_tail_copy(m).wait_recv()
            total = total + far_tail[m]
        input_gradient(
            total, lambda: far_cot[...].astype(F32) + far_cols[:, 2:3] * far_value[...].astype(F32),
            far_saved, far_cols, 1)
        for m in range(1, H):
            tail_copy(m).wait_send()
        for n in range(halves):
            there_copy(n, half_rows).wait_send()

    for build in to_send:
        build().wait_send()
    for tau in range(3):
        for k in range(E):
            if k:
                dispatch_copy(tau, k).wait_send()
            for piece in [0] + relays:
                for build in forwards(tau, piece, k):
                    build().wait_send()
    for which in range(2):
        for m in range(1, H):
            for c in range(n_cols):
                reduce_copy(which, m, c).wait_send()


def per_device(
    saved_input,
    cotangent,
    next_input,
    routes_saved,
    routes_next,
    norm_gain,
    router,
    expert_gate,
    expert_up,
    expert_down,
):
    E, H = lax.axis_size("expert"), lax.axis_size("hid")
    T, F = saved_input.shape[1:]
    D, ffd = expert_gate.shape[2:]
    cap = 3 * T // router.shape[2]
    tn = 2 * LANES if ffd % (2 * LANES) == 0 else LANES
    tw = 2 * LANES if F % (2 * LANES) == 0 else LANES
    tc = LANES
    n_cols, all_rows = F // tc, E * cap
    deep, wide = max(tn, tw), max(D, 2 * ffd)
    vmem = pl.BlockSpec(memory_space=pltpu.VMEM)
    hbm = pl.BlockSpec(memory_space=pl.ANY)
    dma = pltpu.SemaphoreType.DMA
    scratch = [
        pltpu.VMEM((3, all_rows, D), BF16),
        pltpu.VMEM((3, E - 1, cap, F), BF16),
        pltpu.VMEM((A_SLOTS, D, 2 * deep), BF16),
        pltpu.VMEM((R_SLOTS, deep, wide), BF16),
        pltpu.VMEM((2, all_rows, ffd), F32),
        pltpu.VMEM((all_rows, ffd), BF16),
        pltpu.VMEM((2, all_rows, ffd), BF16),
        pltpu.VMEM((2, H - 1, n_cols, all_rows, tc), BF16),
        pltpu.VMEM((2, H - 1, n_cols, all_rows, tc), BF16),
        pltpu.VMEM((2, n_cols, all_rows, tc), F32),
        pltpu.VMEM((2, n_cols, all_rows, tc), BF16),
        pltpu.VMEM((2, all_rows, F), BF16),
        pltpu.VMEM((32, T), F32),
        pltpu.VMEM((H - 1, 32, T), F32),
        pltpu.VMEM((all_rows, LANES), F32),
        pltpu.VMEM((8, all_rows), F32),
        pltpu.VMEM((E - 1, 8, all_rows), F32),
        pltpu.VMEM((8, T), F32),
        pltpu.VMEM((H - 1, 8, T), F32),
        pltpu.VMEM((T, LANES), F32),
        pltpu.VMEM((T, F), F32),
        pltpu.VMEM((T, F), BF16),
        pltpu.VMEM((T, F), BF16),
        pltpu.VMEM((T, F), BF16),
        pltpu.VMEM((T, F), BF16),
        pltpu.VMEM((T, F), BF16),
        pltpu.VMEM((1, F), F32),
        pltpu.VMEM((E, F), F32),
        pltpu.VMEM((T, LANES), F32),
        pltpu.VMEM((H, 8, T), F32),
        pltpu.VMEM((E, 8, LANES), F32),
        pltpu.VMEM((E - 1, 8, LANES), F32),
        pltpu.VMEM((all_rows, LANES), F32),
        pltpu.VMEM((2, T, F), F32),
        dma((A_SLOTS, 2)),
        dma((R_SLOTS, 2)),
        dma((3, E)),
        dma((3, E)),
        dma((3, H, E)),
        dma((3, H, E)),
        dma((H,)),
        dma((H,)),
        dma((2, H, n_cols)),
        dma((2, H, n_cols)),
        dma((2, E, n_cols)),
        dma((2, E, n_cols)),
        dma((E,)),
        dma((E,)),
        dma((H,)),
        dma((H,)),
        dma((2,)),
        dma((2,)),
        dma((5 + n_cols,)),
        dma((5 + n_cols,)),
        dma((H,)),
        dma((H,)),
        dma((E,)),
        dma((E,)),
    ]
    result = pl.pallas_call(
        functools.partial(kernel, (E, H, T, F, D, ffd, cap, tn, tw, tc)),
        out_shape=jax.ShapeDtypeStruct((2, T, F), BF16),
        in_specs=[vmem] * 7 + [hbm] * 3,
        out_specs=vmem,
        scratch_shapes=scratch,
        compiler_params=pltpu.CompilerParams(
            collective_id=0, has_side_effects=True, vmem_limit_bytes=67043328
        ),
        name="relay",
    )(
        saved_input[0], cotangent[0], next_input[0], routes_saved[0].T, routes_next[0].T, norm_gain, router[0].T,
        expert_gate[0, 0], expert_up[0, 0], expert_down[0, 0],
    )
    return (result[0:1], result[1:2])


def solution(mesh):
    placed = (
        P("section", "expert", "hid"),
        P("section", "expert", "hid"),
        P("section", "expert", "hid"),
        P("section", "expert", None),
        P("section", "expert", None),
        P("section", "hid"),
        P("section", "hid", None),
        P("section", "expert", None, "hid"),
        P("section", "expert", None, "hid"),
        P("section", "expert", "hid", None),
    )
    return jax.shard_map(
        per_device,
        mesh=mesh,
        in_specs=placed,
        out_specs=(P("section", "expert", "hid"), P("section", "expert", "hid")),
        check_vma=False,
    )
```

```python
import functools

import jax
import jax.numpy as jnp
from jax import lax
from jax.experimental import pallas as pl
from jax.experimental.pallas import tpu as pltpu
from jax.sharding import PartitionSpec as P

EPSILON = 1e-05
F32 = jnp.float32
BF16 = jnp.bfloat16
I32 = jnp.int32
NN = (((1,), (0,)), ((), ()))
NT = (((1,), (1,)), ((), ()))
LANES = 128
A_SLOTS = 3
R_SLOTS = 4
NXT, SAV, COT = 0, 1, 2


def bits_of(count):
    return [1 << bit for bit in range(count.bit_length() - 1)]


def low_bit(number):
    return number & -number


def flip(value, mask, count):
    total = 0
    for bit in bits_of(count):
        own = lax.rem(lax.div(value, bit), 2)
        if isinstance(mask, int):
            got = 1 - own if mask & bit else own
        else:
            other = lax.rem(lax.div(mask, bit), 2)
            got = own + other - 2 * own * other
        total = total + bit * got
    return total


def dot(a, b, dims=NN):
    return lax.dot_general(a, b, dims, preferred_element_type=F32)


def kernel(
    sizes,
    saved_ref, cot_ref, next_ref, pair_saved_ref, pair_next_ref, gain_ref, table_ref, wg_ref, wu_ref, wd_ref,
    out_ref,
    rows, slots, wa, wr, pair, hid_n, grads, rs_send, rs_recv, own_part, home_send, home,
    stat_send, stat_recv, dots_acc, dots_send, dots_recv, tail_send, tail_recv,
    cols, mixed, there_send, there_recv, far_cot, far_saved, far_value, far_gain, far_table, far_cols, far_tail, scale_send, scale_recv, scales, leans,
    wa_sem, wr_sem,
    z_send, z_recv, g_send, g_recv, s_send, s_recv, r_send, r_recv,
    b_send, b_recv, d_send, d_recv, t_send, t_recv, y_send, y_recv, e_send, e_recv, f_send, f_recv, c_send, c_recv,
):
    E, H, T, F, D, ffd, cap, tn, tw, tc = sizes
    n_tiles, n_wide, n_cols = ffd // tn, F // tw, F // tc
    steps = H * n_wide
    all_rows = E * cap
    sec, me, hi = lax.axis_index("section"), lax.axis_index("expert"), lax.axis_index("hid")
    hid_peer = [flip(hi, m, H) for m in range(H)]
    exp_peer = [flip(me, k, E) for k in range(E)]
    to_send = []
    none = me * 0

    def remote(src, dst, send, recv, e=None, h=None, s=None):
        where = (sec if s is None else s, me if e is None else e, hi if h is None else h)
        return pltpu.make_async_remote_copy(
            src_ref=src, dst_ref=dst, send_sem=send, recv_sem=recv,
            device_id=where, device_id_type=pl.DeviceIdType.MESH,
        )

    def send(build):
        build().start()
        to_send.append(build)

    back_order = [(m, c) for c in range(n_wide) for m in reversed(range(H))]
    if H == 4 and n_wide == 4:
        back_order = [(m, c) for c in (0, 1) for m in (3, 2)] + [(1, 0), (0, 0)]
        back_order += [(m, c) for c in (2, 3) for m in (3, 2)] + [(m, c) for c in (1, 2, 3) for m in (1, 0)]

    def place_of(i, kind):
        if kind == "out":
            return H - 1 - lax.div(i, n_wide // 2), lax.rem(i, n_wide // 2)
        code = sum(jnp.where(i == j, m * n_wide + c, 0) for j, (m, c) in enumerate(back_order))
        return lax.div(code, n_wide), lax.rem(code, n_wide)

    def out_copy(i, slot):
        m, c = place_of(i, "out")
        col = pl.multiple_of(flip(hi, m, H) * F + c * 2 * tw, 2 * tw)
        return pltpu.make_async_copy(
            wd_ref.at[:, pl.ds(col, 2 * tw)], wa.at[slot, pl.ds(0, ffd), pl.ds(0, 2 * tw)], wa_sem.at[slot, 0])

    def a_copies(kind, j, slot):
        if kind == "out":
            return [out_copy(j, slot)]
        col = pl.multiple_of(j * tn, tn)
        return [
            pltpu.make_async_copy(w.at[:, pl.ds(col, tn)], wa.at[slot, :, pl.ds(half * tn, tn)], wa_sem.at[slot, half])
            for half, w in enumerate((wg_ref, wu_ref))
        ]

    out_items = steps // 2

    def start_a(g):
        slot = lax.rem(g, A_SLOTS)

        @pl.when((g < n_tiles) | (g >= n_tiles + out_items) & (g < 2 * n_tiles + out_items))
        def _():
            for copy in a_copies("pair", lax.rem(jnp.where(g < n_tiles, g, g - out_items - n_tiles), n_tiles), slot):
                copy.start()

        @pl.when((g >= n_tiles) & (g < n_tiles + out_items))
        def _():
            for copy in a_copies("out", g - n_tiles, slot):
                copy.start()

    def gh_copy(j):
        slot = lax.rem(j, R_SLOTS)
        return pltpu.make_async_copy(
            wd_ref.at[pl.ds(pl.multiple_of(j * tn, tn), tn), :], wr.at[slot, pl.ds(0, tn), pl.ds(0, D)],
            wr_sem.at[slot, 0])

    def back_copies(i):
        slot = lax.rem(n_tiles + i, R_SLOTS)
        m, c = place_of(i, "back")
        row = pl.multiple_of(flip(hi, m, H) * F + c * tw, tw)
        return [
            pltpu.make_async_copy(
                w.at[pl.ds(row, tw), :], wr.at[slot, pl.ds(0, tw), pl.ds(half * ffd, ffd)], wr_sem.at[slot, half])
            for half, w in enumerate((wg_ref, wu_ref))
        ]

    def start_r(g):
        @pl.when(g < n_tiles)
        def _():
            gh_copy(g).start()

        @pl.when((g >= n_tiles) & (g < n_tiles + steps))
        def _():
            for copy in back_copies(g - n_tiles):
                copy.start()

    for j in range(min(R_SLOTS - 1, n_tiles)):
        gh_copy(none + j).start()
    for g in range(A_SLOTS - 1):
        for copy in a_copies("pair", none + g, none + g):
            copy.start()

    barrier = pltpu.get_barrier_semaphore()
    partners = [(sec, me, hid_peer[m]) for m in range(1, H)]
    partners += [(sec, exp_peer[k], hi) for k in range(1, E)]
    partners += [(1 - sec, me, hid_peer[m]) for m in range(H)]
    for where in partners:
        pl.semaphore_signal(barrier, inc=1, device_id=where, device_id_type=pl.DeviceIdType.MESH)
    lane = lax.broadcasted_iota(I32, (T, LANES), 1)
    gain = gain_ref[...]
    route_rows = jnp.concatenate(
        [pair_saved_ref[...].astype(F32), pair_next_ref[...].astype(F32), jnp.zeros((LANES - 4, T), F32)], axis=0)
    spread = route_rows.T
    route_cols = [spread[:, n:n + 1] for n in range(4)]
    first_i = lax.broadcasted_iota(I32, (T, T), 0)
    second_i = lax.broadcasted_iota(I32, (T, T), 1)
    upper = jnp.where(first_i < second_i, 1.0, 0.0).astype(BF16)
    lower = jnp.where(first_i > second_i, 1.0, 0.0).astype(BF16)
    slot_i = lax.broadcasted_iota(I32, (cap, T), 0).astype(F32)
    lane_f = lane.astype(F32)

    def chosen(base, expert):
        first, second = route_rows[base:base + 1], route_rows[base + 1:base + 2]
        wanted = expert.astype(F32)
        hit = jnp.where(first == wanted, 1.0, 0.0) + jnp.where(second == wanted, 1.0, 0.0)
        rank = dot(jnp.broadcast_to(hit, (16, T)).astype(BF16), upper)[0:1]
        rank = jnp.where(hit > 0.5, rank, -1.0)
        return jnp.where(slot_i == rank, 1.0, 0.0).astype(BF16)

    def put(n, value):
        cols[:, n:n + 1] = value

    order = list(range(E - 1, 0, -1))
    inner = flip(lax.rem(me, 2), lax.rem(lax.div(me, 2), 2), 2)
    arrivals = [1, 3, 2] if E == 4 else order

    def by_class(build):
        if E != 4:
            build(0)
            return
        for kind in range(2):
            pl.when(inner == kind)(functools.partial(build, kind))

    def first_wave(tau):
        for k in arrivals:
            for part in parts:
                dispatch_copy(tau, k, part).start()

    parts, width = range(2), F // 2

    def region(tau, expert, feature, part):
        start = pl.multiple_of(feature * F + part * width, LANES)
        return rows.at[tau, pl.ds(pl.multiple_of(expert * cap, 16), cap), pl.ds(start, width)]

    def forward_copy(tau, piece, bit, k, part):
        block = region(tau, exp_peer[k], hid_peer[piece], part)
        return remote(
            block, block, g_send.at[tau, piece + bit, k, part], g_recv.at[tau, piece + bit, k, part],
            h=hid_peer[bit])

    def forwards(tau, piece, k, part):
        return [
            functools.partial(forward_copy, tau, piece, bit, k, part)
            for bit in reversed(bits_of(H)) if piece == 0 or bit < low_bit(piece)
        ]

    def forward(tau, k, some=parts):
        for part in some:
            for build in forwards(tau, 0, k, part):
                build().start()

    def got_piece(tau, piece, k, part):
        block = region(tau, exp_peer[k], hid_peer[piece], part)
        remote(
            block, block, g_send.at[tau, piece, k, part], g_recv.at[tau, piece, k, part],
            h=hid_peer[low_bit(piece)]).wait_recv()

    def dispatch_copy(tau, k, part):
        return remote(
            slots.at[tau, k - 1, :, pl.ds(part * width, width)], region(tau, me, hi, part),
            z_send.at[tau, k, part], z_recv.at[tau, k, part], e=exp_peer[k])

    def dispatch(tau, base, tokens):
        for k in order + [0]:
            picked = dot(chosen(base, exp_peer[k]), tokens).astype(BF16)
            if k == 0:
                rows[tau, pl.ds(pl.multiple_of(me * cap, 16), cap), pl.ds(pl.multiple_of(hi * F, LANES), F)] = picked
            else:
                slots[tau, k - 1] = picked

    def z_event(tau, n):
        k = arrivals[n]
        for part in parts:
            block = region(tau, exp_peer[k], hi, part)
            remote(block, block, z_send.at[tau, k, part], z_recv.at[tau, k, part], e=exp_peer[k]).wait_recv()
            forward(tau, k, [part])
        if tau == NXT and n == E - 2:
            first_wave(SAV)
        if tau == SAV and n >= E - 3:
            by_class(lambda kind: first_wave(COT) if kind == E - 2 - n or E != 4 and n == E - 2 else None)
        if tau + 1 == SAV and n == E - 2:
            forward(SAV, 0)

    relays = [p for top in reversed(bits_of(H)) if top > 1 for p in range(top, H, 2 * top)]

    def relay(tau, k):
        for piece in relays:
            for part in parts:
                got_piece(tau, piece, k, part)
                for build in forwards(tau, piece, k, part):
                    build().start()

    def x_event(tau, n):
        relay(tau, arrivals[n - 1] if n else 0)

    def gather_events(tau):
        events = [functools.partial(x_event, tau, 0)]
        for n in range(E - 1):
            events.insert(-1, functools.partial(z_event, tau, n))
            events.append(functools.partial(x_event, tau, n + 1))
        return events

    def complete(tau):
        for piece in range(1, H, 2):
            for k in range(E):
                for part in parts:
                    got_piece(tau, piece, k, part)

    def all_to_hid(src, dst, sent, recv):
        copies = [remote(src, dst.at[m - 1], sent.at[m], recv.at[m], h=hid_peer[m]) for m in range(1, H)]
        for copy in copies:
            send(lambda copy=copy: copy)
        return copies

    dispatch(NXT, 2, (next_ref[...].astype(F32) * gain).astype(BF16))
    pl.semaphore_wait(barrier, len(partners))
    first_wave(NXT)
    forward(NXT, 0)

    stats = jnp.zeros((T, LANES), F32)
    for offset, ref in ((0, saved_ref), (16, next_ref)):
        values = ref[...].astype(F32)
        stats = stats + jnp.where(lane == offset, jnp.sum(values * values, axis=1, keepdims=True), 0.0)
        for e in range(E):
            weights = table_ref[e:e + 1, :] * gain
            stats = stats + jnp.where(lane == offset + 1 + e, jnp.sum(values * weights, axis=1, keepdims=True), 0.0)
    stat_send[...] = stats.T[0:32]

    stat_copies = all_to_hid(stat_send, stat_recv, s_send, s_recv)
    dispatch(COT, 0, cot_ref[...])
    forward(COT, 0)

    kept_ranks = []
    for n, base in enumerate((0, 2)):
        hits = jnp.where(lane_f == route_cols[base], 1.0, 0.0) + jnp.where(lane_f == route_cols[base + 1], 1.0, 0.0)
        ranks = dot(lower, hits.astype(BF16))
        kept_ranks.append((hits, ranks))
        for c in range(2):
            route = route_cols[base + c]
            put(16 + 2 * n + c, jnp.sum(jnp.where(lane_f == route, ranks, 0.0), axis=1, keepdims=True))
            put(20 + 2 * n + c, route)

    next_events, cot_events = gather_events(NXT), gather_events(COT)
    next_events[0]()
    total = stats.T[0:32]
    for m, copy in enumerate(stat_copies):
        copy.wait_recv()
        total = total + stat_recv[m]
    stats = jnp.concatenate([total, jnp.zeros((LANES - 32, T), F32)], axis=0).T

    def finish_norm(offset, base, keep):
        scale = lax.rsqrt(stats[:, offset:offset + 1] / D + EPSILON)
        first_score = jnp.zeros((T, 1), F32)
        second_score = jnp.zeros((T, 1), F32)
        for e in range(E):
            score = stats[:, offset + 1 + e:offset + 2 + e]
            first_score = first_score + jnp.where(route_cols[base] == e, score, 0.0)
            second_score = second_score + jnp.where(route_cols[base + 1] == e, score, 0.0)
        first, second = first_score * scale, second_score * scale
        put(keep, jax.nn.sigmoid(first - second))
        put(keep + 1, jax.nn.sigmoid(second - first))
        put(keep + 2, scale)
        put(keep + 3, first_score - second_score)
        return scale

    scale = finish_norm(16, 2, 4)
    hits, ranks = kept_ranks[1]
    for k in range(E):
        named = lane == exp_peer[k]
        rank = jnp.sum(jnp.where(named, ranks, 0.0), axis=1, keepdims=True)
        hit = jnp.sum(jnp.where(named, hits, 0.0), axis=1, keepdims=True)
        rank = jnp.where(hit > 0.5, rank, -1.0)
        row = jnp.sum(jnp.where(lane_f == rank, scale, 0.0), axis=0, keepdims=True)
        scale_send[k] = jnp.broadcast_to(row, (8, LANES))

    def scale_copy(k):
        return remote(scale_send.at[k], scale_recv.at[k - 1], c_send.at[k], c_recv.at[k], e=exp_peer[k])

    for k in range(1, E):
        send(functools.partial(scale_copy, k))
    scale = finish_norm(0, 0, 0)
    dispatch(SAV, 0, (saved_ref[...].astype(F32) * scale * gain).astype(BF16))

    far = [(cols, far_cols), (gain_ref, far_gain), (table_ref, far_table), (cot_ref, far_cot), (saved_ref, far_saved)]

    def far_copy(n):
        return remote(far[n][0], far[n][1], e_send.at[n], e_recv.at[n], s=1 - sec)

    def far_value_copy(c):
        part = pl.ds(c * tc, tc)
        n = len(far) + c
        return remote(there_send.at[:, part], far_value.at[:, part], e_send.at[n], e_recv.at[n], s=1 - sec)

    @pl.when(sec == 1)
    def _():
        for n in range(len(far)):
            far_copy(n).start()

    def lean_of(place_in, kept, table, gains):
        total = jnp.zeros((T, F), F32)
        for e in range(E):
            sign = jnp.where(kept[:, 20:21] == e, 1.0, 0.0) - jnp.where(kept[:, 21:22] == e, 1.0, 0.0)
            total = total + sign * table[e:e + 1, :]
        leans[place_in] = kept[:, 2:3] * total * gains[...]

    def reduce_step(which, acc, m_now, first, count):
        @pl.when(m_now == 0)
        def _():
            for n in range(count):
                own_part[which, first + n] = acc[:, n * tc:(n + 1) * tc]

        for m in range(1, H):
            @pl.when(m_now == m)
            def _():
                for n in range(count):
                    c = first + n
                    value = acc[:, n * tc:(n + 1) * tc]
                    for bit in bits_of(low_bit(m) * 2)[:-1]:
                        received(which, m + bit, c)
                        value = value + rs_recv[which, m + bit - 1, c].astype(F32)
                    rs_send[which, m - 1, c] = value.astype(BF16)
                    if which == 1 or m == 1 or m != low_bit(m):
                        reduce_copy(which, m, c).start()

    def reduce_copy(which, m, c):
        return remote(
            rs_send.at[which, m - 1, c], rs_recv.at[which, m - 1, c],
            r_send.at[which, m, c], r_recv.at[which, m, c], h=hid_peer[low_bit(m)])

    def received(which, m, c):
        reduce_copy(which, m, c).wait_recv()

    def home_region(which, expert, c):
        return home.at[which, pl.ds(pl.multiple_of(expert * cap, 16), cap), pl.ds(c * tc, tc)]

    def home_copy(which, k, c):
        return remote(
            home_send.at[which, c, pl.ds(pl.multiple_of(exp_peer[k] * cap, 16), cap)], home_region(which, me, c),
            b_send.at[which, k, c], b_recv.at[which, k, c], e=exp_peer[k])

    def home_event(which, c):
        value = own_part[which, c]
        for bit in bits_of(H):
            received(which, bit, c)
            value = value + rs_recv[which, bit - 1, c].astype(F32)
        home_send[which, c] = value.astype(BF16)
        for k in arrivals:
            send(functools.partial(home_copy, which, k, c))
        mine = pl.ds(pl.multiple_of(me * cap, 16), cap)
        home[which, mine, c * tc:(c + 1) * tc] = home_send[which, c, mine, :]

    def home_wait(which, c):
        for k in order:
            part = home_region(which, exp_peer[k], c)
            remote(part, part, b_send.at[which, k, c], b_recv.at[which, k, c], e=exp_peer[k]).wait_recv()

    wide_i = lax.broadcasted_iota(I32, (T, all_rows), 1).astype(F32)

    def selectors(n):
        picks = []
        for c in range(2):
            rank, route = cols[:, 16 + 2 * n + c:17 + 2 * n + c], cols[:, 20 + 2 * n + c:21 + 2 * n + c]
            picks.append(jnp.where(wide_i == route * cap + rank, 1.0, 0.0).astype(BF16))
        return picks

    def blended(which, keep, part, picks):
        part = home[which, :, part]
        return cols[:, keep:keep + 1] * dot(picks[0], part) + cols[:, keep + 1:keep + 2] * dot(picks[1], part)

    def there_copy(n, height):
        part = pl.ds(n * height, height)
        return remote(there_send.at[part], there_recv.at[part], y_send.at[n], y_recv.at[n], s=1 - sec)

    halves = 2
    half_rows = T // halves

    def forward_out():
        picks = selectors(1)
        for c in range(n_wide):
            for n in range(c * tw // tc, (c + 1) * tw // tc):
                home_wait(0, n)
            part = slice(c * tw, (c + 1) * tw)
            value = (next_ref[:, part].astype(F32) + blended(0, 4, part, picks)).astype(BF16)

            @pl.when(sec == 0)
            def _():
                there_send[:, part] = value

            @pl.when(sec == 1)
            def _():
                out_ref[0, :, part] = value

        @pl.when(sec == 0)
        def _():
            for n in range(halves):
                there_copy(n, half_rows).start()

    def run(events, index):
        for at, event in events:
            pl.when(index == at)(event)

    for event in next_events[1:-2]:
        event()
    for event in next_events[-2:]:
        event()
    complete(NXT)
    for k in range(E):
        if k:
            scale_copy(k).wait_recv()
        row = scale_recv[k - 1, 0:1] if k else scale_send[0, 0:1]
        scales[pl.ds(pl.multiple_of(exp_peer[k] * cap, 16), cap), :] = jnp.broadcast_to(row, (LANES, LANES)).T[0:cap]

    def at(events, spots):
        return list(zip(spots, events))

    def split(event, late, soon):
        return [(late + (soon - late) * (1 - inner), event)]

    wide_sends = [(m, c) for m in reversed(bits_of(H)) if m > 1 for c in range(n_cols)]

    def wave(start, stop):
        return [functools.partial(lambda m, c: reduce_copy(0, m, c).start(), m, c) for m, c in wide_sends[start:stop]]

    downs = [functools.partial(home_event, 0, c) for c in range(n_cols)]
    tuned = E == 4 and H == 4 and n_cols == 8 and n_wide == 4 and n_tiles == 7
    saved_events = gather_events(SAV)
    if tuned:
        up_events = at(saved_events[:6], [1, 2, 3, 4, 5, 6])
        out_events = at(saved_events[6:], [3]) + at(cot_events[:1], [4])
        gate_events = at(cot_events[2:3], [0]) + at(cot_events[3:5], [2, 2]) + at(wave(0, 8), [2] * 8) + at(cot_events[5:], [4, 6])
        gh_events = at(downs[:4], [1, 1, 4, 5])
        back_events = at(downs[4:], [1, 1, 4, 5])
        back_spots = [6, 8, 12, 12, 14]
    else:
        up_events = at(saved_events, [n_tiles * n // len(saved_events) for n in range(len(saved_events))])
        out_events = []
        late_events = cot_events[:1] + cot_events[2:]
        gate_events = at(late_events, [n_tiles * n // len(late_events) for n in range(len(late_events))])
        waves = wave(0, len(wide_sends))
        gate_events += at(waves, [n_tiles - 1] * len(waves))
        gh_events = []
        back_events = at(downs, [2 + c for c in range(n_cols)])
        back_spots = []
    cot_events[1]()

    @pl.loop(0, n_tiles)
    def _(j):
        start_a(j + A_SLOTS - 1)
        run(up_events, j)
        slot = lax.rem(j, A_SLOTS)
        for copy in a_copies("pair", j, slot):
            copy.wait()
        both = dot(rows[NXT], wa[slot, :, 0:2 * tn]) * scales[:, 0:1]
        gate, up = both[:, 0:tn], both[:, tn:2 * tn]
        hid_n[:, pl.ds(pl.multiple_of(j * tn, tn), tn)] = (gate * jax.nn.sigmoid(gate) * up).astype(BF16)

    @pl.loop(0, out_items)
    def _(i):
        g = n_tiles + i
        start_a(g + A_SLOTS - 1)
        run(out_events, i)
        slot = lax.rem(g, A_SLOTS)
        out_copy(i, slot).wait()
        acc = dot(hid_n[...], wa[slot, 0:ffd, 0:2 * tw])
        m, c = place_of(i, "out")
        reduce_step(0, acc, m, c * (2 * tw // tc), 2 * tw // tc)

    complete(SAV)

    dots_acc[...] = jnp.zeros_like(dots_acc)
    @pl.loop(0, n_tiles)
    def _(j):
        g = n_tiles + out_items + j
        start_a(g + A_SLOTS - 1)
        run(gate_events, j)
        slot = lax.rem(g, A_SLOTS)
        for copy in a_copies("pair", j, slot):
            copy.wait()
        part = pl.ds(pl.multiple_of(j * tn, tn), tn)
        both = dot(rows[SAV], wa[slot, :, 0:2 * tn])
        pair[0, :, part] = both[:, 0:tn]
        pair[1, :, part] = both[:, tn:2 * tn]

    complete(COT)

    @pl.loop(0, n_tiles)
    def _(j):
        start_r(j + R_SLOTS - 1)
        run(gh_events, j)
        gh_copy(j).wait()
        slot = lax.rem(j, R_SLOTS)
        grad = dot(rows[COT], wr[slot, 0:tn, 0:D], NT)
        part = pl.ds(pl.multiple_of(j * tn, tn), tn)
        gate, up = pair[0, :, part], pair[1, :, part]
        sig = jax.nn.sigmoid(gate)
        silu = gate * sig
        hidden = (silu * up).astype(BF16).astype(F32)
        grads[0, :, part] = (grad * up * (sig * (1.0 + gate * (1.0 - sig)))).astype(BF16)
        grads[1, :, part] = (grad * silu).astype(BF16)
        product = grad * hidden
        partial = product[:, 0:LANES]
        for n in range(1, tn // LANES):
            partial = partial + product[:, n * LANES:(n + 1) * LANES]
        dots_acc[...] += partial

    def dots_copy(k):
        return remote(dots_send, dots_recv.at[k - 1], d_send.at[k], d_recv.at[k], e=exp_peer[k])

    dots_send[...] = jnp.broadcast_to(jnp.sum(dots_acc[...].T, axis=0, keepdims=True), (8, all_rows))
    for k in order:
        send(functools.partial(dots_copy, k))

    def dots_event():
        for k in order:
            dots_copy(k).wait_recv()
        gap = jnp.zeros((T, 1), F32)
        for k in range(E):
            row = dots_send[0:1] if k == 0 else dots_recv[k - 1, 0:1]
            expert = exp_peer[k].astype(F32)
            for c, sign in ((0, 1.0), (1, -1.0)):
                rank, route = cols[:, 16 + c:17 + c], cols[:, 20 + c:21 + c]
                spot = jnp.where(route == expert, me.astype(F32) * cap + rank, -1.0)
                gap = gap + sign * jnp.sum(jnp.where(wide_i == spot, row, 0.0), axis=1, keepdims=True)
        dots_acc[0:T, 0:1] = gap

    back_events += at([functools.partial(home_event, 1, c) for c in range(n_cols)], back_spots)

    @pl.loop(0, steps)
    def _(i):
        start_r(n_tiles + i + R_SLOTS - 1)
        run(back_events, i)
        for copy in back_copies(i):
            copy.wait()
        slot = lax.rem(n_tiles + i, R_SLOTS)
        acc = dot(grads[0], wr[slot, 0:tw, 0:ffd], NT) + dot(grads[1], wr[slot, 0:tw, ffd:2 * ffd], NT)
        m, c = place_of(i, "back")
        reduce_step(1, acc, m, c * (tw // tc), tw // tc)

    later = list(range(len(back_spots), n_cols))
    for c in later[:1]:
        home_event(1, c)
    forward_out()
    dots_event()
    for c in later[1:]:
        home_event(1, c)
    lean_of(0, cols, table_ref, gain_ref)

    @pl.when(sec == 0)
    def _():
        for n in range(len(far)):
            far_copy(n).wait_recv()
        lean_of(1, far_cols, far_table, far_gain)

    picks = selectors(0)
    inner = jnp.zeros((T, 1), F32)
    for c in range(n_cols):
        home_wait(1, c)
        part = slice(c * tc, (c + 1) * tc)
        value = blended(1, 0, part, picks) * gain_ref[:, part]
        mixed[:, part] = cot_ref[:, part].astype(F32) + cols[:, 2:3] * value

        @pl.when(sec == 1)
        def _():
            there_send[:, part] = value.astype(BF16)
            far_value_copy(c).start()

        inner = inner + jnp.sum(value * saved_ref[:, part].astype(F32), axis=1, keepdims=True)
    message = jnp.where(lane == 0, inner, 0.0) + jnp.where(lane == 1, dots_acc[0:T, 0:1], 0.0)
    message = message.T[0:8]
    tail_send[...] = message

    def tail_copy(m):
        return remote(tail_send, tail_recv.at[m - 1], t_send.at[m], t_recv.at[m], h=hid_peer[m])

    def far_tail_copy(m):
        return remote(tail_send, far_tail.at[m], f_send.at[m], f_recv.at[m], h=hid_peer[m], s=1 - sec)

    def input_gradient(message, base, saved, kept, place_in):
        message = jnp.concatenate([message, jnp.zeros((LANES - 8, T), F32)], axis=0).T
        scale = kept[:, 2:3]
        slope = message[:, 1:2] * kept[:, 0:1] * kept[:, 1:2]
        inner = message[:, 0:1] + slope * kept[:, 3:4]
        pull = scale * scale * scale * (inner / D)
        out_ref[place_in] = (base() + slope * leans[place_in] - saved[...].astype(F32) * pull).astype(BF16)

    @pl.when(sec == 1)
    def _():
        for m in range(H):
            far_tail_copy(m).start()
        for n in range(halves):
            there_copy(n, half_rows).wait_recv()
        out_ref[1] = there_recv[...]
        for n in range(len(far)):
            far_copy(n).wait_send()
        for c in range(n_cols):
            far_value_copy(c).wait_send()
        for m in range(H):
            far_tail_copy(m).wait_send()

    @pl.when(sec == 0)
    def _():
        for m in range(1, H):
            tail_copy(m).start()
        total = message
        for m in range(1, H):
            tail_copy(m).wait_recv()
            total = total + tail_recv[m - 1]
        input_gradient(total, lambda: mixed[...], saved_ref, cols, 0)
        for c in range(n_cols):
            far_value_copy(c).wait_recv()
        total = jnp.zeros((8, T), F32)
        for m in range(H):
            far_tail_copy(m).wait_recv()
            total = total + far_tail[m]
        input_gradient(
            total, lambda: far_cot[...].astype(F32) + far_cols[:, 2:3] * far_value[...].astype(F32),
            far_saved, far_cols, 1)
        for m in range(1, H):
            tail_copy(m).wait_send()
        for n in range(halves):
            there_copy(n, half_rows).wait_send()

    for build in to_send:
        build().wait_send()
    for tau in range(3):
        for k in range(E):
            for part in parts:
                if k:
                    dispatch_copy(tau, k, part).wait_send()
                for piece in [0] + relays:
                    for build in forwards(tau, piece, k, part):
                        build().wait_send()
    for which in range(2):
        for m in range(1, H):
            for c in range(n_cols):
                reduce_copy(which, m, c).wait_send()


def per_device(
    saved_input,
    cotangent,
    next_input,
    routes_saved,
    routes_next,
    norm_gain,
    router,
    expert_gate,
    expert_up,
    expert_down,
):
    E, H = lax.axis_size("expert"), lax.axis_size("hid")
    T, F = saved_input.shape[1:]
    D, ffd = expert_gate.shape[2:]
    cap = 3 * T // router.shape[2]
    tn = 2 * LANES if ffd % (2 * LANES) == 0 else LANES
    tw = 2 * LANES if F % (2 * LANES) == 0 else LANES
    tc = LANES
    n_cols, all_rows = F // tc, E * cap
    deep, wide = max(tn, tw), max(D, 2 * ffd)
    vmem = pl.BlockSpec(memory_space=pltpu.VMEM)
    hbm = pl.BlockSpec(memory_space=pl.ANY)
    dma = pltpu.SemaphoreType.DMA
    scratch = [
        pltpu.VMEM((3, all_rows, D), BF16),
        pltpu.VMEM((3, E - 1, cap, F), BF16),
        pltpu.VMEM((A_SLOTS, D, 2 * deep), BF16),
        pltpu.VMEM((R_SLOTS, deep, wide), BF16),
        pltpu.VMEM((2, all_rows, ffd), F32),
        pltpu.VMEM((all_rows, ffd), BF16),
        pltpu.VMEM((2, all_rows, ffd), BF16),
        pltpu.VMEM((2, H - 1, n_cols, all_rows, tc), BF16),
        pltpu.VMEM((2, H - 1, n_cols, all_rows, tc), BF16),
        pltpu.VMEM((2, n_cols, all_rows, tc), F32),
        pltpu.VMEM((2, n_cols, all_rows, tc), BF16),
        pltpu.VMEM((2, all_rows, F), BF16),
        pltpu.VMEM((32, T), F32),
        pltpu.VMEM((H - 1, 32, T), F32),
        pltpu.VMEM((all_rows, LANES), F32),
        pltpu.VMEM((8, all_rows), F32),
        pltpu.VMEM((E - 1, 8, all_rows), F32),
        pltpu.VMEM((8, T), F32),
        pltpu.VMEM((H - 1, 8, T), F32),
        pltpu.VMEM((T, LANES), F32),
        pltpu.VMEM((T, F), F32),
        pltpu.VMEM((T, F), BF16),
        pltpu.VMEM((T, F), BF16),
        pltpu.VMEM((T, F), BF16),
        pltpu.VMEM((T, F), BF16),
        pltpu.VMEM((T, F), BF16),
        pltpu.VMEM((1, F), F32),
        pltpu.VMEM((E, F), F32),
        pltpu.VMEM((T, LANES), F32),
        pltpu.VMEM((H, 8, T), F32),
        pltpu.VMEM((E, 8, LANES), F32),
        pltpu.VMEM((E - 1, 8, LANES), F32),
        pltpu.VMEM((all_rows, LANES), F32),
        pltpu.VMEM((2, T, F), F32),
        dma((A_SLOTS, 2)),
        dma((R_SLOTS, 2)),
        dma((3, E, 2)),
        dma((3, E, 2)),
        dma((3, H, E, 2)),
        dma((3, H, E, 2)),
        dma((H,)),
        dma((H,)),
        dma((2, H, n_cols)),
        dma((2, H, n_cols)),
        dma((2, E, n_cols)),
        dma((2, E, n_cols)),
        dma((E,)),
        dma((E,)),
        dma((H,)),
        dma((H,)),
        dma((2,)),
        dma((2,)),
        dma((5 + n_cols,)),
        dma((5 + n_cols,)),
        dma((H,)),
        dma((H,)),
        dma((E,)),
        dma((E,)),
    ]
    result = pl.pallas_call(
        functools.partial(kernel, (E, H, T, F, D, ffd, cap, tn, tw, tc)),
        out_shape=jax.ShapeDtypeStruct((2, T, F), BF16),
        in_specs=[vmem] * 7 + [hbm] * 3,
        out_specs=vmem,
        scratch_shapes=scratch,
        compiler_params=pltpu.CompilerParams(
            collective_id=0, has_side_effects=True, vmem_limit_bytes=67043328
        ),
        name="relay",
    )(
        saved_input[0], cotangent[0], next_input[0], routes_saved[0].T, routes_next[0].T, norm_gain, router[0].T,
        expert_gate[0, 0], expert_up[0, 0], expert_down[0, 0],
    )
    return (result[0:1], result[1:2])


def solution(mesh):
    placed = (
        P("section", "expert", "hid"),
        P("section", "expert", "hid"),
        P("section", "expert", "hid"),
        P("section", "expert", None),
        P("section", "expert", None),
        P("section", "hid"),
        P("section", "hid", None),
        P("section", "expert", None, "hid"),
        P("section", "expert", None, "hid"),
        P("section", "expert", "hid", None),
    )
    return jax.shard_map(
        per_device,
        mesh=mesh,
        in_specs=placed,
        out_specs=(P("section", "expert", "hid"), P("section", "expert", "hid")),
        check_vma=False,
    )
```
